32 devices in a mesh: row: 8 (over y, x, core), col: 4 (over z).
Axes of the slice: x: 2, y: 2, z: 4, core: 2. Of those that a mesh axis runs over, the one named last changes fastest.
Arguments:
- inverse: float32 [20480, 20480], P('row', 'col'), may hold values from -6 to 6
- factor: float32 [20480, 2, 256], P(('row', 'col')), may hold values from -0.0390625 to 0.0390625
- diag_inverse: float32 [2, 256, 256], replicated, may hold values from -6 to 6
- block_sizes: int32 [64], replicated, may hold values from 1 to 1280, 20480 in all
- listed: int32 [2, 64], replicated, may hold values 0 or 1
Outputs:
- ancestor_rows: float32 [20480, 2, 256], P(('row', 'col'))
- diagonal_block: float32 [2, 256, 256], replicated
The draws below stay inside these ranges and needn't reach their ends.
Inputs may be any that keep to these rules, and one draw needn't show every extreme that they name: `block_sizes`: positive sizes that sum to 20480; the largest is exactly 1280.
All inputs are finite; a program needn't handle non-finite values.
Results may differ from the reference program's by a relative error of at most 0.00007.
Values sent between devices are 32-bit elements; how exact they have to be, the bound alone decides.
A program may use at most 128 MiB of HBM per device.

```python
import math
import jax
import jax.numpy as jnp
import numpy as np
from jax import lax

NA = 20480
W = 256
SIBS = 2
NBLK = 64
MOSTB = 1280


def place_ends(array, own_key, smallest, top_value):
    longest = array.shape.index(max(array.shape))
    spots = []
    for shift in (0, 1):
        where = [jax.random.randint(jax.random.fold_in(own_key, axis), (), 0, length) for axis, length in enumerate(array.shape)]
        where[longest] = (where[longest] + shift) % array.shape[longest]
        spots.append(tuple(where))
    return array.at[spots[0]].set(smallest).at[spots[1]].set(top_value)


def steps_of(key, extent, cuts, smallest, largest):
    def one(axis_at, shards_of):
        draws = jax.random.uniform(jax.random.fold_in(jax.random.fold_in(key, 6), axis_at), (shards_of,), jnp.float32, smallest / len(cuts), largest / len(cuts))
        return jnp.repeat(jnp.exp(draws), extent[axis_at] // shards_of).reshape((-1,) + (1,) * (len(extent) - axis_at - 1))

    level = one(*cuts[0])
    for cut in cuts[1:]:
        level = level * one(*cut)
    return level


def profile(count, total, reach, lean):
    weights = [(1 << 20) // math.isqrt(rank ** lean) + 1 for rank in range(2, count + 1)]
    rest, given = total - reach - (count - 1), [1] * (count - 1)
    while rest > 0:
        movable = [i for i in range(count - 1) if given[i] < reach]
        pool, left = sum([weights[i] for i in movable]), rest
        for i in movable:
            addition = min(reach - given[i], max(1, left * weights[i] // pool), rest)
            given[i] = given[i] + addition
            rest = rest - addition
    return np.array([reach] + given)


def uneven(key, count, total, limit, slope):
    if count == 2:
        one = jax.random.randint(key, (), max(1, total - limit), min(limit, total - 1) + 1)
        return jnp.stack([one, total - one])
    tallies = jnp.asarray(profile(count, total, limit, slope), jnp.int32)
    pairs = (count - 1) // 2
    donor, taker = tallies[1:1 + 2 * pairs:2], tallies[2:2 + 2 * pairs:2]
    room = jnp.minimum(donor - 1, limit - taker)
    passed = jax.random.randint(jax.random.fold_in(key, 1), (pairs,), 0, 1 << 20) % (room + 1)
    tallies = tallies.at[1:1 + 2 * pairs:2].set(donor - passed).at[2:2 + 2 * pairs:2].set(taker + passed)
    return tallies[jax.random.permutation(jax.random.fold_in(key, 2), count)]


def scatter_about(rng, dims, deviation, bound, shards=(), held_as=jnp.bfloat16):
    factor_of = steps_of(rng, dims, shards, -0.22, 0.18) if shards else 1.0
    result = jax.random.normal(rng, dims, jnp.float32) * deviation * factor_of
    return jnp.minimum(jnp.maximum(result, -bound), bound).astype(held_as)


def setup_inputs(seed: int = 0) -> dict:
    key_of = jax.random.split(jax.random.key(seed), 6)
    return {
        "inverse": scatter_about(key_of[0], (NA, NA), 1.0, 6.0, ((0, 8), (1, 4)), jnp.float32),
        "factor": scatter_about(key_of[1], (NA, SIBS, W), NA ** -0.5, 0.0390625, ((0, 32),), jnp.float32),
        "diag_inverse": scatter_about(key_of[2], (SIBS, W, W), 1.0, 6.0, (), jnp.float32),
        "block_sizes": uneven(key_of[3], NBLK, NA, MOSTB, 2).astype(jnp.int32),
        "listed": place_ends((jax.random.randint(key_of[4], (SIBS, NBLK), 0, 2) < 1).astype(jnp.int32), jax.random.fold_in(key_of[4], 1), 0, 1),
    }


def membership(first_row, row_total, block_sizes, listed):
    block_ends = jnp.cumsum(block_sizes).astype(jnp.int32)
    block_starts = block_ends - block_sizes.astype(jnp.int32)
    positions = first_row + jnp.arange(row_total, dtype=jnp.int32)
    inside = ((positions[:, None] >= block_starts[None, :]) & (positions[:, None] < block_ends[None, :])).astype(jnp.float32)
    return jnp.dot(inside, listed.astype(jnp.float32).T, precision=lax.Precision.HIGHEST, preferred_element_type=jnp.float32)


def reference(inverse, factor, diag_inverse, block_sizes, listed):
    member = membership(0, NA, block_sizes, listed)
    masked = factor * member[:, :, None]
    panel = masked.reshape(NA, SIBS * W)
    product = -jnp.dot(inverse, panel, precision=lax.Precision.HIGHEST, preferred_element_type=jnp.float32)
    ancestor_rows = product.reshape(NA, SIBS, W) * member[:, :, None]
    schur = jnp.einsum("isw,isv->swv", factor, ancestor_rows, precision=lax.Precision.HIGHEST)
    return ancestor_rows, diag_inverse - schur
```

```python
import functools
import math

import jax
import jax.numpy as jnp
from jax import lax
from jax.experimental import pallas as pl
from jax.experimental.pallas import tpu as pltpu
from jax.sharding import PartitionSpec as P

MESH = pl.DeviceIdType.MESH


def membership(first_row, row_total, block_sizes, listed):
    count = block_sizes.shape[0]
    until = lax.broadcasted_iota(jnp.int32, (count, count), 1) <= lax.broadcasted_iota(jnp.int32, (count, count), 0)
    block_ends = jnp.sum(jnp.where(until, block_sizes[None, :], 0), axis=1)
    block_starts = block_ends - block_sizes
    positions = first_row + jnp.arange(row_total, dtype=jnp.int32)
    inside = (
        (positions[:, None] >= block_starts[None, :]) & (positions[:, None] < block_ends[None, :])
    ).astype(jnp.float32)
    return jnp.dot(
        inside,
        listed.astype(jnp.float32).T,
        precision=lax.Precision.HIGHEST,
        preferred_element_type=jnp.float32,
    )


def holder(k, n_rowdev, n_coldev):
    ratio = n_rowdev // n_coldev
    part = k // n_coldev
    place = k % n_coldev
    return (place + (part % 2) * (n_coldev - 1 - 2 * place)) * ratio + part


def shard_of(row, n_rowdev, n_coldev):
    ratio = n_rowdev // n_coldev
    part = row % ratio
    place = row // ratio
    return part * n_coldev + place + (part % 2) * (n_coldev - 1 - 2 * place)


def flip(row, bit):
    return row + bit * (1 - 2 * ((row // bit) % 2))


def general_kernel(
    n_rowdev, n_coldev, parts, depth,
    own_ref, inverse_ref, out_ref,
    panel, high, low, tiles, sums, from_below, from_above,
    gather_send, gather_recv, tile_sem, sum_send, below_recv, above_recv,
):
    row = lax.axis_index("row")
    col = lax.axis_index("col")
    sibling_count, shard_rows, width = own_ref.shape
    col_rows = panel.shape[1]
    piece = shard_rows // parts
    bits = [1 << i for i in range(n_rowdev.bit_length() - 1)]

    number = row * n_coldev + col
    target_row = holder(number % n_rowdev, n_rowdev, n_coldev)
    target_col = number // n_rowdev
    source = col * n_rowdev + shard_of(row, n_rowdev, n_coldev)
    source_row = source // n_coldev
    source_col = source % n_coldev
    moving = target_row * n_coldev + target_col != number

    barrier = pltpu.get_barrier_semaphore()

    def greet(to_row, to_col):
        pl.semaphore_signal(barrier, inc=1, device_id=(to_row, to_col), device_id_type=MESH)

    for bit in bits:
        greet(flip(row, bit), col)

    @pl.when(moving)
    def _():
        greet(target_row, target_col)
        greet(source_row, source_col)

    @pl.when(col > 0)
    def _():
        greet(row, col - 1)

    @pl.when(col < n_coldev - 1)
    def _():
        greet(row, col + 1)

    pl.semaphore_wait(
        barrier,
        len(bits)
        + jnp.where(moving, 2, 0)
        + jnp.where(col > 0, 1, 0)
        + jnp.where(col < n_coldev - 1, 1, 0),
    )

    def place(of_row, part):
        start = shard_of(of_row, n_rowdev, n_coldev) * shard_rows + part * piece
        return pl.ds(pl.multiple_of(start, 8), piece)

    def orders(part):
        rest = bits[1:]
        return (rest if part % 2 else rest[::-1]) + bits[:1]

    def move(s, part):
        return pltpu.make_async_remote_copy(
            src_ref=own_ref.at[s, pl.ds(part * piece, piece)],
            dst_ref=panel.at[s, place(target_row, part)],
            send_sem=gather_send.at[s, part, 0],
            recv_sem=gather_recv.at[s, part, 0],
            device_id=(target_row, target_col),
            device_id_type=MESH,
        )

    def keep(s, part):
        return pltpu.make_async_copy(
            own_ref.at[s, pl.ds(part * piece, piece)],
            panel.at[s, place(row, part)],
            gather_recv.at[s, part, 0],
        )

    def exchanges(s, part, stage):
        order = orders(part)
        held = [row]
        for bit in order[:stage - 1]:
            held = held + [flip(r, bit) for r in held]
        partner = flip(row, order[stage - 1])
        copies = []
        for m, slot in enumerate(held):
            entry = (1 << (stage - 1)) + m
            where = panel.at[s, place(slot, part)]
            copies.append(pltpu.make_async_remote_copy(
                src_ref=where,
                dst_ref=where,
                send_sem=gather_send.at[s, part, entry],
                recv_sem=gather_recv.at[s, part, entry],
                device_id=(partner, col),
                device_id_type=MESH,
            ))
        return copies

    def start_stage(s, part, stage):
        if stage == 0:
            @pl.when(moving)
            def _():
                move(s, part).start()

            @pl.when(jnp.logical_not(moving))
            def _():
                keep(s, part).start()
        else:
            for copy in exchanges(s, part, stage):
                copy.start()

    def end_stage(s, part, stage):
        if stage == 0:
            @pl.when(moving)
            def _():
                move(s, part).wait_recv()

            @pl.when(jnp.logical_not(moving))
            def _():
                keep(s, part).wait()
        else:
            for copy in exchanges(s, part, stage):
                copy.wait_recv()

    items = [(s, part) for s in range(sibling_count) for part in range(parts)]
    for s, part in items:
        start_stage(s, part, 0)

    others = (n_coldev - 1) * parts
    total = n_coldev * parts
    swap = col > n_coldev - 1 - col
    near = jnp.where(swap, n_coldev - 1 - col, col)
    lead = n_coldev - 1 - 2 * near
    minor_total = near * parts

    def plan(t):
        inner = t - lead
        paired = jnp.logical_and(inner >= 0, inner < 2 * minor_total)
        minor = jnp.logical_and(paired, inner % 2 == 1)
        major_at = jnp.where(inner < 0, t, jnp.where(paired, lead + inner // 2, t - minor_total))
        index = jnp.where(minor, inner // 2, major_at)
        up = jnp.where(swap, minor, jnp.logical_not(minor))
        block = jnp.where(up, n_coldev - 1 - index // parts, index // parts)
        is_own = t >= others
        block = jnp.where(is_own, col, block)
        part = jnp.where(is_own, t - others, index % parts)
        up = jnp.logical_and(up, jnp.logical_not(is_own))
        down = jnp.logical_and(jnp.logical_not(up), jnp.logical_not(is_own))
        return block, part, up, down, is_own

    def load(s, t):
        block, part, _, _, _ = plan(t % total)
        start = pl.multiple_of(block * shard_rows + part * piece, 8)
        slot = (s * total + t) % 2
        return pltpu.make_async_copy(
            inverse_ref.at[pl.ds(start, piece)], tiles.at[slot], tile_sem.at[slot]
        )

    load(0, 0).start()

    stages = 1 + len(bits)
    for tick in range(parts + stages):
        for part in range(parts):
            stage = tick - part
            if 0 <= stage < stages:
                end_stage(0, part, stage)
                if stage + 1 < stages:
                    start_stage(0, part, stage + 1)

    step = math.gcd(col_rows, 256)

    def split(s):
        @pl.loop(0, col_rows // step)
        def _(i):
            rows = pl.ds(pl.multiple_of(i * step, step), step)
            value = panel[s, rows, :]
            top = value.astype(jnp.bfloat16)
            high[s, rows, :] = top
            low[s, rows, :] = (value - top.astype(jnp.float32)).astype(jnp.bfloat16)

    def pass_up(s, block, part):
        return pltpu.make_async_remote_copy(
            src_ref=sums.at[s, block, part],
            dst_ref=from_below.at[s, block, part],
            send_sem=sum_send.at[s, block, part],
            recv_sem=below_recv.at[s, block, part],
            device_id=(row, col + 1),
            device_id_type=MESH,
        )

    def pass_down(s, block, part):
        return pltpu.make_async_remote_copy(
            src_ref=sums.at[s, block, part],
            dst_ref=from_above.at[s, block, part],
            send_sem=sum_send.at[s, block, part],
            recv_sem=above_recv.at[s, block, part],
            device_id=(row, col - 1),
            device_id_type=MESH,
        )

    hooks = [(stage, part) for stage in range(stages - 1) for part in range(parts)]

    def advance(s, hook):
        stage, part = hook
        end_stage(s, part, stage)
        start_stage(s, part, stage + 1)

    for s in range(sibling_count):
        split(s)
        follows = s + 1 < sibling_count

        @pl.loop(0, total)
        def _(t):
            block, part, up, down, is_own = plan(t)
            slot = (s * total + t) % 2

            @pl.when(t + 1 < (total + 1 if follows else total))
            def _():
                load(s, t + 1).start()

            load(s, t).wait()
            sums[s, block, part] = jnp.zeros((piece, width), jnp.float32)

            @pl.loop(0, col_rows // depth)
            def _(k):
                span = pl.ds(pl.multiple_of(k * depth, depth), depth)
                value = tiles[slot, :, span]
                top = value.astype(jnp.bfloat16)
                rest = (value - top.astype(jnp.float32)).astype(jnp.bfloat16)
                dot = functools.partial(jnp.dot, preferred_element_type=jnp.float32)
                sums[s, block, part] += (
                    dot(top, low[s, span, :])
                    + dot(rest, high[s, span, :])
                    + dot(top, high[s, span, :])
                )

            @pl.when(jnp.logical_and(jnp.logical_not(down), col > 0))
            def _():
                pass_up(s, block, part).wait_recv()
                sums[s, block, part] += from_below[s, block, part]

            @pl.when(jnp.logical_and(jnp.logical_not(up), col < n_coldev - 1))
            def _():
                pass_down(s, block, part).wait_recv()
                sums[s, block, part] += from_above[s, block, part]

            @pl.when(up)
            def _():
                pass_up(s, block, part).start()

            @pl.when(down)
            def _():
                pass_down(s, block, part).start()

            @pl.when(is_own)
            def _():
                out_ref[s, part] = sums[s, block, part]

            if follows:
                for at, hook in enumerate(hooks[:total]):
                    @pl.when(t == at)
                    def _(hook=hook):
                        advance(s + 1, hook)

        if follows:
            for hook in hooks[total:]:
                advance(s + 1, hook)
            for part in range(parts):
                end_stage(s + 1, part, stages - 1)

    for s in range(sibling_count):
        @pl.loop(0, others)
        def _(t):
            block, part, up, down, _ = plan(t)

            @pl.when(up)
            def _():
                pass_up(s, block, part).wait_send()

            @pl.when(down)
            def _():
                pass_down(s, block, part).wait_send()

    for s, part in items:
        @pl.when(moving)
        def _():
            move(s, part).wait_send()

        for stage in range(1, stages):
            for copy in exchanges(s, part, stage):
                copy.wait_send()


def general_product(n_rowdev, n_coldev, inverse, own):
    sibling_count, shard_rows, width = own.shape
    block_total, col_rows = inverse.shape
    parts = 2 if shard_rows % 16 == 0 else 1
    piece = shard_rows // parts
    depth = math.gcd(col_rows, 1280)
    f32 = jnp.float32
    vmem = pl.BlockSpec(memory_space=pltpu.VMEM)
    out = pl.pallas_call(
        functools.partial(general_kernel, n_rowdev, n_coldev, parts, depth),
        out_shape=jax.ShapeDtypeStruct((sibling_count, parts, piece, width), f32),
        in_specs=[vmem, pl.BlockSpec(memory_space=pl.ANY)],
        out_specs=vmem,
        scratch_shapes=[
            pltpu.VMEM((sibling_count, col_rows, width), f32),
            pltpu.VMEM((sibling_count, col_rows, width), jnp.bfloat16),
            pltpu.VMEM((sibling_count, col_rows, width), jnp.bfloat16),
            pltpu.VMEM((2, piece, col_rows), f32),
            pltpu.VMEM((sibling_count, n_coldev, parts, piece, width), f32),
            pltpu.VMEM((sibling_count, n_coldev, parts, piece, width), f32),
            pltpu.VMEM((sibling_count, n_coldev, parts, piece, width), f32),
            pltpu.SemaphoreType.DMA((sibling_count, parts, n_rowdev)),
            pltpu.SemaphoreType.DMA((sibling_count, parts, n_rowdev)),
            pltpu.SemaphoreType.DMA((2,)),
            pltpu.SemaphoreType.DMA((sibling_count, n_coldev, parts)),
            pltpu.SemaphoreType.DMA((sibling_count, n_coldev, parts)),
            pltpu.SemaphoreType.DMA((sibling_count, n_coldev, parts)),
        ],
        compiler_params=pltpu.CompilerParams(
            collective_id=0, has_side_effects=True, vmem_limit_bytes=60_000_000
        ),
        name="gather_product_scatter",
    )(own, inverse)
    return out.reshape(sibling_count, shard_rows, width)


def planar_kernel(
    n_rowdev, n_coldev, parts, depth,
    own_ref, inverse_ref, out_ref,
    landing, panel, split_ref, tiles, sums, from_below, from_above,
    spread_send, spread_recv, move_send, move_recv, keep_sem, plane_send, plane_recv,
    core_send, core_recv, tile_sem, sum_send, below_recv, above_recv,
):
    row = lax.axis_index("row")
    col = lax.axis_index("col")
    units, chips, quarter, width = own_ref.shape
    half = quarter // 2
    shard_rows = chips * quarter
    col_rows = n_rowdev * shard_rows
    piece = shard_rows // parts
    core = row % 2
    chip = row // 2
    near_x, near_y, other_core = flip(row, 2), flip(row, 4), flip(row, 1)

    def across(d):
        r = row
        for bit in (1, 2):
            if d & bit:
                r = flip(r, 2 * bit)
        return r

    barrier = pltpu.get_barrier_semaphore()
    greeted = [(across(d), col) for d in range(1, chips)] + [(other_core, col)]
    greeted += [(row, (col + e) % n_coldev) for e in range(1, n_coldev)]
    for who in greeted:
        pl.semaphore_signal(barrier, inc=1, device_id=who, device_id_type=MESH)
    pl.semaphore_wait(barrier, len(greeted))

    def remote(src, dst, send, recv, to_row, to_col):
        return pltpu.make_async_remote_copy(
            src_ref=src, dst_ref=dst, send_sem=send, recv_sem=recv,
            device_id=(to_row, to_col), device_id_type=MESH,
        )

    def spread(u, d):
        to_row = across(d)
        return remote(
            own_ref.at[u, to_row // 2], landing.at[u, d - 1],
            spread_send.at[u, d - 1], spread_recv.at[u, d - 1], to_row, col,
        )

    def taken(u, d):
        return own_ref.at[u, chip] if d == 0 else landing.at[u, d - 1]

    def plane_of(d):
        return across(d) // 2

    def move(u, d):
        return remote(
            taken(u, d), panel.at[u, core * n_coldev + col, chip],
            move_send.at[u, d], move_recv.at[u, col], row, plane_of(d),
        )

    def arrival(u, source):
        where = panel.at[u, core * n_coldev + source, chip]
        return remote(where, where, move_send.at[u, 0], move_recv.at[u, source], row, source)

    def keep(u, d):
        return pltpu.make_async_copy(
            taken(u, d), panel.at[u, core * n_coldev + col, chip], keep_sem.at[u]
        )

    def mine(u, of_core, of_chip, part):
        shards = pl.ds(of_core * n_coldev, n_coldev)
        if part is None:
            return panel.at[u, shards, of_chip]
        return panel.at[u, shards, of_chip, pl.ds(part * half, half)]

    def in_plane(u, at):
        of_chip, part, to_row = (
            (chip, 0, near_x), (chip, 1, near_y), (chip, 1, near_x), (chip, 0, near_y),
            (near_x // 2, 0, near_y), (near_y // 2, 1, near_x),
        )[at]
        where = mine(u, core, of_chip, part)
        return remote(where, where, plane_send.at[u, at], plane_recv.at[u, at], to_row, col)

    def to_core(u, d):
        where = mine(u, core, plane_of(d), None)
        return remote(where, where, core_send.at[u, d], core_recv.at[u, d], other_core, col)

    def stage_spread(u):
        for d in range(1, chips):
            spread(u, d).start()

    def stage_move(u):
        for d in range(chips):
            if d:
                spread(u, d).wait_recv()

            @pl.when(plane_of(d) != col)
            def _():
                move(u, d).start()

            @pl.when(plane_of(d) == col)
            def _():
                keep(u, d).start()

    def stage_plane(u):
        keep(u, 0).wait()
        for e in range(1, n_coldev):
            arrival(u, (col + e) % n_coldev).wait_recv()
        for at in range(4):
            in_plane(u, at).start()
        to_core(u, 0).start()

    def stage_pass(u):
        in_plane(u, 0).wait_recv()
        in_plane(u, 4).start()
        in_plane(u, 1).wait_recv()
        in_plane(u, 5).start()

    def stage_core(u):
        in_plane(u, 2).wait_recv()
        to_core(u, 1).start()
        in_plane(u, 3).wait_recv()
        to_core(u, 2).start()

    def stage_last(u):
        in_plane(u, 4).wait_recv()
        in_plane(u, 5).wait_recv()
        to_core(u, 3).start()

    def stage_ready(u):
        for d in range(chips):
            to_core(u, d).wait_recv()

    stages = (stage_spread, stage_move, stage_plane, stage_pass, stage_core, stage_last, stage_ready)
    lag = 2.5
    order = sorted(
        ((u * lag + at, u, at) for u in range(units) for at in range(len(stages)))
    )
    order = [(u, at) for _, u, at in order]

    def advance(step):
        u, at = step
        stages[at](u)

    others = (n_coldev - 1) * parts
    total = n_coldev * parts
    swap = col > n_coldev - 1 - col
    near = jnp.where(swap, n_coldev - 1 - col, col)
    lead = n_coldev - 1 - 2 * near
    minor_total = near * parts

    def plan(t):
        inner = t - lead
        paired = jnp.logical_and(inner >= 0, inner < 2 * minor_total)
        minor = jnp.logical_and(paired, inner % 2 == 1)
        major_at = jnp.where(inner < 0, t, jnp.where(paired, lead + inner // 2, t - minor_total))
        index = jnp.where(minor, inner // 2, major_at)
        up = jnp.where(swap, minor, jnp.logical_not(minor))
        block = jnp.where(up, n_coldev - 1 - index // parts, index // parts)
        is_own = t >= others
        block = jnp.where(is_own, col, block)
        part = jnp.where(is_own, t - others, index % parts)
        up = jnp.logical_and(up, jnp.logical_not(is_own))
        down = jnp.logical_and(jnp.logical_not(up), jnp.logical_not(is_own))
        return block, part, up, down, is_own

    def load(u, t):
        block, part, _, _, _ = plan(t % total)
        start = pl.multiple_of(block * shard_rows + part * piece, 8)
        slot = (u * total + t) % 2
        return pltpu.make_async_copy(
            inverse_ref.at[pl.ds(start, piece)], tiles.at[slot], tile_sem.at[slot]
        )

    def split(u):
        @pl.loop(0, n_rowdev)
        def _(i):
            for j in range(chips):
                rows = pl.ds(pl.multiple_of(i * shard_rows + j * quarter, 16), quarter)
                value = panel[u, i, j]
                top = value.astype(jnp.bfloat16)
                split_ref[u, rows, pl.ds(0, width)] = top
                split_ref[u, rows, pl.ds(width, width)] = (
                    value - top.astype(jnp.float32)
                ).astype(jnp.bfloat16)

    def pass_up(u, block, part):
        return remote(
            sums.at[u, block, part], from_below.at[u, block, part],
            sum_send.at[u, block, part], below_recv.at[u, block, part], row, col + 1,
        )

    def pass_down(u, block, part):
        return remote(
            sums.at[u, block, part], from_above.at[u, block, part],
            sum_send.at[u, block, part], above_recv.at[u, block, part], row, col - 1,
        )

    dot = functools.partial(jnp.dot, preferred_element_type=jnp.float32)
    load(0, 0).start()
    first_ready = order.index((0, len(stages) - 1)) + 1
    for step in order[:first_ready]:
        advance(step)
    pending = order[first_ready:]

    for u in range(units):
        split(u)
        follows = u + 1 < units
        hooks = []
        if follows:
            upto = pending.index((u + 1, len(stages) - 1)) + 1
            hooks, pending = pending[:upto], pending[upto:]

        @pl.loop(0, total)
        def _(t):
            block, part, up, down, is_own = plan(t)
            slot = (u * total + t) % 2

            @pl.when(t + 1 < (total + 1 if follows else total))
            def _():
                load(u, t + 1).start()

            load(u, t).wait()
            sums[u, block, part] = jnp.zeros((piece, width), jnp.float32)

            @pl.loop(0, col_rows // depth)
            def _(k):
                span = pl.ds(pl.multiple_of(k * depth, depth), depth)
                value = tiles[slot, :, span]
                top = value.astype(jnp.bfloat16)
                rest = (value - top.astype(jnp.float32)).astype(jnp.bfloat16)
                main = dot(top, split_ref[u, span, :])
                sums[u, block, part] += (
                    main[:, width:] + dot(rest, split_ref[u, span, pl.ds(0, width)])
                    + main[:, :width]
                )

            @pl.when(jnp.logical_and(jnp.logical_not(down), col > 0))
            def _():
                pass_up(u, block, part).wait_recv()
                sums[u, block, part] += from_below[u, block, part]

            @pl.when(jnp.logical_and(jnp.logical_not(up), col < n_coldev - 1))
            def _():
                pass_down(u, block, part).wait_recv()
                sums[u, block, part] += from_above[u, block, part]

            @pl.when(up)
            def _():
                pass_up(u, block, part).start()

            @pl.when(down)
            def _():
                pass_down(u, block, part).start()

            @pl.when(is_own)
            def _():
                out_ref[u, part] = sums[u, block, part]

            for number, hook in enumerate(hooks):
                @pl.when(t == number * total // len(hooks))
                def _(hook=hook):
                    advance(hook)

    for u in range(units):
        @pl.loop(0, others)
        def _(t):
            block, part, up, down, _ = plan(t)

            @pl.when(up)
            def _():
                pass_up(u, block, part).wait_send()

            @pl.when(down)
            def _():
                pass_down(u, block, part).wait_send()

    for u in range(units):
        for d in range(1, chips):
            spread(u, d).wait_send()
        for d in range(chips):
            @pl.when(plane_of(d) != col)
            def _():
                move(u, d).wait_send()

            to_core(u, d).wait_send()
        for at in range(6):
            in_plane(u, at).wait_send()


def planar_product(n_rowdev, n_coldev, inverse, own):
    units, shard_rows, width = own.shape
    block_total, col_rows = inverse.shape
    chips = n_rowdev // 2
    quarter = shard_rows // chips
    parts = 2
    piece = shard_rows // parts
    depth = math.gcd(col_rows, 1280)
    f32 = jnp.float32
    vmem = pl.BlockSpec(memory_space=pltpu.VMEM)
    dma = pltpu.SemaphoreType.DMA
    block_shape = (units, n_coldev, parts, piece, width)
    out = pl.pallas_call(
        functools.partial(planar_kernel, n_rowdev, n_coldev, parts, depth),
        out_shape=jax.ShapeDtypeStruct((units, parts, piece, width), f32),
        in_specs=[vmem, pl.BlockSpec(memory_space=pl.ANY)],
        out_specs=vmem,
        scratch_shapes=[
            pltpu.VMEM((units, chips - 1, quarter, width), f32),
            pltpu.VMEM((units, n_rowdev, chips, quarter, width), f32),
            pltpu.VMEM((units, col_rows, 2 * width), jnp.bfloat16),
            pltpu.VMEM((2, piece, col_rows), f32),
            pltpu.VMEM(block_shape, f32),
            pltpu.VMEM(block_shape, f32),
            pltpu.VMEM(block_shape, f32),
            dma((units, chips - 1)), dma((units, chips - 1)),
            dma((units, chips)), dma((units, n_coldev)), dma((units,)),
            dma((units, 6)), dma((units, 6)),
            dma((units, chips)), dma((units, chips)),
            dma((2,)),
            dma((units, n_coldev, parts)), dma((units, n_coldev, parts)),
            dma((units, n_coldev, parts)),
        ],
        compiler_params=pltpu.CompilerParams(
            collective_id=0, has_side_effects=True, vmem_limit_bytes=62_000_000
        ),
        name="gather_product_scatter",
    )(own.reshape(units, chips, quarter, width), inverse)
    return out.reshape(units, shard_rows, width)


def product(n_rowdev, n_coldev, inverse, own):
    sibling_count, shard_rows, width = own.shape
    chips = n_rowdev // 2
    if n_rowdev == 2 * n_coldev and chips == 4 and shard_rows % (chips * 16) == 0:
        pieces = 2
        own = own.reshape(sibling_count, shard_rows, pieces, width // pieces)
        own = jnp.transpose(own, (0, 2, 1, 3)).reshape(-1, shard_rows, width // pieces)
        out = planar_product(n_rowdev, n_coldev, inverse, own)
        out = out.reshape(sibling_count, pieces, shard_rows, width // pieces)
        return jnp.transpose(out, (0, 2, 1, 3)).reshape(sibling_count, shard_rows, width)
    return general_product(n_rowdev, n_coldev, inverse, own)


def total_kernel(
    n_rowdev, n_coldev, x_ref, out_ref,
    got, mine, gathered, whole, first_send, first_recv, second_send, second_recv,
    third_send, third_recv,
):
    row = lax.axis_index("row")
    col = lax.axis_index("col")
    barrier = pltpu.get_barrier_semaphore()
    for step in range(1, n_rowdev):
        pl.semaphore_signal(
            barrier, inc=1, device_id=((row + step) % n_rowdev, col), device_id_type=MESH
        )
    for step in range(1, n_coldev):
        pl.semaphore_signal(
            barrier, inc=1, device_id=(row, (col + step) % n_coldev), device_id_type=MESH
        )
    pl.semaphore_wait(barrier, n_rowdev + n_coldev - 2)

    def scatter(step):
        peer = (row + step) % n_rowdev
        return pltpu.make_async_remote_copy(
            src_ref=x_ref.at[peer], dst_ref=got.at[step],
            send_sem=first_send.at[step], recv_sem=first_recv.at[step],
            device_id=(peer, col), device_id_type=MESH,
        )

    def share(step):
        return pltpu.make_async_remote_copy(
            src_ref=mine, dst_ref=gathered.at[step],
            send_sem=second_send.at[step], recv_sem=second_recv.at[step],
            device_id=(row, (col + step) % n_coldev), device_id_type=MESH,
        )

    def spread(step):
        return pltpu.make_async_remote_copy(
            src_ref=whole, dst_ref=out_ref.at[row],
            send_sem=third_send.at[step], recv_sem=third_recv.at[step],
            device_id=((row + step) % n_rowdev, col), device_id_type=MESH,
        )

    for step in range(1, n_rowdev):
        scatter(step).start()
    value = x_ref[row]
    for step in range(1, n_rowdev):
        scatter(step).wait_recv()
        value = value + got[step]
    mine[...] = value
    for step in range(1, n_coldev):
        share(step).start()
    for step in range(1, n_coldev):
        share(step).wait_recv()
    gathered[0] = mine[...]
    value = gathered[col]
    for place in range(1, n_coldev):
        value = value + gathered[(col - place + n_coldev) % n_coldev]
    whole[...] = value
    for step in range(1, n_rowdev):
        spread(step).start()
    out_ref[row] = whole[...]
    for step in range(1, n_rowdev):
        spread(step).wait_recv()
    for step in range(1, n_rowdev):
        scatter(step).wait_send()
        spread(step).wait_send()
    for step in range(1, n_coldev):
        share(step).wait_send()


def total(n_rowdev, n_coldev, value):
    rows, columns = value.shape
    piece = rows // n_rowdev
    vmem = pl.BlockSpec(memory_space=pltpu.VMEM)
    dma = pltpu.SemaphoreType.DMA
    out = pl.pallas_call(
        functools.partial(total_kernel, n_rowdev, n_coldev),
        out_shape=jax.ShapeDtypeStruct((n_rowdev, piece, columns), jnp.float32),
        in_specs=[vmem],
        out_specs=vmem,
        scratch_shapes=[
            pltpu.VMEM((n_rowdev, piece, columns), jnp.float32),
            pltpu.VMEM((piece, columns), jnp.float32),
            pltpu.VMEM((n_coldev, piece, columns), jnp.float32),
            pltpu.VMEM((piece, columns), jnp.float32),
            dma((n_rowdev,)), dma((n_rowdev,)), dma((n_coldev,)), dma((n_coldev,)),
            dma((n_rowdev,)), dma((n_rowdev,)),
        ],
        compiler_params=pltpu.CompilerParams(collective_id=1, has_side_effects=True),
        name="schur_total",
    )(value.reshape(n_rowdev, piece, columns))
    return out.reshape(rows, columns)


def per_device(inverse, factor, diag_inverse, block_sizes, listed):
    n_rowdev = lax.axis_size("row")
    n_coldev = lax.axis_size("col")
    row_place = lax.axis_index("row")
    col_place = lax.axis_index("col")
    shard_rows, sibling_count, width = factor.shape

    member = membership(
        (row_place * n_coldev + col_place) * shard_rows, shard_rows, block_sizes, listed
    )
    own = jnp.transpose(factor, (1, 0, 2))
    summed = product(n_rowdev, n_coldev, inverse, own * member.T[:, :, None])
    results = [
        -(summed[s] * member[:, s:s + 1])
        for s in range(sibling_count)
    ]
    terms = [
        lax.dot_general(
            own[s], results[s], (((0,), (0,)), ((), ())),
            precision=lax.Precision.HIGHEST, preferred_element_type=jnp.float32,
        )
        for s in range(sibling_count)
    ]
    schur = total(n_rowdev, n_coldev, jnp.concatenate(terms, axis=0))
    schur = schur.reshape(sibling_count, width, width)
    ancestor_rows = jnp.stack(results, axis=1)
    return (ancestor_rows, diag_inverse - schur)


def solution(mesh):
    in_specs = (P("row", "col"), P(("row", "col"), None, None), P(), P(), P())
    out_specs = (P(("row", "col"), None, None), P())
    return jax.shard_map(
        per_device, mesh=mesh, in_specs=in_specs, out_specs=out_specs, check_vma=False
    )
```

```python
import functools
import math

import jax
import jax.numpy as jnp
from jax import lax
from jax.experimental import pallas as pl
from jax.experimental.pallas import tpu as pltpu
from jax.sharding import PartitionSpec as P

MESH = pl.DeviceIdType.MESH


def membership(first_row, row_total, block_sizes, listed):
    count = block_sizes.shape[0]
    until = lax.broadcasted_iota(jnp.int32, (count, count), 1) <= lax.broadcasted_iota(jnp.int32, (count, count), 0)
    block_ends = jnp.sum(jnp.where(until, block_sizes[None, :], 0), axis=1)
    block_starts = block_ends - block_sizes
    positions = first_row + jnp.arange(row_total, dtype=jnp.int32)
    inside = (
        (positions[:, None] >= block_starts[None, :]) & (positions[:, None] < block_ends[None, :])
    ).astype(jnp.float32)
    return jnp.dot(
        inside,
        listed.astype(jnp.float32).T,
        precision=lax.Precision.HIGHEST,
        preferred_element_type=jnp.float32,
    )


def holder(k, n_rowdev, n_coldev):
    ratio = n_rowdev // n_coldev
    part = k // n_coldev
    place = k % n_coldev
    return (place + (part % 2) * (n_coldev - 1 - 2 * place)) * ratio + part


def shard_of(row, n_rowdev, n_coldev):
    ratio = n_rowdev // n_coldev
    part = row % ratio
    place = row // ratio
    return part * n_coldev + place + (part % 2) * (n_coldev - 1 - 2 * place)


def flip(row, bit):
    return row + bit * (1 - 2 * ((row // bit) % 2))


def general_kernel(
    n_rowdev, n_coldev, parts, depth,
    own_ref, inverse_ref, out_ref,
    panel, high, low, tiles, sums, from_below, from_above,
    gather_send, gather_recv, tile_sem, sum_send, below_recv, above_recv,
):
    row = lax.axis_index("row")
    col = lax.axis_index("col")
    sibling_count, shard_rows, width = own_ref.shape
    col_rows = panel.shape[1]
    piece = shard_rows // parts
    bits = [1 << i for i in range(n_rowdev.bit_length() - 1)]

    number = row * n_coldev + col
    target_row = holder(number % n_rowdev, n_rowdev, n_coldev)
    target_col = number // n_rowdev
    source = col * n_rowdev + shard_of(row, n_rowdev, n_coldev)
    source_row = source // n_coldev
    source_col = source % n_coldev
    moving = target_row * n_coldev + target_col != number

    barrier = pltpu.get_barrier_semaphore()

    def greet(to_row, to_col):
        pl.semaphore_signal(barrier, inc=1, device_id=(to_row, to_col), device_id_type=MESH)

    for bit in bits:
        greet(flip(row, bit), col)

    @pl.when(moving)
    def _():
        greet(target_row, target_col)
        greet(source_row, source_col)

    @pl.when(col > 0)
    def _():
        greet(row, col - 1)

    @pl.when(col < n_coldev - 1)
    def _():
        greet(row, col + 1)

    pl.semaphore_wait(
        barrier,
        len(bits)
        + jnp.where(moving, 2, 0)
        + jnp.where(col > 0, 1, 0)
        + jnp.where(col < n_coldev - 1, 1, 0),
    )

    def place(of_row, part):
        start = shard_of(of_row, n_rowdev, n_coldev) * shard_rows + part * piece
        return pl.ds(pl.multiple_of(start, 8), piece)

    def orders(part):
        rest = bits[1:]
        return (rest if part % 2 else rest[::-1]) + bits[:1]

    def move(s, part):
        return pltpu.make_async_remote_copy(
            src_ref=own_ref.at[s, pl.ds(part * piece, piece)],
            dst_ref=panel.at[s, place(target_row, part)],
            send_sem=gather_send.at[s, part, 0],
            recv_sem=gather_recv.at[s, part, 0],
            device_id=(target_row, target_col),
            device_id_type=MESH,
        )

    def keep(s, part):
        return pltpu.make_async_copy(
            own_ref.at[s, pl.ds(part * piece, piece)],
            panel.at[s, place(row, part)],
            gather_recv.at[s, part, 0],
        )

    def exchanges(s, part, stage):
        order = orders(part)
        held = [row]
        for bit in order[:stage - 1]:
            held = held + [flip(r, bit) for r in held]
        partner = flip(row, order[stage - 1])
        copies = []
        for m, slot in enumerate(held):
            entry = (1 << (stage - 1)) + m
            where = panel.at[s, place(slot, part)]
            copies.append(pltpu.make_async_remote_copy(
                src_ref=where,
                dst_ref=where,
                send_sem=gather_send.at[s, part, entry],
                recv_sem=gather_recv.at[s, part, entry],
                device_id=(partner, col),
                device_id_type=MESH,
            ))
        return copies

    def start_stage(s, part, stage):
        if stage == 0:
            @pl.when(moving)
            def _():
                move(s, part).start()

            @pl.when(jnp.logical_not(moving))
            def _():
                keep(s, part).start()
        else:
            for copy in exchanges(s, part, stage):
                copy.start()

    def end_stage(s, part, stage):
        if stage == 0:
            @pl.when(moving)
            def _():
                move(s, part).wait_recv()

            @pl.when(jnp.logical_not(moving))
            def _():
                keep(s, part).wait()
        else:
            for copy in exchanges(s, part, stage):
                copy.wait_recv()

    items = [(s, part) for s in range(sibling_count) for part in range(parts)]
    for s, part in items:
        start_stage(s, part, 0)

    others = (n_coldev - 1) * parts
    total = n_coldev * parts
    swap = col > n_coldev - 1 - col
    near = jnp.where(swap, n_coldev - 1 - col, col)
    lead = n_coldev - 1 - 2 * near
    minor_total = near * parts

    def plan(t):
        inner = t - lead
        paired = jnp.logical_and(inner >= 0, inner < 2 * minor_total)
        minor = jnp.logical_and(paired, inner % 2 == 1)
        major_at = jnp.where(inner < 0, t, jnp.where(paired, lead + inner // 2, t - minor_total))
        index = jnp.where(minor, inner // 2, major_at)
        up = jnp.where(swap, minor, jnp.logical_not(minor))
        block = jnp.where(up, n_coldev - 1 - index // parts, index // parts)
        is_own = t >= others
        block = jnp.where(is_own, col, block)
        part = jnp.where(is_own, t - others, index % parts)
        up = jnp.logical_and(up, jnp.logical_not(is_own))
        down = jnp.logical_and(jnp.logical_not(up), jnp.logical_not(is_own))
        return block, part, up, down, is_own

    def load(s, t):
        block, part, _, _, _ = plan(t % total)
        start = pl.multiple_of(block * shard_rows + part * piece, 8)
        slot = (s * total + t) % 2
        return pltpu.make_async_copy(
            inverse_ref.at[pl.ds(start, piece)], tiles.at[slot], tile_sem.at[slot]
        )

    load(0, 0).start()

    stages = 1 + len(bits)
    for tick in range(parts + stages):
        for part in range(parts):
            stage = tick - part
            if 0 <= stage < stages:
                end_stage(0, part, stage)
                if stage + 1 < stages:
                    start_stage(0, part, stage + 1)

    step = math.gcd(col_rows, 256)

    def split(s):
        @pl.loop(0, col_rows // step)
        def _(i):
            rows = pl.ds(pl.multiple_of(i * step, step), step)
            value = panel[s, rows, :]
            top = value.astype(jnp.bfloat16)
            high[s, rows, :] = top
            low[s, rows, :] = (value - top.astype(jnp.float32)).astype(jnp.bfloat16)

    def pass_up(s, block, part):
        return pltpu.make_async_remote_copy(
            src_ref=sums.at[s, block, part],
            dst_ref=from_below.at[s, block, part],
            send_sem=sum_send.at[s, block, part],
            recv_sem=below_recv.at[s, block, part],
            device_id=(row, col + 1),
            device_id_type=MESH,
        )

    def pass_down(s, block, part):
        return pltpu.make_async_remote_copy(
            src_ref=sums.at[s, block, part],
            dst_ref=from_above.at[s, block, part],
            send_sem=sum_send.at[s, block, part],
            recv_sem=above_recv.at[s, block, part],
            device_id=(row, col - 1),
            device_id_type=MESH,
        )

    hooks = [(stage, part) for stage in range(stages - 1) for part in range(parts)]

    def advance(s, hook):
        stage, part = hook
        end_stage(s, part, stage)
        start_stage(s, part, stage + 1)

    for s in range(sibling_count):
        split(s)
        follows = s + 1 < sibling_count

        @pl.loop(0, total)
        def _(t):
            block, part, up, down, is_own = plan(t)
            slot = (s * total + t) % 2

            @pl.when(t + 1 < (total + 1 if follows else total))
            def _():
                load(s, t + 1).start()

            load(s, t).wait()
            sums[s, block, part] = jnp.zeros((piece, width), jnp.float32)

            @pl.loop(0, col_rows // depth)
            def _(k):
                span = pl.ds(pl.multiple_of(k * depth, depth), depth)
                value = tiles[slot, :, span]
                top = value.astype(jnp.bfloat16)
                rest = (value - top.astype(jnp.float32)).astype(jnp.bfloat16)
                dot = functools.partial(jnp.dot, preferred_element_type=jnp.float32)
                sums[s, block, part] += (
                    dot(top, low[s, span, :])
                    + dot(rest, high[s, span, :])
                    + dot(top, high[s, span, :])
                )

            @pl.when(jnp.logical_and(jnp.logical_not(down), col > 0))
            def _():
                pass_up(s, block, part).wait_recv()
                sums[s, block, part] += from_below[s, block, part]

            @pl.when(jnp.logical_and(jnp.logical_not(up), col < n_coldev - 1))
            def _():
                pass_down(s, block, part).wait_recv()
                sums[s, block, part] += from_above[s, block, part]

            @pl.when(up)
            def _():
                pass_up(s, block, part).start()

            @pl.when(down)
            def _():
                pass_down(s, block, part).start()

            @pl.when(is_own)
            def _():
                out_ref[s, part] = sums[s, block, part]

            if follows:
                for at, hook in enumerate(hooks[:total]):
                    @pl.when(t == at)
                    def _(hook=hook):
                        advance(s + 1, hook)

        if follows:
            for hook in hooks[total:]:
                advance(s + 1, hook)
            for part in range(parts):
                end_stage(s + 1, part, stages - 1)

    for s in range(sibling_count):
        @pl.loop(0, others)
        def _(t):
            block, part, up, down, _ = plan(t)

            @pl.when(up)
            def _():
                pass_up(s, block, part).wait_send()

            @pl.when(down)
            def _():
                pass_down(s, block, part).wait_send()

    for s, part in items:
        @pl.when(moving)
        def _():
            move(s, part).wait_send()

        for stage in range(1, stages):
            for copy in exchanges(s, part, stage):
                copy.wait_send()


def general_product(n_rowdev, n_coldev, inverse, own):
    sibling_count, shard_rows, width = own.shape
    block_total, col_rows = inverse.shape
    parts = 2 if shard_rows % 16 == 0 else 1
    piece = shard_rows // parts
    depth = math.gcd(col_rows, 1280)
    f32 = jnp.float32
    vmem = pl.BlockSpec(memory_space=pltpu.VMEM)
    out = pl.pallas_call(
        functools.partial(general_kernel, n_rowdev, n_coldev, parts, depth),
        out_shape=jax.ShapeDtypeStruct((sibling_count, parts, piece, width), f32),
        in_specs=[vmem, pl.BlockSpec(memory_space=pl.ANY)],
        out_specs=vmem,
        scratch_shapes=[
            pltpu.VMEM((sibling_count, col_rows, width), f32),
            pltpu.VMEM((sibling_count, col_rows, width), jnp.bfloat16),
            pltpu.VMEM((sibling_count, col_rows, width), jnp.bfloat16),
            pltpu.VMEM((2, piece, col_rows), f32),
            pltpu.VMEM((sibling_count, n_coldev, parts, piece, width), f32),
            pltpu.VMEM((sibling_count, n_coldev, parts, piece, width), f32),
            pltpu.VMEM((sibling_count, n_coldev, parts, piece, width), f32),
            pltpu.SemaphoreType.DMA((sibling_count, parts, n_rowdev)),
            pltpu.SemaphoreType.DMA((sibling_count, parts, n_rowdev)),
            pltpu.SemaphoreType.DMA((2,)),
            pltpu.SemaphoreType.DMA((sibling_count, n_coldev, parts)),
            pltpu.SemaphoreType.DMA((sibling_count, n_coldev, parts)),
            pltpu.SemaphoreType.DMA((sibling_count, n_coldev, parts)),
        ],
        compiler_params=pltpu.CompilerParams(
            collective_id=0, has_side_effects=True, vmem_limit_bytes=60_000_000
        ),
        name="gather_product_scatter",
    )(own, inverse)
    return out.reshape(sibling_count, shard_rows, width)


def planar_kernel(
    n_rowdev, n_coldev, parts, sibling_count, unit_subs, order,
    own_ref, inverse_ref, out_ref, schur_ref, *scratch,
):
    units = len(unit_subs)
    scratch = list(scratch)

    def take(count):
        taken_refs = scratch[:count]
        del scratch[:count]
        return taken_refs

    landing, panel, tiles, across_high, across_low, terms, got, mine_sum, gathered, whole = take(10)
    split_refs, sums, from_below, from_above = (take(units) for _ in range(4))
    (
        spread_send, spread_recv, move_send, move_recv, keep_sem, plane_send, plane_recv,
        core_send, core_recv, tile_sem, sum_send, below_recv, above_recv,
        scatter_send, scatter_recv, share_send, share_recv, result_send, result_recv,
    ) = scratch

    row = lax.axis_index("row")
    col = lax.axis_index("col")
    subs, chips, quarter, width = own_ref.shape
    half = quarter // 2
    shard_rows = chips * quarter
    col_rows = n_rowdev * shard_rows
    piece = shard_rows // parts
    per_sibling = subs // sibling_count
    core = row % 2
    chip = row // 2
    near_x, near_y, other_core = flip(row, 2), flip(row, 4), flip(row, 1)
    firsts = [sum(unit_subs[:u]) for u in range(units)]

    def across(d):
        r = row
        for bit in (1, 2):
            if d & bit:
                r = flip(r, 2 * bit)
        return r

    barrier = pltpu.get_barrier_semaphore()
    greeted = [((row + e) % n_rowdev, col) for e in range(1, n_rowdev)]
    greeted += [(row, (col + e) % n_coldev) for e in range(1, n_coldev)]
    for who in greeted:
        pl.semaphore_signal(barrier, inc=1, device_id=who, device_id_type=MESH)
    pl.semaphore_wait(barrier, len(greeted))

    def group(u):
        return pl.ds(firsts[u], unit_subs[u])

    def remote(src, dst, send, recv, to_row, to_col):
        return pltpu.make_async_remote_copy(
            src_ref=src, dst_ref=dst, send_sem=send, recv_sem=recv,
            device_id=(to_row, to_col), device_id_type=MESH,
        )

    def spread(u, d):
        to_row = across(d)
        return remote(
            own_ref.at[group(u), to_row // 2], landing.at[group(u), d - 1],
            spread_send.at[u, d - 1], spread_recv.at[u, d - 1], to_row, col,
        )

    def taken(u, d):
        return own_ref.at[group(u), chip] if d == 0 else landing.at[group(u), d - 1]

    def plane_of(d):
        return across(d) // 2

    def move(u, d):
        return remote(
            taken(u, d), panel.at[group(u), core * n_coldev + col, chip],
            move_send.at[u, d], move_recv.at[u, col], row, plane_of(d),
        )

    def arrival(u, source):
        where = panel.at[group(u), core * n_coldev + source, chip]
        return remote(where, where, move_send.at[u, 0], move_recv.at[u, source], row, source)

    def keep(u, d):
        return pltpu.make_async_copy(
            taken(u, d), panel.at[group(u), core * n_coldev + col, chip], keep_sem.at[u]
        )

    def mine(u, of_chip, part):
        shards = pl.ds(core * n_coldev, n_coldev)
        if part is None:
            return panel.at[group(u), shards, of_chip]
        return panel.at[group(u), shards, of_chip, pl.ds(part * half, half)]

    def in_plane(u, at):
        of_chip, part, to_row = (
            (chip, 0, near_x), (chip, 1, near_y), (chip, 1, near_x), (chip, 0, near_y),
            (near_x // 2, 0, near_y), (near_y // 2, 1, near_x),
        )[at]
        where = mine(u, of_chip, part)
        return remote(where, where, plane_send.at[u, at], plane_recv.at[u, at], to_row, col)

    def to_core(u, d):
        where = mine(u, plane_of(d), None)
        return remote(where, where, core_send.at[u, d], core_recv.at[u, d], other_core, col)

    def stage_spread(u):
        for d in range(1, chips):
            spread(u, d).start()

    def stage_move(u):
        for d in range(chips):
            if d:
                spread(u, d).wait_recv()

            @pl.when(plane_of(d) != col)
            def _():
                move(u, d).start()

            @pl.when(plane_of(d) == col)
            def _():
                keep(u, d).start()

    def stage_plane(u):
        keep(u, 0).wait()
        for e in range(1, n_coldev):
            arrival(u, (col + e) % n_coldev).wait_recv()
        for at in range(4):
            in_plane(u, at).start()
        to_core(u, 0).start()

    def stage_pass(u):
        in_plane(u, 0).wait_recv()
        in_plane(u, 4).start()
        in_plane(u, 1).wait_recv()
        in_plane(u, 5).start()

    def stage_core(u):
        in_plane(u, 2).wait_recv()
        to_core(u, 1).start()
        in_plane(u, 3).wait_recv()
        to_core(u, 2).start()

    def stage_last(u):
        in_plane(u, 4).wait_recv()
        in_plane(u, 5).wait_recv()
        to_core(u, 3).start()

    def stage_ready(u):
        for d in range(chips):
            to_core(u, d).wait_recv()

    def scatter(u, step):
        peer = (row + step) % n_rowdev
        return remote(
            terms.at[group(u), peer], got.at[group(u), step],
            scatter_send.at[u, step], scatter_recv.at[u, step], peer, col,
        )

    def share(u, step):
        return remote(
            mine_sum.at[group(u)], gathered.at[group(u), step],
            share_send.at[u, step], share_recv.at[u, step], row, (col + step) % n_coldev,
        )

    def result(u, step):
        return remote(
            whole.at[group(u)], schur_ref.at[group(u), row],
            result_send.at[u, step], result_recv.at[u, step], (row + step) % n_rowdev, col,
        )

    dot = functools.partial(jnp.dot, preferred_element_type=jnp.float32)
    bf16 = jnp.bfloat16

    def halves(value):
        top = value.astype(bf16)
        return top, (value - top.astype(jnp.float32)).astype(bf16)

    def stage_term(u):
        for at in range(unit_subs[u]):
            sub = firsts[u] + at
            sibling = sub // per_sibling
            top, rest = halves(out_ref[:, pl.ds(sub * width, width)])
            high, low = across_high[sibling], across_low[sibling]
            term = dot(high, rest) + dot(low, top) + dot(high, top)
            terms[sub] = term.reshape(n_rowdev, term.shape[0] // n_rowdev, width)
        for step in range(1, n_rowdev):
            scatter(u, step).start()

    def stage_share(u):
        value = terms[group(u), row]
        for step in range(1, n_rowdev):
            scatter(u, step).wait_recv()
            value = value + got[group(u), step]
        mine_sum[group(u)] = value
        for step in range(1, n_coldev):
            share(u, step).start()

    def stage_result(u):
        for step in range(1, n_coldev):
            share(u, step).wait_recv()
        gathered[group(u), 0] = mine_sum[group(u)]
        value = gathered[group(u), col]
        for place in range(1, n_coldev):
            value = value + gathered[group(u), (col - place + n_coldev) % n_coldev]
        whole[group(u)] = value
        for step in range(1, n_rowdev):
            result(u, step).start()
        schur_ref[group(u), row] = value

    def stage_done(u):
        for step in range(1, n_rowdev):
            result(u, step).wait_recv()

    stages = (stage_spread, stage_move, stage_plane, stage_pass, stage_core, stage_last, stage_ready)
    ready = len(stages) - 1
    after = (stage_term, stage_share, stage_result, stage_done)

    others = (n_coldev - 1) * parts
    total = n_coldev * parts
    swap = col > n_coldev - 1 - col
    near = jnp.where(swap, n_coldev - 1 - col, col)
    lead = n_coldev - 1 - 2 * near
    minor_total = near * parts

    def plan(t):
        inner = t - lead
        paired = jnp.logical_and(inner >= 0, inner < 2 * minor_total)
        minor = jnp.logical_and(paired, inner % 2 == 1)
        major_at = jnp.where(inner < 0, t, jnp.where(paired, lead + inner // 2, t - minor_total))
        index = jnp.where(minor, inner // 2, major_at)
        up = jnp.where(swap, minor, jnp.logical_not(minor))
        block = jnp.where(up, n_coldev - 1 - index // parts, index // parts)
        is_own = t >= others
        block = jnp.where(is_own, col, block)
        part = jnp.where(is_own, t - others, index % parts)
        up = jnp.logical_and(up, jnp.logical_not(is_own))
        down = jnp.logical_and(jnp.logical_not(up), jnp.logical_not(is_own))
        return block, part, up, down, is_own

    def load(u, t):
        block, part, _, _, _ = plan(t % total)
        start = pl.multiple_of(block * shard_rows + part * piece, 8)
        slot = (u * total + t) % 2
        return pltpu.make_async_copy(
            inverse_ref.at[pl.ds(start, piece)], tiles.at[slot], tile_sem.at[slot]
        )

    def split(u):
        wide = unit_subs[u] * width

        @pl.loop(0, n_rowdev)
        def _(i):
            for at in range(unit_subs[u]):
                for j in range(chips):
                    rows = pl.ds(pl.multiple_of(i * shard_rows + j * quarter, 16), quarter)
                    top, rest = halves(panel[firsts[u] + at, i, j])
                    split_refs[u][rows, pl.ds(at * width, width)] = top
                    split_refs[u][rows, pl.ds(wide + at * width, width)] = rest

    def pass_up(u, block, part):
        return remote(
            sums[u].at[block, part], from_below[u].at[block, part],
            sum_send.at[u, block, part], below_recv.at[u, block, part], row, col + 1,
        )

    def pass_down(u, block, part):
        return remote(
            sums[u].at[block, part], from_above[u].at[block, part],
            sum_send.at[u, block, part], above_recv.at[u, block, part], row, col - 1,
        )

    def multiply(u, slot):
        wide = unit_subs[u] * width
        top, rest = halves(tiles[slot])
        if unit_subs[u] == 1:
            main = dot(top, split_refs[u][...])
            return main[:, wide:] + dot(rest, split_refs[u][:, pl.ds(0, wide)]) + main[:, :wide]
        high = split_refs[u][:, pl.ds(0, wide)]
        return dot(top, split_refs[u][:, pl.ds(wide, wide)]) + dot(rest, high) + dot(top, high)

    def turn_own():
        for sub in range(subs):
            value = own_ref[sub].reshape(shard_rows, width)
            top, rest = halves(value.T)
            rows = pl.ds((sub % per_sibling) * width, width)
            across_high[sub // per_sibling, rows, :] = top
            across_low[sub // per_sibling, rows, :] = rest

    def advance(step):
        u, at = step
        (stages + after)[at](u)

    load(0, 0).start()
    pending = list(order)
    first_ready = pending.index((0, ready)) + 1
    for number, step in enumerate(pending[:first_ready]):
        advance(step)
        if number == 3:
            turn_own()
    pending = pending[first_ready:]

    for u in range(units):
        split(u)
        follows = u + 1 < units
        hooks = []
        if follows:
            upto = pending.index((u + 1, ready)) + 1
            hooks, pending = pending[:upto], pending[upto:]
        if u:
            hooks = [(u - 1, ready + 2)] + hooks[:2] + [(u - 1, ready + 3)] + hooks[2:] + [(u - 1, ready + 4)]

        @pl.loop(0, total)
        def _(t):
            block, part, up, down, is_own = plan(t)
            slot = (u * total + t) % 2

            @pl.when(t + 1 < (total + 1 if follows else total))
            def _():
                load(u, t + 1).start()

            load(u, t).wait()
            sums[u][block, part] = multiply(u, slot)

            @pl.when(jnp.logical_and(jnp.logical_not(down), col > 0))
            def _():
                pass_up(u, block, part).wait_recv()
                sums[u][block, part] += from_below[u][block, part]

            @pl.when(jnp.logical_and(jnp.logical_not(up), col < n_coldev - 1))
            def _():
                pass_down(u, block, part).wait_recv()
                sums[u][block, part] += from_above[u][block, part]

            @pl.when(up)
            def _():
                pass_up(u, block, part).start()

            @pl.when(down)
            def _():
                pass_down(u, block, part).start()

            @pl.when(is_own)
            def _():
                rows = pl.ds(pl.multiple_of(part * piece, 8), piece)
                out_ref[rows, pl.ds(firsts[u] * width, unit_subs[u] * width)] = sums[u][block, part]

            for number, hook in enumerate(hooks):
                @pl.when(t == number * total // len(hooks))
                def _(hook=hook):
                    advance(hook)

        stage_term(u)

    for stage in after[1:]:
        stage(units - 1)

    for u in range(units):
        @pl.loop(0, others)
        def _(t):
            block, part, up, down, _ = plan(t)

            @pl.when(up)
            def _():
                pass_up(u, block, part).wait_send()

            @pl.when(down)
            def _():
                pass_down(u, block, part).wait_send()

    for u in range(units):
        for d in range(1, chips):
            spread(u, d).wait_send()
        for d in range(chips):
            @pl.when(plane_of(d) != col)
            def _():
                move(u, d).wait_send()

            to_core(u, d).wait_send()
        for at in range(6):
            in_plane(u, at).wait_send()
        for step in range(1, n_rowdev):
            scatter(u, step).wait_send()
            result(u, step).wait_send()
        for step in range(1, n_coldev):
            share(u, step).wait_send()


def planar_product(n_rowdev, n_coldev, sibling_count, inverse, own):
    subs, shard_rows, width = own.shape
    block_total, col_rows = inverse.shape
    chips = n_rowdev // 2
    quarter = shard_rows // chips
    parts = 2
    piece = shard_rows // parts
    unit_subs = (1, subs - 2, 1)
    units = len(unit_subs)
    order = ((0, 0), (1, 0), (0, 1), (2, 0), (1, 1), (0, 2), (2, 1), (0, 3), (0, 4), (0, 5), (1, 2), (0, 6), (1, 3), (1, 4), (2, 2), (1, 5), (1, 6), (2, 3), (2, 4), (2, 5), (2, 6))
    own_columns = subs // sibling_count * width
    share_rows = own_columns // n_rowdev
    f32, bf16 = jnp.float32, jnp.bfloat16
    vmem = pl.BlockSpec(memory_space=pltpu.VMEM)
    dma = pltpu.SemaphoreType.DMA
    blocks = [pltpu.VMEM((n_coldev, parts, piece, n * width), f32) for n in unit_subs]
    return pl.pallas_call(
        functools.partial(
            planar_kernel, n_rowdev, n_coldev, parts, sibling_count, unit_subs, order
        ),
        out_shape=(
            jax.ShapeDtypeStruct((shard_rows, subs * width), f32),
            jax.ShapeDtypeStruct((subs, n_rowdev, share_rows, width), f32),
        ),
        in_specs=[vmem, pl.BlockSpec(memory_space=pl.ANY)],
        out_specs=(vmem, vmem),
        scratch_shapes=[
            pltpu.VMEM((subs, chips - 1, quarter, width), f32),
            pltpu.VMEM((subs, n_rowdev, chips, quarter, width), f32),
            pltpu.VMEM((2, piece, col_rows), f32),
            pltpu.VMEM((sibling_count, own_columns, shard_rows), bf16),
            pltpu.VMEM((sibling_count, own_columns, shard_rows), bf16),
            pltpu.VMEM((subs, n_rowdev, share_rows, width), f32),
            pltpu.VMEM((subs, n_rowdev, share_rows, width), f32),
            pltpu.VMEM((subs, share_rows, width), f32),
            pltpu.VMEM((subs, n_coldev, share_rows, width), f32),
            pltpu.VMEM((subs, share_rows, width), f32),
            *[pltpu.VMEM((col_rows, 2 * n * width), bf16) for n in unit_subs],
            *blocks, *blocks, *blocks,
            dma((units, chips - 1)), dma((units, chips - 1)),
            dma((units, chips)), dma((units, n_coldev)), dma((units,)),
            dma((units, 6)), dma((units, 6)),
            dma((units, chips)), dma((units, chips)),
            dma((2,)),
            dma((units, n_coldev, parts)), dma((units, n_coldev, parts)),
            dma((units, n_coldev, parts)),
            dma((units, n_rowdev)), dma((units, n_rowdev)),
            dma((units, n_coldev)), dma((units, n_coldev)),
            dma((units, n_rowdev)), dma((units, n_rowdev)),
        ],
        compiler_params=pltpu.CompilerParams(
            collective_id=0, has_side_effects=True, vmem_limit_bytes=62_000_000
        ),
        name="gather_product_scatter",
    )(own.reshape(subs, chips, quarter, width), inverse)


def total_kernel(
    n_rowdev, n_coldev, x_ref, out_ref,
    got, mine, gathered, whole, first_send, first_recv, second_send, second_recv,
    third_send, third_recv,
):
    row = lax.axis_index("row")
    col = lax.axis_index("col")
    barrier = pltpu.get_barrier_semaphore()
    for step in range(1, n_rowdev):
        pl.semaphore_signal(
            barrier, inc=1, device_id=((row + step) % n_rowdev, col), device_id_type=MESH
        )
    for step in range(1, n_coldev):
        pl.semaphore_signal(
            barrier, inc=1, device_id=(row, (col + step) % n_coldev), device_id_type=MESH
        )
    pl.semaphore_wait(barrier, n_rowdev + n_coldev - 2)

    def scatter(step):
        peer = (row + step) % n_rowdev
        return pltpu.make_async_remote_copy(
            src_ref=x_ref.at[peer], dst_ref=got.at[step],
            send_sem=first_send.at[step], recv_sem=first_recv.at[step],
            device_id=(peer, col), device_id_type=MESH,
        )

    def share(step):
        return pltpu.make_async_remote_copy(
            src_ref=mine, dst_ref=gathered.at[step],
            send_sem=second_send.at[step], recv_sem=second_recv.at[step],
            device_id=(row, (col + step) % n_coldev), device_id_type=MESH,
        )

    def spread(step):
        return pltpu.make_async_remote_copy(
            src_ref=whole, dst_ref=out_ref.at[row],
            send_sem=third_send.at[step], recv_sem=third_recv.at[step],
            device_id=((row + step) % n_rowdev, col), device_id_type=MESH,
        )

    for step in range(1, n_rowdev):
        scatter(step).start()
    value = x_ref[row]
    for step in range(1, n_rowdev):
        scatter(step).wait_recv()
        value = value + got[step]
    mine[...] = value
    for step in range(1, n_coldev):
        share(step).start()
    for step in range(1, n_coldev):
        share(step).wait_recv()
    gathered[0] = mine[...]
    value = gathered[col]
    for place in range(1, n_coldev):
        value = value + gathered[(col - place + n_coldev) % n_coldev]
    whole[...] = value
    for step in range(1, n_rowdev):
        spread(step).start()
    out_ref[row] = whole[...]
    for step in range(1, n_rowdev):
        spread(step).wait_recv()
    for step in range(1, n_rowdev):
        scatter(step).wait_send()
        spread(step).wait_send()
    for step in range(1, n_coldev):
        share(step).wait_send()


def total(n_rowdev, n_coldev, value):
    rows, columns = value.shape
    piece = rows // n_rowdev
    vmem = pl.BlockSpec(memory_space=pltpu.VMEM)
    dma = pltpu.SemaphoreType.DMA
    out = pl.pallas_call(
        functools.partial(total_kernel, n_rowdev, n_coldev),
        out_shape=jax.ShapeDtypeStruct((n_rowdev, piece, columns), jnp.float32),
        in_specs=[vmem],
        out_specs=vmem,
        scratch_shapes=[
            pltpu.VMEM((n_rowdev, piece, columns), jnp.float32),
            pltpu.VMEM((piece, columns), jnp.float32),
            pltpu.VMEM((n_coldev, piece, columns), jnp.float32),
            pltpu.VMEM((piece, columns), jnp.float32),
            dma((n_rowdev,)), dma((n_rowdev,)), dma((n_coldev,)), dma((n_coldev,)),
            dma((n_rowdev,)), dma((n_rowdev,)),
        ],
        compiler_params=pltpu.CompilerParams(collective_id=1, has_side_effects=True),
        name="schur_total",
    )(value.reshape(n_rowdev, piece, columns))
    return out.reshape(rows, columns)


def per_device(inverse, factor, diag_inverse, block_sizes, listed):
    n_rowdev = lax.axis_size("row")
    n_coldev = lax.axis_size("col")
    row_place = lax.axis_index("row")
    col_place = lax.axis_index("col")
    shard_rows, sibling_count, width = factor.shape

    member = membership(
        (row_place * n_coldev + col_place) * shard_rows, shard_rows, block_sizes, listed
    )
    chips = n_rowdev // 2
    if n_rowdev == 2 * n_coldev and chips == 4 and shard_rows % (chips * 32) == 0:
        part = width // 2
        masked = (factor * member[:, :, None]).reshape(shard_rows, 2 * sibling_count, part)
        summed, schur = planar_product(
            n_rowdev, n_coldev, sibling_count, inverse, jnp.transpose(masked, (1, 0, 2))
        )
        ancestor_rows = -(summed.reshape(shard_rows, sibling_count, width) * member[:, :, None])
        schur = schur.reshape(sibling_count, 2, width, part)
        schur = jnp.transpose(schur, (0, 2, 1, 3)).reshape(sibling_count, width, width)
        return (ancestor_rows, diag_inverse + schur)
    own = jnp.transpose(factor, (1, 0, 2))
    summed = general_product(n_rowdev, n_coldev, inverse, own * member.T[:, :, None])
    results = [
        -(summed[s] * member[:, s:s + 1])
        for s in range(sibling_count)
    ]
    terms = [
        lax.dot_general(
            own[s], results[s], (((0,), (0,)), ((), ())),
            precision=lax.Precision.HIGHEST, preferred_element_type=jnp.float32,
        )
        for s in range(sibling_count)
    ]
    schur = total(n_rowdev, n_coldev, jnp.concatenate(terms, axis=0))
    schur = schur.reshape(sibling_count, width, width)
    ancestor_rows = jnp.stack(results, axis=1)
    return (ancestor_rows, diag_inverse - schur)


def solution(mesh):
    in_specs = (P("row", "col"), P(("row", "col"), None, None), P(), P(), P())
    out_specs = (P(("row", "col"), None, None), P())
    return jax.shard_map(
        per_device, mesh=mesh, in_specs=in_specs, out_specs=out_specs, check_vma=False
    )
```

```python
import functools
import math

import jax
import jax.numpy as jnp
from jax import lax
from jax.experimental import pallas as pl
from jax.experimental.pallas import tpu as pltpu
from jax.sharding import PartitionSpec as P

MESH = pl.DeviceIdType.MESH


def membership(first_row, row_total, block_sizes, listed):
    count = block_sizes.shape[0]
    until = lax.broadcasted_iota(jnp.int32, (count, count), 1) <= lax.broadcasted_iota(jnp.int32, (count, count), 0)
    block_ends = jnp.sum(jnp.where(until, block_sizes[None, :], 0), axis=1)
    block_starts = block_ends - block_sizes
    positions = first_row + jnp.arange(row_total, dtype=jnp.int32)
    inside = (
        (positions[:, None] >= block_starts[None, :]) & (positions[:, None] < block_ends[None, :])
    ).astype(jnp.float32)
    return jnp.dot(
        inside,
        listed.astype(jnp.float32).T,
        precision=lax.Precision.HIGHEST,
        preferred_element_type=jnp.float32,
    )


def holder(k, n_rowdev, n_coldev):
    ratio = n_rowdev // n_coldev
    part = k // n_coldev
    place = k % n_coldev
    return (place + (part % 2) * (n_coldev - 1 - 2 * place)) * ratio + part


def shard_of(row, n_rowdev, n_coldev):
    ratio = n_rowdev // n_coldev
    part = row % ratio
    place = row // ratio
    return part * n_coldev + place + (part % 2) * (n_coldev - 1 - 2 * place)


def flip(row, bit):
    return row + bit * (1 - 2 * ((row // bit) % 2))


def general_kernel(
    n_rowdev, n_coldev, parts, depth,
    own_ref, inverse_ref, out_ref,
    panel, high, low, tiles, sums, from_below, from_above,
    gather_send, gather_recv, tile_sem, sum_send, below_recv, above_recv,
):
    row = lax.axis_index("row")
    col = lax.axis_index("col")
    sibling_count, shard_rows, width = own_ref.shape
    col_rows = panel.shape[1]
    piece = shard_rows // parts
    bits = [1 << i for i in range(n_rowdev.bit_length() - 1)]

    number = row * n_coldev + col
    target_row = holder(number % n_rowdev, n_rowdev, n_coldev)
    target_col = number // n_rowdev
    source = col * n_rowdev + shard_of(row, n_rowdev, n_coldev)
    source_row = source // n_coldev
    source_col = source % n_coldev
    moving = target_row * n_coldev + target_col != number

    barrier = pltpu.get_barrier_semaphore()

    def greet(to_row, to_col):
        pl.semaphore_signal(barrier, inc=1, device_id=(to_row, to_col), device_id_type=MESH)

    for bit in bits:
        greet(flip(row, bit), col)

    @pl.when(moving)
    def _():
        greet(target_row, target_col)
        greet(source_row, source_col)

    @pl.when(col > 0)
    def _():
        greet(row, col - 1)

    @pl.when(col < n_coldev - 1)
    def _():
        greet(row, col + 1)

    pl.semaphore_wait(
        barrier,
        len(bits)
        + jnp.where(moving, 2, 0)
        + jnp.where(col > 0, 1, 0)
        + jnp.where(col < n_coldev - 1, 1, 0),
    )

    def place(of_row, part):
        start = shard_of(of_row, n_rowdev, n_coldev) * shard_rows + part * piece
        return pl.ds(pl.multiple_of(start, 8), piece)

    def orders(part):
        rest = bits[1:]
        return (rest if part % 2 else rest[::-1]) + bits[:1]

    def move(s, part):
        return pltpu.make_async_remote_copy(
            src_ref=own_ref.at[s, pl.ds(part * piece, piece)],
            dst_ref=panel.at[s, place(target_row, part)],
            send_sem=gather_send.at[s, part, 0],
            recv_sem=gather_recv.at[s, part, 0],
            device_id=(target_row, target_col),
            device_id_type=MESH,
        )

    def keep(s, part):
        return pltpu.make_async_copy(
            own_ref.at[s, pl.ds(part * piece, piece)],
            panel.at[s, place(row, part)],
            gather_recv.at[s, part, 0],
        )

    def exchanges(s, part, stage):
        order = orders(part)
        held = [row]
        for bit in order[:stage - 1]:
            held = held + [flip(r, bit) for r in held]
        partner = flip(row, order[stage - 1])
        copies = []
        for m, slot in enumerate(held):
            entry = (1 << (stage - 1)) + m
            where = panel.at[s, place(slot, part)]
            copies.append(pltpu.make_async_remote_copy(
                src_ref=where,
                dst_ref=where,
                send_sem=gather_send.at[s, part, entry],
                recv_sem=gather_recv.at[s, part, entry],
                device_id=(partner, col),
                device_id_type=MESH,
            ))
        return copies

    def start_stage(s, part, stage):
        if stage == 0:
            @pl.when(moving)
            def _():
                move(s, part).start()

            @pl.when(jnp.logical_not(moving))
            def _():
                keep(s, part).start()
        else:
            for copy in exchanges(s, part, stage):
                copy.start()

    def end_stage(s, part, stage):
        if stage == 0:
            @pl.when(moving)
            def _():
                move(s, part).wait_recv()

            @pl.when(jnp.logical_not(moving))
            def _():
                keep(s, part).wait()
        else:
            for copy in exchanges(s, part, stage):
                copy.wait_recv()

    items = [(s, part) for s in range(sibling_count) for part in range(parts)]
    for s, part in items:
        start_stage(s, part, 0)

    others = (n_coldev - 1) * parts
    total = n_coldev * parts
    swap = col > n_coldev - 1 - col
    near = jnp.where(swap, n_coldev - 1 - col, col)
    lead = n_coldev - 1 - 2 * near
    minor_total = near * parts

    def plan(t):
        inner = t - lead
        paired = jnp.logical_and(inner >= 0, inner < 2 * minor_total)
        minor = jnp.logical_and(paired, inner % 2 == 1)
        major_at = jnp.where(inner < 0, t, jnp.where(paired, lead + inner // 2, t - minor_total))
        index = jnp.where(minor, inner // 2, major_at)
        up = jnp.where(swap, minor, jnp.logical_not(minor))
        block = jnp.where(up, n_coldev - 1 - index // parts, index // parts)
        is_own = t >= others
        block = jnp.where(is_own, col, block)
        part = jnp.where(is_own, t - others, index % parts)
        up = jnp.logical_and(up, jnp.logical_not(is_own))
        down = jnp.logical_and(jnp.logical_not(up), jnp.logical_not(is_own))
        return block, part, up, down, is_own

    def load(s, t):
        block, part, _, _, _ = plan(t % total)
        start = pl.multiple_of(block * shard_rows + part * piece, 8)
        slot = (s * total + t) % 2
        return pltpu.make_async_copy(
            inverse_ref.at[pl.ds(start, piece)], tiles.at[slot], tile_sem.at[slot]
        )

    load(0, 0).start()

    stages = 1 + len(bits)
    for tick in range(parts + stages):
        for part in range(parts):
            stage = tick - part
            if 0 <= stage < stages:
                end_stage(0, part, stage)
                if stage + 1 < stages:
                    start_stage(0, part, stage + 1)

    step = math.gcd(col_rows, 256)

    def split(s):
        @pl.loop(0, col_rows // step)
        def _(i):
            rows = pl.ds(pl.multiple_of(i * step, step), step)
            value = panel[s, rows, :]
            top = value.astype(jnp.bfloat16)
            high[s, rows, :] = top
            low[s, rows, :] = (value - top.astype(jnp.float32)).astype(jnp.bfloat16)

    def pass_up(s, block, part):
        return pltpu.make_async_remote_copy(
            src_ref=sums.at[s, block, part],
            dst_ref=from_below.at[s, block, part],
            send_sem=sum_send.at[s, block, part],
            recv_sem=below_recv.at[s, block, part],
            device_id=(row, col + 1),
            device_id_type=MESH,
        )

    def pass_down(s, block, part):
        return pltpu.make_async_remote_copy(
            src_ref=sums.at[s, block, part],
            dst_ref=from_above.at[s, block, part],
            send_sem=sum_send.at[s, block, part],
            recv_sem=above_recv.at[s, block, part],
            device_id=(row, col - 1),
            device_id_type=MESH,
        )

    hooks = [(stage, part) for stage in range(stages - 1) for part in range(parts)]

    def advance(s, hook):
        stage, part = hook
        end_stage(s, part, stage)
        start_stage(s, part, stage + 1)

    for s in range(sibling_count):
        split(s)
        follows = s + 1 < sibling_count

        @pl.loop(0, total)
        def _(t):
            block, part, up, down, is_own = plan(t)
            slot = (s * total + t) % 2

            @pl.when(t + 1 < (total + 1 if follows else total))
            def _():
                load(s, t + 1).start()

            load(s, t).wait()
            sums[s, block, part] = jnp.zeros((piece, width), jnp.float32)

            @pl.loop(0, col_rows // depth)
            def _(k):
                span = pl.ds(pl.multiple_of(k * depth, depth), depth)
                value = tiles[slot, :, span]
                top = value.astype(jnp.bfloat16)
                rest = (value - top.astype(jnp.float32)).astype(jnp.bfloat16)
                dot = functools.partial(jnp.dot, preferred_element_type=jnp.float32)
                sums[s, block, part] += (
                    dot(top, low[s, span, :])
                    + dot(rest, high[s, span, :])
                    + dot(top, high[s, span, :])
                )

            @pl.when(jnp.logical_and(jnp.logical_not(down), col > 0))
            def _():
                pass_up(s, block, part).wait_recv()
                sums[s, block, part] += from_below[s, block, part]

            @pl.when(jnp.logical_and(jnp.logical_not(up), col < n_coldev - 1))
            def _():
                pass_down(s, block, part).wait_recv()
                sums[s, block, part] += from_above[s, block, part]

            @pl.when(up)
            def _():
                pass_up(s, block, part).start()

            @pl.when(down)
            def _():
                pass_down(s, block, part).start()

            @pl.when(is_own)
            def _():
                out_ref[s, part] = sums[s, block, part]

            if follows:
                for at, hook in enumerate(hooks[:total]):
                    @pl.when(t == at)
                    def _(hook=hook):
                        advance(s + 1, hook)

        if follows:
            for hook in hooks[total:]:
                advance(s + 1, hook)
            for part in range(parts):
                end_stage(s + 1, part, stages - 1)

    for s in range(sibling_count):
        @pl.loop(0, others)
        def _(t):
            block, part, up, down, _ = plan(t)

            @pl.when(up)
            def _():
                pass_up(s, block, part).wait_send()

            @pl.when(down)
            def _():
                pass_down(s, block, part).wait_send()

    for s, part in items:
        @pl.when(moving)
        def _():
            move(s, part).wait_send()

        for stage in range(1, stages):
            for copy in exchanges(s, part, stage):
                copy.wait_send()


def general_product(n_rowdev, n_coldev, inverse, own):
    sibling_count, shard_rows, width = own.shape
    block_total, col_rows = inverse.shape
    parts = 2 if shard_rows % 16 == 0 else 1
    piece = shard_rows // parts
    depth = math.gcd(col_rows, 1280)
    f32 = jnp.float32
    vmem = pl.BlockSpec(memory_space=pltpu.VMEM)
    out = pl.pallas_call(
        functools.partial(general_kernel, n_rowdev, n_coldev, parts, depth),
        out_shape=jax.ShapeDtypeStruct((sibling_count, parts, piece, width), f32),
        in_specs=[vmem, pl.BlockSpec(memory_space=pl.ANY)],
        out_specs=vmem,
        scratch_shapes=[
            pltpu.VMEM((sibling_count, col_rows, width), f32),
            pltpu.VMEM((sibling_count, col_rows, width), jnp.bfloat16),
            pltpu.VMEM((sibling_count, col_rows, width), jnp.bfloat16),
            pltpu.VMEM((2, piece, col_rows), f32),
            pltpu.VMEM((sibling_count, n_coldev, parts, piece, width), f32),
            pltpu.VMEM((sibling_count, n_coldev, parts, piece, width), f32),
            pltpu.VMEM((sibling_count, n_coldev, parts, piece, width), f32),
            pltpu.SemaphoreType.DMA((sibling_count, parts, n_rowdev)),
            pltpu.SemaphoreType.DMA((sibling_count, parts, n_rowdev)),
            pltpu.SemaphoreType.DMA((2,)),
            pltpu.SemaphoreType.DMA((sibling_count, n_coldev, parts)),
            pltpu.SemaphoreType.DMA((sibling_count, n_coldev, parts)),
            pltpu.SemaphoreType.DMA((sibling_count, n_coldev, parts)),
        ],
        compiler_params=pltpu.CompilerParams(
            collective_id=0, has_side_effects=True, vmem_limit_bytes=60_000_000
        ),
        name="gather_product_scatter",
    )(own, inverse)
    return out.reshape(sibling_count, shard_rows, width)


def planar_kernel(
    n_rowdev, n_coldev, parts, sibling_count, unit_subs, order,
    factor_ref, sizes_ref, listed_ref, inverse_ref, out_ref, schur_ref, *scratch,
):
    units = len(unit_subs)
    scratch = list(scratch)

    def take(count):
        taken_refs = scratch[:count]
        del scratch[:count]
        return taken_refs

    own_ref, member_ref, landing, panel, tiles, across_high, across_low = take(7)
    terms, got, mine_sum, gathered, whole = take(5)
    split_refs, sums, from_below, from_above = (take(units) for _ in range(4))
    (
        spread_send, spread_recv, move_send, move_recv, keep_sem, plane_send, plane_recv,
        core_send, core_recv, tile_sem, sum_send, below_recv, above_recv,
        scatter_send, scatter_recv, share_send, share_recv, result_send, result_recv,
    ) = scratch

    row = lax.axis_index("row")
    col = lax.axis_index("col")
    subs, chips, quarter, width = own_ref.shape
    half = quarter // 2
    shard_rows = chips * quarter
    col_rows = n_rowdev * shard_rows
    piece = shard_rows // parts
    per_sibling = subs // sibling_count
    core = row % 2
    chip = row // 2
    near_x, near_y, other_core = flip(row, 2), flip(row, 4), flip(row, 1)
    firsts = [sum(unit_subs[:u]) for u in range(units)]

    def across(d):
        r = row
        for bit in (1, 2):
            if d & bit:
                r = flip(r, 2 * bit)
        return r

    barrier = pltpu.get_barrier_semaphore()
    greeted = [((row + e) % n_rowdev, col) for e in range(1, n_rowdev)]
    greeted += [(row, (col + e) % n_coldev) for e in range(1, n_coldev)]
    for who in greeted:
        pl.semaphore_signal(barrier, inc=1, device_id=who, device_id_type=MESH)

    f32 = jnp.float32
    count = sizes_ref.shape[1]
    down_axis = lax.broadcasted_iota(jnp.int32, (count, count), 0)
    along_axis = lax.broadcasted_iota(jnp.int32, (count, count), 1)
    sizes = sizes_ref[...].astype(f32)
    upright = jnp.sum(jnp.where(down_axis == along_axis, sizes, 0.0), axis=1, keepdims=True)
    ends = jnp.sum(jnp.where(down_axis <= along_axis, upright, 0.0), axis=0, keepdims=True)
    first_row = (row * n_coldev + col) * shard_rows
    positions = (first_row + lax.broadcasted_iota(jnp.int32, (shard_rows, count), 0)).astype(f32)
    inside = jnp.logical_and(positions >= ends - sizes, positions < ends)
    for s in range(sibling_count):
        chosen = jnp.where(inside, listed_ref[s:s + 1, :].astype(f32), 0.0)
        member_ref[s] = jnp.broadcast_to(
            jnp.sum(chosen, axis=1, keepdims=True), (shard_rows, width)
        )

    def lines(sub):
        at = sub % per_sibling * sibling_count + sub // per_sibling
        return pl.ds(at, shard_rows, stride=subs)

    for sub in range(subs):
        masked = factor_ref[lines(sub), :] * member_ref[sub // per_sibling]
        own_ref[sub] = masked.reshape(chips, quarter, width)

    pl.semaphore_wait(barrier, len(greeted))

    def group(u):
        return pl.ds(firsts[u], unit_subs[u])

    def remote(src, dst, send, recv, to_row, to_col):
        return pltpu.make_async_remote_copy(
            src_ref=src, dst_ref=dst, send_sem=send, recv_sem=recv,
            device_id=(to_row, to_col), device_id_type=MESH,
        )

    def spread(u, d):
        to_row = across(d)
        return remote(
            own_ref.at[group(u), to_row // 2], landing.at[group(u), d - 1],
            spread_send.at[u, d - 1], spread_recv.at[u, d - 1], to_row, col,
        )

    def taken(u, d):
        return own_ref.at[group(u), chip] if d == 0 else landing.at[group(u), d - 1]

    def plane_of(d):
        return across(d) // 2

    def move(u, d):
        return remote(
            taken(u, d), panel.at[group(u), core * n_coldev + col, chip],
            move_send.at[u, d], move_recv.at[u, col], row, plane_of(d),
        )

    def arrival(u, source):
        where = panel.at[group(u), core * n_coldev + source, chip]
        return remote(where, where, move_send.at[u, 0], move_recv.at[u, source], row, source)

    def keep(u, d):
        return pltpu.make_async_copy(
            taken(u, d), panel.at[group(u), core * n_coldev + col, chip], keep_sem.at[u]
        )

    def mine(u, of_chip, part):
        shards = pl.ds(core * n_coldev, n_coldev)
        if part is None:
            return panel.at[group(u), shards, of_chip]
        return panel.at[group(u), shards, of_chip, pl.ds(part * half, half)]

    def in_plane(u, at):
        of_chip, part, to_row = (
            (chip, 0, near_x), (chip, 1, near_y), (chip, 1, near_x), (chip, 0, near_y),
            (near_x // 2, 0, near_y), (near_y // 2, 1, near_x),
        )[at]
        where = mine(u, of_chip, part)
        return remote(where, where, plane_send.at[u, at], plane_recv.at[u, at], to_row, col)

    def to_core(u, d):
        where = mine(u, plane_of(d), None)
        return remote(where, where, core_send.at[u, d], core_recv.at[u, d], other_core, col)

    def stage_spread(u):
        for d in range(1, chips):
            spread(u, d).start()

    def stage_move(u):
        for d in range(chips):
            if d:
                spread(u, d).wait_recv()

            @pl.when(plane_of(d) != col)
            def _():
                move(u, d).start()

            @pl.when(plane_of(d) == col)
            def _():
                keep(u, d).start()

    def stage_plane(u):
        keep(u, 0).wait()
        for e in range(1, n_coldev):
            arrival(u, (col + e) % n_coldev).wait_recv()
        for at in range(4):
            in_plane(u, at).start()
        to_core(u, 0).start()

    def stage_pass(u):
        in_plane(u, 0).wait_recv()
        in_plane(u, 4).start()
        in_plane(u, 1).wait_recv()
        in_plane(u, 5).start()

    def stage_core(u):
        in_plane(u, 2).wait_recv()
        to_core(u, 1).start()
        in_plane(u, 3).wait_recv()
        to_core(u, 2).start()

    def stage_last(u):
        in_plane(u, 4).wait_recv()
        in_plane(u, 5).wait_recv()
        to_core(u, 3).start()

    def stage_ready(u):
        for d in range(chips):
            to_core(u, d).wait_recv()

    def scatter(u, step):
        peer = (row + step) % n_rowdev
        return remote(
            terms.at[group(u), peer], got.at[group(u), step],
            scatter_send.at[u, step], scatter_recv.at[u, step], peer, col,
        )

    def share(u, step):
        return remote(
            mine_sum.at[group(u)], gathered.at[group(u), step],
            share_send.at[u, step], share_recv.at[u, step], row, (col + step) % n_coldev,
        )

    def result(u, step):
        return remote(
            whole.at[group(u)], schur_ref.at[group(u), row],
            result_send.at[u, step], result_recv.at[u, step], (row + step) % n_rowdev, col,
        )

    dot = functools.partial(jnp.dot, preferred_element_type=jnp.float32)
    bf16 = jnp.bfloat16

    def halves(value):
        top = value.astype(bf16)
        return top, (value - top.astype(jnp.float32)).astype(bf16)

    def stage_term(u):
        for part in range(parts):
            @pl.when(col > 0)
            def _():
                pass_up(u, col, part).wait_recv()
                sums[u][col, part] += from_below[u][col, part]

            @pl.when(col < n_coldev - 1)
            def _():
                pass_down(u, col, part).wait_recv()
                sums[u][col, part] += from_above[u][col, part]

        for at in range(unit_subs[u]):
            sub = firsts[u] + at
            value = sums[u][col, :, :, pl.ds(at * width, width)].reshape(shard_rows, width)
            out_ref[lines(sub), :] = -(value * member_ref[sub // per_sibling])
        diagonal_term(u)

    def diagonal_term(u):
        for at in range(unit_subs[u]):
            sub = firsts[u] + at
            sibling = sub // per_sibling
            top, rest = halves(
                sums[u][col, :, :, pl.ds(at * width, width)].reshape(shard_rows, width)
            )
            high, low = across_high[sibling], across_low[sibling]
            term = dot(high, rest) + dot(low, top) + dot(high, top)
            terms[sub] = term.reshape(n_rowdev, term.shape[0] // n_rowdev, width)
        for step in range(1, n_rowdev):
            scatter(u, step).start()

    def stage_share(u):
        value = terms[group(u), row]
        for step in range(1, n_rowdev):
            scatter(u, step).wait_recv()
            value = value + got[group(u), step]
        mine_sum[group(u)] = value
        for step in range(1, n_coldev):
            share(u, step).start()

    def stage_result(u):
        for step in range(1, n_coldev):
            share(u, step).wait_recv()
        gathered[group(u), 0] = mine_sum[group(u)]
        value = gathered[group(u), col]
        for place in range(1, n_coldev):
            value = value + gathered[group(u), (col - place + n_coldev) % n_coldev]
        whole[group(u)] = value
        for step in range(1, n_rowdev):
            result(u, step).start()
        schur_ref[group(u), row] = value

    def stage_done(u):
        for step in range(1, n_rowdev):
            result(u, step).wait_recv()

    late = ((1, 1, 3), (4, 1, 4), (5, 2, 2), (7, 1, 5), (7, 1, 6), (10, 2, 3), (12, 2, 4), (14, 2, 5), (15, 2, 6), (13, 0, 7), (18, 0, 8), (23, 0, 9), (23, 1, 7), (24, 1, 8), (25, 2, 7), (26, 1, 9), (27, 2, 8), (28, 2, 9), (29, 0, 10), (29, 1, 10), (29, 2, 10))
    stages = (stage_spread, stage_move, stage_plane, stage_pass, stage_core, stage_last, stage_ready)
    ready = len(stages) - 1
    after = (stage_term, stage_share, stage_result, stage_done)

    others = (n_coldev - 1) * parts
    total = n_coldev * parts
    swap = col > n_coldev - 1 - col
    near = jnp.where(swap, n_coldev - 1 - col, col)
    lead = n_coldev - 1 - 2 * near
    minor_total = near * parts

    def plan(t):
        inner = t - lead
        paired = jnp.logical_and(inner >= 0, inner < 2 * minor_total)
        minor = jnp.logical_and(paired, inner % 2 == 1)
        major_at = jnp.where(inner < 0, t, jnp.where(paired, lead + inner // 2, t - minor_total))
        index = jnp.where(minor, inner // 2, major_at)
        up = jnp.where(swap, minor, jnp.logical_not(minor))
        block = jnp.where(up, n_coldev - 1 - index // parts, index // parts)
        is_own = t >= others
        block = jnp.where(is_own, col, block)
        part = jnp.where(is_own, t - others, index % parts)
        up = jnp.logical_and(up, jnp.logical_not(is_own))
        down = jnp.logical_and(jnp.logical_not(up), jnp.logical_not(is_own))
        return block, part, up, down

    def load(u, t):
        block, part, _, _ = plan(t % total)
        start = pl.multiple_of(block * shard_rows + part * piece, 8)
        slot = (u * total + t) % 2
        return pltpu.make_async_copy(
            inverse_ref.at[pl.ds(start, piece)], tiles.at[slot], tile_sem.at[slot]
        )

    def split(u):
        wide = unit_subs[u] * width

        @pl.loop(0, n_rowdev)
        def _(i):
            for at in range(unit_subs[u]):
                for j in range(chips):
                    rows = pl.ds(pl.multiple_of(i * shard_rows + j * quarter, 16), quarter)
                    top, rest = halves(panel[firsts[u] + at, i, j])
                    split_refs[u][rows, pl.ds(at * width, width)] = top
                    split_refs[u][rows, pl.ds(wide + at * width, width)] = rest

    def pass_up(u, block, part):
        return remote(
            sums[u].at[block, part], from_below[u].at[block, part],
            sum_send.at[u, block, part], below_recv.at[u, block, part], row, col + 1,
        )

    def pass_down(u, block, part):
        return remote(
            sums[u].at[block, part], from_above[u].at[block, part],
            sum_send.at[u, block, part], above_recv.at[u, block, part], row, col - 1,
        )

    def multiply(u, slot):
        wide = unit_subs[u] * width
        top, rest = halves(tiles[slot])
        if unit_subs[u] == 1:
            main = dot(top, split_refs[u][...])
            return main[:, wide:] + dot(rest, split_refs[u][:, pl.ds(0, wide)]) + main[:, :wide]
        high = split_refs[u][:, pl.ds(0, wide)]
        return dot(top, split_refs[u][:, pl.ds(wide, wide)]) + dot(rest, high) + dot(top, high)

    def turn_own():
        for sub in range(subs):
            value = own_ref[sub].reshape(shard_rows, width)
            top, rest = halves(value.T)
            rows = pl.ds((sub % per_sibling) * width, width)
            across_high[sub // per_sibling, rows, :] = top
            across_low[sub // per_sibling, rows, :] = rest

    def advance(step):
        u, at = step
        (stages + after)[at](u)

    load(0, 0).start()
    for number, step in enumerate(order):
        advance(step)
        if number == 3:
            turn_own()

    for u in range(units):
        split(u)
        follows = u + 1 < units
        timed = [(at % total, (v, n)) for at, v, n in late if at // total == u]

        @pl.loop(0, total)
        def _(t):
            block, part, up, down = plan(t)
            slot = (u * total + t) % 2

            @pl.when(t + 1 < (total + 1 if follows else total))
            def _():
                load(u, t + 1).start()

            load(u, t).wait()
            sums[u][block, part] = multiply(u, slot)

            @pl.when(jnp.logical_and(up, col > 0))
            def _():
                pass_up(u, block, part).wait_recv()
                sums[u][block, part] += from_below[u][block, part]

            @pl.when(jnp.logical_and(down, col < n_coldev - 1))
            def _():
                pass_down(u, block, part).wait_recv()
                sums[u][block, part] += from_above[u][block, part]

            @pl.when(up)
            def _():
                pass_up(u, block, part).start()

            @pl.when(down)
            def _():
                pass_down(u, block, part).start()

            for when, hook in timed:
                @pl.when(t == when)
                def _(hook=hook):
                    advance(hook)

    for at, v, n in late:
        if at // total == units:
            advance((v, n))

    for u in range(units):
        @pl.loop(0, others)
        def _(t):
            block, part, up, down = plan(t)

            @pl.when(up)
            def _():
                pass_up(u, block, part).wait_send()

            @pl.when(down)
            def _():
                pass_down(u, block, part).wait_send()

    for u in range(units):
        for d in range(1, chips):
            spread(u, d).wait_send()
        for d in range(chips):
            @pl.when(plane_of(d) != col)
            def _():
                move(u, d).wait_send()

            to_core(u, d).wait_send()
        for at in range(6):
            in_plane(u, at).wait_send()
        for step in range(1, n_rowdev):
            scatter(u, step).wait_send()
            result(u, step).wait_send()
        for step in range(1, n_coldev):
            share(u, step).wait_send()


def planar_product(n_rowdev, n_coldev, inverse, factor, block_sizes, listed):
    shard_rows, sibling_count, own_columns = factor.shape
    width = own_columns // 2
    subs = 2 * sibling_count
    block_total, col_rows = inverse.shape
    chips = n_rowdev // 2
    quarter = shard_rows // chips
    parts = 2
    piece = shard_rows // parts
    unit_subs = (1, subs - 2, 1)
    units = len(unit_subs)
    order = ((0, 0), (1, 0), (0, 1), (2, 0), (1, 1), (0, 2), (2, 1), (0, 3), (0, 4), (0, 5), (1, 2), (0, 6))
    share_rows = own_columns // n_rowdev
    f32, bf16 = jnp.float32, jnp.bfloat16
    vmem = pl.BlockSpec(memory_space=pltpu.VMEM)
    dma = pltpu.SemaphoreType.DMA
    blocks = [pltpu.VMEM((n_coldev, parts, piece, n * width), f32) for n in unit_subs]
    lines = factor.reshape(shard_rows, sibling_count, 2, width)
    lines = jnp.transpose(lines, (0, 2, 1, 3)).reshape(shard_rows * subs, width)
    out, schur = pl.pallas_call(
        functools.partial(
            planar_kernel, n_rowdev, n_coldev, parts, sibling_count, unit_subs, order
        ),
        out_shape=(
            jax.ShapeDtypeStruct((shard_rows * subs, width), f32),
            jax.ShapeDtypeStruct((subs, n_rowdev, share_rows, width), f32),
        ),
        in_specs=[vmem, vmem, vmem, pl.BlockSpec(memory_space=pl.ANY)],
        out_specs=(vmem, vmem),
        scratch_shapes=[
            pltpu.VMEM((subs, chips, quarter, width), f32),
            pltpu.VMEM((sibling_count, shard_rows, width), f32),
            pltpu.VMEM((subs, chips - 1, quarter, width), f32),
            pltpu.VMEM((subs, n_rowdev, chips, quarter, width), f32),
            pltpu.VMEM((2, piece, col_rows), f32),
            pltpu.VMEM((sibling_count, own_columns, shard_rows), bf16),
            pltpu.VMEM((sibling_count, own_columns, shard_rows), bf16),
            pltpu.VMEM((subs, n_rowdev, share_rows, width), f32),
            pltpu.VMEM((subs, n_rowdev, share_rows, width), f32),
            pltpu.VMEM((subs, share_rows, width), f32),
            pltpu.VMEM((subs, n_coldev, share_rows, width), f32),
            pltpu.VMEM((subs, share_rows, width), f32),
            *[pltpu.VMEM((col_rows, 2 * n * width), bf16) for n in unit_subs],
            *blocks, *blocks, *blocks,
            dma((units, chips - 1)), dma((units, chips - 1)),
            dma((units, chips)), dma((units, n_coldev)), dma((units,)),
            dma((units, 6)), dma((units, 6)),
            dma((units, chips)), dma((units, chips)),
            dma((2,)),
            dma((units, n_coldev, parts)), dma((units, n_coldev, parts)),
            dma((units, n_coldev, parts)),
            dma((units, n_rowdev)), dma((units, n_rowdev)),
            dma((units, n_coldev)), dma((units, n_coldev)),
            dma((units, n_rowdev)), dma((units, n_rowdev)),
        ],
        compiler_params=pltpu.CompilerParams(
            collective_id=0, has_side_effects=True, vmem_limit_bytes=64_000_000
        ),
        name="gather_product_scatter",
    )(lines, block_sizes.reshape(1, -1), listed, inverse)
    rows = jnp.transpose(out.reshape(shard_rows, 2, sibling_count, width), (0, 2, 1, 3))
    schur = jnp.transpose(schur.reshape(sibling_count, 2, own_columns, width), (0, 2, 1, 3))
    return (
        rows.reshape(shard_rows, sibling_count, own_columns),
        schur.reshape(sibling_count, own_columns, own_columns),
    )


def total_kernel(
    n_rowdev, n_coldev, x_ref, out_ref,
    got, mine, gathered, whole, first_send, first_recv, second_send, second_recv,
    third_send, third_recv,
):
    row = lax.axis_index("row")
    col = lax.axis_index("col")
    barrier = pltpu.get_barrier_semaphore()
    for step in range(1, n_rowdev):
        pl.semaphore_signal(
            barrier, inc=1, device_id=((row + step) % n_rowdev, col), device_id_type=MESH
        )
    for step in range(1, n_coldev):
        pl.semaphore_signal(
            barrier, inc=1, device_id=(row, (col + step) % n_coldev), device_id_type=MESH
        )
    pl.semaphore_wait(barrier, n_rowdev + n_coldev - 2)

    def scatter(step):
        peer = (row + step) % n_rowdev
        return pltpu.make_async_remote_copy(
            src_ref=x_ref.at[peer], dst_ref=got.at[step],
            send_sem=first_send.at[step], recv_sem=first_recv.at[step],
            device_id=(peer, col), device_id_type=MESH,
        )

    def share(step):
        return pltpu.make_async_remote_copy(
            src_ref=mine, dst_ref=gathered.at[step],
            send_sem=second_send.at[step], recv_sem=second_recv.at[step],
            device_id=(row, (col + step) % n_coldev), device_id_type=MESH,
        )

    def spread(step):
        return pltpu.make_async_remote_copy(
            src_ref=whole, dst_ref=out_ref.at[row],
            send_sem=third_send.at[step], recv_sem=third_recv.at[step],
            device_id=((row + step) % n_rowdev, col), device_id_type=MESH,
        )

    for step in range(1, n_rowdev):
        scatter(step).start()
    value = x_ref[row]
    for step in range(1, n_rowdev):
        scatter(step).wait_recv()
        value = value + got[step]
    mine[...] = value
    for step in range(1, n_coldev):
        share(step).start()
    for step in range(1, n_coldev):
        share(step).wait_recv()
    gathered[0] = mine[...]
    value = gathered[col]
    for place in range(1, n_coldev):
        value = value + gathered[(col - place + n_coldev) % n_coldev]
    whole[...] = value
    for step in range(1, n_rowdev):
        spread(step).start()
    out_ref[row] = whole[...]
    for step in range(1, n_rowdev):
        spread(step).wait_recv()
    for step in range(1, n_rowdev):
        scatter(step).wait_send()
        spread(step).wait_send()
    for step in range(1, n_coldev):
        share(step).wait_send()


def total(n_rowdev, n_coldev, value):
    rows, columns = value.shape
    piece = rows // n_rowdev
    vmem = pl.BlockSpec(memory_space=pltpu.VMEM)
    dma = pltpu.SemaphoreType.DMA
    out = pl.pallas_call(
        functools.partial(total_kernel, n_rowdev, n_coldev),
        out_shape=jax.ShapeDtypeStruct((n_rowdev, piece, columns), jnp.float32),
        in_specs=[vmem],
        out_specs=vmem,
        scratch_shapes=[
            pltpu.VMEM((n_rowdev, piece, columns), jnp.float32),
            pltpu.VMEM((piece, columns), jnp.float32),
            pltpu.VMEM((n_coldev, piece, columns), jnp.float32),
            pltpu.VMEM((piece, columns), jnp.float32),
            dma((n_rowdev,)), dma((n_rowdev,)), dma((n_coldev,)), dma((n_coldev,)),
            dma((n_rowdev,)), dma((n_rowdev,)),
        ],
        compiler_params=pltpu.CompilerParams(collective_id=1, has_side_effects=True),
        name="schur_total",
    )(value.reshape(n_rowdev, piece, columns))
    return out.reshape(rows, columns)


def per_device(inverse, factor, diag_inverse, block_sizes, listed):
    n_rowdev = lax.axis_size("row")
    n_coldev = lax.axis_size("col")
    row_place = lax.axis_index("row")
    col_place = lax.axis_index("col")
    shard_rows, sibling_count, width = factor.shape

    chips = n_rowdev // 2
    if n_rowdev == 2 * n_coldev and chips == 4 and shard_rows % (chips * 32) == 0:
        ancestor_rows, terms = planar_product(
            n_rowdev, n_coldev, inverse, factor, block_sizes, listed
        )
        return (ancestor_rows, diag_inverse + terms)
    member = membership(
        (row_place * n_coldev + col_place) * shard_rows, shard_rows, block_sizes, listed
    )
    own = jnp.transpose(factor, (1, 0, 2))
    summed = general_product(n_rowdev, n_coldev, inverse, own * member.T[:, :, None])
    results = [
        -(summed[s] * member[:, s:s + 1])
        for s in range(sibling_count)
    ]
    terms = [
        lax.dot_general(
            own[s], results[s], (((0,), (0,)), ((), ())),
            precision=lax.Precision.HIGHEST, preferred_element_type=jnp.float32,
        )
        for s in range(sibling_count)
    ]
    schur = total(n_rowdev, n_coldev, jnp.concatenate(terms, axis=0))
    schur = schur.reshape(sibling_count, width, width)
    ancestor_rows = jnp.stack(results, axis=1)
    return (ancestor_rows, diag_inverse - schur)


def solution(mesh):
    in_specs = (P("row", "col"), P(("row", "col"), None, None), P(), P(), P())
    out_specs = (P(("row", "col"), None, None), P())
    return jax.shard_map(
        per_device, mesh=mesh, in_specs=in_specs, out_specs=out_specs, check_vma=False
    )
```

```python
import functools
import math

import jax
import jax.numpy as jnp
from jax import lax
from jax.experimental import pallas as pl
from jax.experimental.pallas import tpu as pltpu
from jax.sharding import PartitionSpec as P

MESH = pl.DeviceIdType.MESH


def membership(first_row, row_total, block_sizes, listed):
    count = block_sizes.shape[0]
    until = lax.broadcasted_iota(jnp.int32, (count, count), 1) <= lax.broadcasted_iota(jnp.int32, (count, count), 0)
    block_ends = jnp.sum(jnp.where(until, block_sizes[None, :], 0), axis=1)
    block_starts = block_ends - block_sizes
    positions = first_row + jnp.arange(row_total, dtype=jnp.int32)
    inside = (
        (positions[:, None] >= block_starts[None, :]) & (positions[:, None] < block_ends[None, :])
    ).astype(jnp.float32)
    return jnp.dot(
        inside,
        listed.astype(jnp.float32).T,
        precision=lax.Precision.HIGHEST,
        preferred_element_type=jnp.float32,
    )


def holder(k, n_rowdev, n_coldev):
    ratio = n_rowdev // n_coldev
    part = k // n_coldev
    place = k % n_coldev
    return (place + (part % 2) * (n_coldev - 1 - 2 * place)) * ratio + part


def shard_of(row, n_rowdev, n_coldev):
    ratio = n_rowdev // n_coldev
    part = row % ratio
    place = row // ratio
    return part * n_coldev + place + (part % 2) * (n_coldev - 1 - 2 * place)


def flip(row, bit):
    return row + bit * (1 - 2 * ((row // bit) % 2))


def general_kernel(
    n_rowdev, n_coldev, parts, depth,
    own_ref, inverse_ref, out_ref,
    panel, high, low, tiles, sums, from_below, from_above,
    gather_send, gather_recv, tile_sem, sum_send, below_recv, above_recv,
):
    row = lax.axis_index("row")
    col = lax.axis_index("col")
    sibling_count, shard_rows, width = own_ref.shape
    col_rows = panel.shape[1]
    piece = shard_rows // parts
    bits = [1 << i for i in range(n_rowdev.bit_length() - 1)]

    number = row * n_coldev + col
    target_row = holder(number % n_rowdev, n_rowdev, n_coldev)
    target_col = number // n_rowdev
    source = col * n_rowdev + shard_of(row, n_rowdev, n_coldev)
    source_row = source // n_coldev
    source_col = source % n_coldev
    moving = target_row * n_coldev + target_col != number

    barrier = pltpu.get_barrier_semaphore()

    def greet(to_row, to_col):
        pl.semaphore_signal(barrier, inc=1, device_id=(to_row, to_col), device_id_type=MESH)

    for bit in bits:
        greet(flip(row, bit), col)

    @pl.when(moving)
    def _():
        greet(target_row, target_col)
        greet(source_row, source_col)

    @pl.when(col > 0)
    def _():
        greet(row, col - 1)

    @pl.when(col < n_coldev - 1)
    def _():
        greet(row, col + 1)

    pl.semaphore_wait(
        barrier,
        len(bits)
        + jnp.where(moving, 2, 0)
        + jnp.where(col > 0, 1, 0)
        + jnp.where(col < n_coldev - 1, 1, 0),
    )

    def place(of_row, part):
        start = shard_of(of_row, n_rowdev, n_coldev) * shard_rows + part * piece
        return pl.ds(pl.multiple_of(start, 8), piece)

    def orders(part):
        rest = bits[1:]
        return (rest if part % 2 else rest[::-1]) + bits[:1]

    def move(s, part):
        return pltpu.make_async_remote_copy(
            src_ref=own_ref.at[s, pl.ds(part * piece, piece)],
            dst_ref=panel.at[s, place(target_row, part)],
            send_sem=gather_send.at[s, part, 0],
            recv_sem=gather_recv.at[s, part, 0],
            device_id=(target_row, target_col),
            device_id_type=MESH,
        )

    def keep(s, part):
        return pltpu.make_async_copy(
            own_ref.at[s, pl.ds(part * piece, piece)],
            panel.at[s, place(row, part)],
            gather_recv.at[s, part, 0],
        )

    def exchanges(s, part, stage):
        order = orders(part)
        held = [row]
        for bit in order[:stage - 1]:
            held = held + [flip(r, bit) for r in held]
        partner = flip(row, order[stage - 1])
        copies = []
        for m, slot in enumerate(held):
            entry = (1 << (stage - 1)) + m
            where = panel.at[s, place(slot, part)]
            copies.append(pltpu.make_async_remote_copy(
                src_ref=where,
                dst_ref=where,
                send_sem=gather_send.at[s, part, entry],
                recv_sem=gather_recv.at[s, part, entry],
                device_id=(partner, col),
                device_id_type=MESH,
            ))
        return copies

    def start_stage(s, part, stage):
        if stage == 0:
            @pl.when(moving)
            def _():
                move(s, part).start()

            @pl.when(jnp.logical_not(moving))
            def _():
                keep(s, part).start()
        else:
            for copy in exchanges(s, part, stage):
                copy.start()

    def end_stage(s, part, stage):
        if stage == 0:
            @pl.when(moving)
            def _():
                move(s, part).wait_recv()

            @pl.when(jnp.logical_not(moving))
            def _():
                keep(s, part).wait()
        else:
            for copy in exchanges(s, part, stage):
                copy.wait_recv()

    items = [(s, part) for s in range(sibling_count) for part in range(parts)]
    for s, part in items:
        start_stage(s, part, 0)

    others = (n_coldev - 1) * parts
    total = n_coldev * parts
    swap = col > n_coldev - 1 - col
    near = jnp.where(swap, n_coldev - 1 - col, col)
    lead = n_coldev - 1 - 2 * near
    minor_total = near * parts

    def plan(t):
        inner = t - lead
        paired = jnp.logical_and(inner >= 0, inner < 2 * minor_total)
        minor = jnp.logical_and(paired, inner % 2 == 1)
        major_at = jnp.where(inner < 0, t, jnp.where(paired, lead + inner // 2, t - minor_total))
        index = jnp.where(minor, inner // 2, major_at)
        up = jnp.where(swap, minor, jnp.logical_not(minor))
        block = jnp.where(up, n_coldev - 1 - index // parts, index // parts)
        is_own = t >= others
        block = jnp.where(is_own, col, block)
        part = jnp.where(is_own, t - others, index % parts)
        up = jnp.logical_and(up, jnp.logical_not(is_own))
        down = jnp.logical_and(jnp.logical_not(up), jnp.logical_not(is_own))
        return block, part, up, down, is_own

    def load(s, t):
        block, part, _, _, _ = plan(t % total)
        start = pl.multiple_of(block * shard_rows + part * piece, 8)
        slot = (s * total + t) % 2
        return pltpu.make_async_copy(
            inverse_ref.at[pl.ds(start, piece)], tiles.at[slot], tile_sem.at[slot]
        )

    load(0, 0).start()

    stages = 1 + len(bits)
    for tick in range(parts + stages):
        for part in range(parts):
            stage = tick - part
            if 0 <= stage < stages:
                end_stage(0, part, stage)
                if stage + 1 < stages:
                    start_stage(0, part, stage + 1)

    step = math.gcd(col_rows, 256)

    def split(s):
        @pl.loop(0, col_rows // step)
        def _(i):
            rows = pl.ds(pl.multiple_of(i * step, step), step)
            value = panel[s, rows, :]
            top = value.astype(jnp.bfloat16)
            high[s, rows, :] = top
            low[s, rows, :] = (value - top.astype(jnp.float32)).astype(jnp.bfloat16)

    def pass_up(s, block, part):
        return pltpu.make_async_remote_copy(
            src_ref=sums.at[s, block, part],
            dst_ref=from_below.at[s, block, part],
            send_sem=sum_send.at[s, block, part],
            recv_sem=below_recv.at[s, block, part],
            device_id=(row, col + 1),
            device_id_type=MESH,
        )

    def pass_down(s, block, part):
        return pltpu.make_async_remote_copy(
            src_ref=sums.at[s, block, part],
            dst_ref=from_above.at[s, block, part],
            send_sem=sum_send.at[s, block, part],
            recv_sem=above_recv.at[s, block, part],
            device_id=(row, col - 1),
            device_id_type=MESH,
        )

    hooks = [(stage, part) for stage in range(stages - 1) for part in range(parts)]

    def advance(s, hook):
        stage, part = hook
        end_stage(s, part, stage)
        start_stage(s, part, stage + 1)

    for s in range(sibling_count):
        split(s)
        follows = s + 1 < sibling_count

        @pl.loop(0, total)
        def _(t):
            block, part, up, down, is_own = plan(t)
            slot = (s * total + t) % 2

            @pl.when(t + 1 < (total + 1 if follows else total))
            def _():
                load(s, t + 1).start()

            load(s, t).wait()
            sums[s, block, part] = jnp.zeros((piece, width), jnp.float32)

            @pl.loop(0, col_rows // depth)
            def _(k):
                span = pl.ds(pl.multiple_of(k * depth, depth), depth)
                value = tiles[slot, :, span]
                top = value.astype(jnp.bfloat16)
                rest = (value - top.astype(jnp.float32)).astype(jnp.bfloat16)
                dot = functools.partial(jnp.dot, preferred_element_type=jnp.float32)
                sums[s, block, part] += (
                    dot(top, low[s, span, :])
                    + dot(rest, high[s, span, :])
                    + dot(top, high[s, span, :])
                )

            @pl.when(jnp.logical_and(jnp.logical_not(down), col > 0))
            def _():
                pass_up(s, block, part).wait_recv()
                sums[s, block, part] += from_below[s, block, part]

            @pl.when(jnp.logical_and(jnp.logical_not(up), col < n_coldev - 1))
            def _():
                pass_down(s, block, part).wait_recv()
                sums[s, block, part] += from_above[s, block, part]

            @pl.when(up)
            def _():
                pass_up(s, block, part).start()

            @pl.when(down)
            def _():
                pass_down(s, block, part).start()

            @pl.when(is_own)
            def _():
                out_ref[s, part] = sums[s, block, part]

            if follows:
                for at, hook in enumerate(hooks[:total]):
                    @pl.when(t == at)
                    def _(hook=hook):
                        advance(s + 1, hook)

        if follows:
            for hook in hooks[total:]:
                advance(s + 1, hook)
            for part in range(parts):
                end_stage(s + 1, part, stages - 1)

    for s in range(sibling_count):
        @pl.loop(0, others)
        def _(t):
            block, part, up, down, _ = plan(t)

            @pl.when(up)
            def _():
                pass_up(s, block, part).wait_send()

            @pl.when(down)
            def _():
                pass_down(s, block, part).wait_send()

    for s, part in items:
        @pl.when(moving)
        def _():
            move(s, part).wait_send()

        for stage in range(1, stages):
            for copy in exchanges(s, part, stage):
                copy.wait_send()


def general_product(n_rowdev, n_coldev, inverse, own):
    sibling_count, shard_rows, width = own.shape
    block_total, col_rows = inverse.shape
    parts = 2 if shard_rows % 16 == 0 else 1
    piece = shard_rows // parts
    depth = math.gcd(col_rows, 1280)
    f32 = jnp.float32
    vmem = pl.BlockSpec(memory_space=pltpu.VMEM)
    out = pl.pallas_call(
        functools.partial(general_kernel, n_rowdev, n_coldev, parts, depth),
        out_shape=jax.ShapeDtypeStruct((sibling_count, parts, piece, width), f32),
        in_specs=[vmem, pl.BlockSpec(memory_space=pl.ANY)],
        out_specs=vmem,
        scratch_shapes=[
            pltpu.VMEM((sibling_count, col_rows, width), f32),
            pltpu.VMEM((sibling_count, col_rows, width), jnp.bfloat16),
            pltpu.VMEM((sibling_count, col_rows, width), jnp.bfloat16),
            pltpu.VMEM((2, piece, col_rows), f32),
            pltpu.VMEM((sibling_count, n_coldev, parts, piece, width), f32),
            pltpu.VMEM((sibling_count, n_coldev, parts, piece, width), f32),
            pltpu.VMEM((sibling_count, n_coldev, parts, piece, width), f32),
            pltpu.SemaphoreType.DMA((sibling_count, parts, n_rowdev)),
            pltpu.SemaphoreType.DMA((sibling_count, parts, n_rowdev)),
            pltpu.SemaphoreType.DMA((2,)),
            pltpu.SemaphoreType.DMA((sibling_count, n_coldev, parts)),
            pltpu.SemaphoreType.DMA((sibling_count, n_coldev, parts)),
            pltpu.SemaphoreType.DMA((sibling_count, n_coldev, parts)),
        ],
        compiler_params=pltpu.CompilerParams(
            collective_id=0, has_side_effects=True, vmem_limit_bytes=60_000_000
        ),
        name="gather_product_scatter",
    )(own, inverse)
    return out.reshape(sibling_count, shard_rows, width)


def planar_kernel(
    n_rowdev, n_coldev, parts, sibling_count, unit_subs, order,
    factor_ref, sizes_ref, listed_ref, inverse_ref, out_ref, schur_ref, *scratch,
):
    units = len(unit_subs)
    scratch = list(scratch)

    def take(count):
        taken_refs = scratch[:count]
        del scratch[:count]
        return taken_refs

    own_ref, member_ref, landing, panel, tiles, across_high, across_low = take(7)
    terms, got, mine_sum, gathered, whole = take(5)
    split_refs, sums, from_below, from_above = (take(units) for _ in range(4))
    (
        spread_send, spread_recv, move_send, move_recv, keep_sem, plane_send, plane_recv,
        core_send, core_recv, tile_sem, sum_send, below_recv, above_recv,
        scatter_send, scatter_recv, share_send, share_recv, result_send, result_recv,
    ) = scratch

    row = lax.axis_index("row")
    col = lax.axis_index("col")
    subs, chips, quarter, width = own_ref.shape
    half = quarter // 2
    shard_rows = chips * quarter
    col_rows = n_rowdev * shard_rows
    piece = shard_rows // parts
    per_sibling = subs // sibling_count
    core = row % 2
    chip = row // 2
    near_x, near_y, other_core = flip(row, 2), flip(row, 4), flip(row, 1)
    firsts = [sum(unit_subs[:u]) for u in range(units)]

    def across(d):
        r = row
        for bit in (1, 2):
            if d & bit:
                r = flip(r, 2 * bit)
        return r

    barrier = pltpu.get_barrier_semaphore()
    greeted = [((row + e) % n_rowdev, col) for e in range(1, n_rowdev)]
    greeted += [(row, (col + e) % n_coldev) for e in range(1, n_coldev)]
    for who in greeted:
        pl.semaphore_signal(barrier, inc=1, device_id=who, device_id_type=MESH)

    f32 = jnp.float32
    count = sizes_ref.shape[1]
    down_axis = lax.broadcasted_iota(jnp.int32, (count, count), 0)
    along_axis = lax.broadcasted_iota(jnp.int32, (count, count), 1)
    sizes = sizes_ref[...].astype(f32)
    upright = jnp.sum(jnp.where(down_axis == along_axis, sizes, 0.0), axis=1, keepdims=True)
    ends = jnp.sum(jnp.where(down_axis <= along_axis, upright, 0.0), axis=0, keepdims=True)
    first_row = (row * n_coldev + col) * shard_rows
    positions = (first_row + lax.broadcasted_iota(jnp.int32, (shard_rows, count), 0)).astype(f32)
    inside = jnp.logical_and(positions >= ends - sizes, positions < ends)
    for s in range(sibling_count):
        chosen = jnp.where(inside, listed_ref[s:s + 1, :].astype(f32), 0.0)
        member_ref[s] = jnp.broadcast_to(
            jnp.sum(chosen, axis=1, keepdims=True), (shard_rows, width)
        )

    def lines(sub):
        at = sub % per_sibling * sibling_count + sub // per_sibling
        return pl.ds(at, shard_rows, stride=subs)

    for sub in range(subs):
        masked = factor_ref[lines(sub), :] * member_ref[sub // per_sibling]
        own_ref[sub] = masked.reshape(chips, quarter, width)

    pl.semaphore_wait(barrier, len(greeted))

    def group(u):
        return pl.ds(firsts[u], unit_subs[u])

    def remote(src, dst, send, recv, to_row, to_col):
        return pltpu.make_async_remote_copy(
            src_ref=src, dst_ref=dst, send_sem=send, recv_sem=recv,
            device_id=(to_row, to_col), device_id_type=MESH,
        )

    def spread(u, d):
        to_row = across(d)
        return remote(
            own_ref.at[group(u), to_row // 2], landing.at[group(u), d - 1],
            spread_send.at[u, d - 1], spread_recv.at[u, d - 1], to_row, col,
        )

    def taken(u, d):
        return own_ref.at[group(u), chip] if d == 0 else landing.at[group(u), d - 1]

    def plane_of(d):
        return across(d) // 2

    def move(u, d):
        return remote(
            taken(u, d), panel.at[group(u), core * n_coldev + col, chip],
            move_send.at[u, d], move_recv.at[u, col], row, plane_of(d),
        )

    def arrival(u, source):
        where = panel.at[group(u), core * n_coldev + source, chip]
        return remote(where, where, move_send.at[u, 0], move_recv.at[u, source], row, source)

    def keep(u, d):
        return pltpu.make_async_copy(
            taken(u, d), panel.at[group(u), core * n_coldev + col, chip], keep_sem.at[u]
        )

    def mine(u, of_chip, part):
        shards = pl.ds(core * n_coldev, n_coldev)
        if part is None:
            return panel.at[group(u), shards, of_chip]
        return panel.at[group(u), shards, of_chip, pl.ds(part * half, half)]

    def in_plane(u, at):
        of_chip, part, to_row = (
            (chip, 0, near_x), (chip, 1, near_y), (chip, 1, near_x), (chip, 0, near_y),
            (near_x // 2, 0, near_y), (near_y // 2, 1, near_x),
        )[at]
        where = mine(u, of_chip, part)
        return remote(where, where, plane_send.at[u, at], plane_recv.at[u, at], to_row, col)

    def to_core(u, d):
        where = mine(u, plane_of(d), None)
        return remote(where, where, core_send.at[u, d], core_recv.at[u, d], other_core, col)

    def stage_spread(u):
        for d in range(1, chips):
            spread(u, d).start()

    def stage_move(u):
        for d in range(chips):
            if d:
                spread(u, d).wait_recv()

            @pl.when(plane_of(d) != col)
            def _():
                move(u, d).start()

            @pl.when(plane_of(d) == col)
            def _():
                keep(u, d).start()

    def stage_plane(u):
        keep(u, 0).wait()
        for e in range(1, n_coldev):
            arrival(u, (col + e) % n_coldev).wait_recv()
        for at in range(4):
            in_plane(u, at).start()
        to_core(u, 0).start()

    def stage_pass(u):
        in_plane(u, 0).wait_recv()
        in_plane(u, 4).start()
        in_plane(u, 1).wait_recv()
        in_plane(u, 5).start()

    def stage_core(u):
        in_plane(u, 2).wait_recv()
        to_core(u, 1).start()
        in_plane(u, 3).wait_recv()
        to_core(u, 2).start()

    def stage_last(u):
        in_plane(u, 4).wait_recv()
        in_plane(u, 5).wait_recv()
        to_core(u, 3).start()

    def stage_ready(u):
        for d in range(chips):
            to_core(u, d).wait_recv()

    def scatter(u, step):
        peer = (row + step) % n_rowdev
        return remote(
            terms.at[group(u), peer], got.at[group(u), step],
            scatter_send.at[u, step], scatter_recv.at[u, step], peer, col,
        )

    def share(u, step):
        return remote(
            mine_sum.at[group(u)], gathered.at[group(u), step],
            share_send.at[u, step], share_recv.at[u, step], row, (col + step) % n_coldev,
        )

    def result(u, step):
        return remote(
            whole.at[group(u)], schur_ref.at[group(u), row],
            result_send.at[u, step], result_recv.at[u, step], (row + step) % n_rowdev, col,
        )

    dot = functools.partial(jnp.dot, preferred_element_type=jnp.float32)
    bf16 = jnp.bfloat16

    def halves(value):
        top = value.astype(bf16)
        return top, (value - top.astype(jnp.float32)).astype(bf16)

    def stage_term(u):
        for part in range(parts):
            @pl.when(col > 0)
            def _():
                pass_up(u, col, part).wait_recv()
                sums[u][col, part] += from_below[u][col, part]

            @pl.when(col < n_coldev - 1)
            def _():
                pass_down(u, col, part).wait_recv()
                sums[u][col, part] += from_above[u][col, part]

        for at in range(unit_subs[u]):
            sub = firsts[u] + at
            value = sums[u][col, :, :, pl.ds(at * width, width)].reshape(shard_rows, width)
            out_ref[lines(sub), :] = -(value * member_ref[sub // per_sibling])
        diagonal_term(u)

    def diagonal_term(u):
        for at in range(unit_subs[u]):
            sub = firsts[u] + at
            sibling = sub // per_sibling
            top, rest = halves(
                sums[u][col, :, :, pl.ds(at * width, width)].reshape(shard_rows, width)
            )
            high, low = across_high[sibling], across_low[sibling]
            term = dot(high, rest) + dot(low, top) + dot(high, top)
            terms[sub] = term.reshape(n_rowdev, term.shape[0] // n_rowdev, width)
        for step in range(1, n_rowdev):
            scatter(u, step).start()

    def stage_share(u):
        value = terms[group(u), row]
        for step in range(1, n_rowdev):
            scatter(u, step).wait_recv()
            value = value + got[group(u), step]
        mine_sum[group(u)] = value
        for step in range(1, n_coldev):
            share(u, step).start()

    def stage_result(u):
        for step in range(1, n_coldev):
            share(u, step).wait_recv()
        gathered[group(u), 0] = mine_sum[group(u)]
        value = gathered[group(u), col]
        for place in range(1, n_coldev):
            value = value + gathered[group(u), (col - place + n_coldev) % n_coldev]
        whole[group(u)] = value
        for step in range(1, n_rowdev):
            result(u, step).start()
        schur_ref[group(u), row] = value

    def stage_done(u):
        for step in range(1, n_rowdev):
            result(u, step).wait_recv()

    late = ((1, 1, 3), (3, 1, 4), (4, 2, 2), (5, 1, 5), (7, 1, 6), (10, 2, 3), (13, 2, 4), (15, 2, 5), (15, 2, 6), (13, 0, 7), (15, 0, 8), (18, 0, 9), (19, 1, 7), (21, 1, 8), (23, 1, 9), (25, 2, 7), (27, 2, 8), (28, 2, 9), (29, 0, 10), (29, 1, 10), (29, 2, 10))
    stages = (stage_spread, stage_move, stage_plane, stage_pass, stage_core, stage_last, stage_ready)
    ready = len(stages) - 1
    after = (stage_term, stage_share, stage_result, stage_done)

    others = (n_coldev - 1) * parts
    total = n_coldev * parts
    swap = col > n_coldev - 1 - col
    near = jnp.where(swap, n_coldev - 1 - col, col)
    lead = n_coldev - 1 - 2 * near
    minor_total = near * parts

    def plan(t):
        inner = t - lead
        paired = jnp.logical_and(inner >= 0, inner < 2 * minor_total)
        minor = jnp.logical_and(paired, inner % 2 == 1)
        major_at = jnp.where(inner < 0, t, jnp.where(paired, lead + inner // 2, t - minor_total))
        index = jnp.where(minor, inner // 2, major_at)
        up = jnp.where(swap, minor, jnp.logical_not(minor))
        block = jnp.where(up, n_coldev - 1 - index // parts, index // parts)
        is_own = t >= others
        block = jnp.where(is_own, col, block)
        part = jnp.where(is_own, t - others, index % parts)
        up = jnp.logical_and(up, jnp.logical_not(is_own))
        down = jnp.logical_and(jnp.logical_not(up), jnp.logical_not(is_own))
        return block, part, up, down

    def load(u, t):
        block, part, _, _ = plan(t % total)
        start = pl.multiple_of(block * shard_rows + part * piece, 8)
        slot = (u * total + t) % 2
        return pltpu.make_async_copy(
            inverse_ref.at[pl.ds(start, piece)], tiles.at[slot], tile_sem.at[slot]
        )

    def split(u):
        wide = unit_subs[u] * width

        @pl.loop(0, n_rowdev)
        def _(i):
            for at in range(unit_subs[u]):
                for j in range(chips):
                    rows = pl.ds(pl.multiple_of(i * shard_rows + j * quarter, 16), quarter)
                    top, rest = halves(panel[firsts[u] + at, i, j])
                    split_refs[u][rows, pl.ds(at * width, width)] = top
                    split_refs[u][rows, pl.ds(wide + at * width, width)] = rest

    def pass_up(u, block, part):
        return remote(
            sums[u].at[block, part], from_below[u].at[block, part],
            sum_send.at[u, block, part], below_recv.at[u, block, part], row, col + 1,
        )

    def pass_down(u, block, part):
        return remote(
            sums[u].at[block, part], from_above[u].at[block, part],
            sum_send.at[u, block, part], above_recv.at[u, block, part], row, col - 1,
        )

    def multiply(u, slot):
        wide = unit_subs[u] * width
        top, rest = halves(tiles[slot])
        if unit_subs[u] == 1:
            main = dot(top, split_refs[u][...])
            return main[:, wide:] + dot(rest, split_refs[u][:, pl.ds(0, wide)]) + main[:, :wide]
        high = split_refs[u][:, pl.ds(0, wide)]
        return dot(top, split_refs[u][:, pl.ds(wide, wide)]) + dot(rest, high) + dot(top, high)

    def turn_own():
        for sub in range(subs):
            value = own_ref[sub].reshape(shard_rows, width)
            top, rest = halves(value.T)
            rows = pl.ds((sub % per_sibling) * width, width)
            across_high[sub // per_sibling, rows, :] = top
            across_low[sub // per_sibling, rows, :] = rest

    def advance(step):
        u, at = step
        (stages + after)[at](u)

    load(0, 0).start()
    for number, step in enumerate(order):
        advance(step)
        if number == 3:
            turn_own()

    for u in range(units):
        split(u)
        follows = u + 1 < units
        timed = [(at % total, (v, n)) for at, v, n in late if at // total == u]

        @pl.loop(0, total)
        def _(t):
            block, part, up, down = plan(t)
            slot = (u * total + t) % 2

            @pl.when(t + 1 < (total + 1 if follows else total))
            def _():
                load(u, t + 1).start()

            load(u, t).wait()
            sums[u][block, part] = multiply(u, slot)

            @pl.when(jnp.logical_and(up, col > 0))
            def _():
                pass_up(u, block, part).wait_recv()
                sums[u][block, part] += from_below[u][block, part]

            @pl.when(jnp.logical_and(down, col < n_coldev - 1))
            def _():
                pass_down(u, block, part).wait_recv()
                sums[u][block, part] += from_above[u][block, part]

            @pl.when(up)
            def _():
                pass_up(u, block, part).start()

            @pl.when(down)
            def _():
                pass_down(u, block, part).start()

            for when, hook in timed:
                @pl.when(t == when)
                def _(hook=hook):
                    advance(hook)

    for at, v, n in late:
        if at // total == units:
            advance((v, n))

    for u in range(units):
        @pl.loop(0, others)
        def _(t):
            block, part, up, down = plan(t)

            @pl.when(up)
            def _():
                pass_up(u, block, part).wait_send()

            @pl.when(down)
            def _():
                pass_down(u, block, part).wait_send()

    for u in range(units):
        for d in range(1, chips):
            spread(u, d).wait_send()
        for d in range(chips):
            @pl.when(plane_of(d) != col)
            def _():
                move(u, d).wait_send()

            to_core(u, d).wait_send()
        for at in range(6):
            in_plane(u, at).wait_send()
        for step in range(1, n_rowdev):
            scatter(u, step).wait_send()
            result(u, step).wait_send()
        for step in range(1, n_coldev):
            share(u, step).wait_send()


def planar_product(n_rowdev, n_coldev, inverse, factor, block_sizes, listed):
    shard_rows, sibling_count, own_columns = factor.shape
    width = own_columns // 2
    subs = 2 * sibling_count
    block_total, col_rows = inverse.shape
    chips = n_rowdev // 2
    quarter = shard_rows // chips
    parts = 2
    piece = shard_rows // parts
    unit_subs = (1, 1, 2)
    units = len(unit_subs)
    order = ((0, 0), (1, 0), (0, 1), (2, 0), (1, 1), (0, 2), (2, 1), (0, 3), (0, 4), (0, 5), (1, 2), (0, 6))
    share_rows = own_columns // n_rowdev
    f32, bf16 = jnp.float32, jnp.bfloat16
    vmem = pl.BlockSpec(memory_space=pltpu.VMEM)
    dma = pltpu.SemaphoreType.DMA
    blocks = [pltpu.VMEM((n_coldev, parts, piece, n * width), f32) for n in unit_subs]
    lines = factor.reshape(shard_rows, sibling_count, 2, width)
    lines = jnp.transpose(lines, (0, 2, 1, 3)).reshape(shard_rows * subs, width)
    out, schur = pl.pallas_call(
        functools.partial(
            planar_kernel, n_rowdev, n_coldev, parts, sibling_count, unit_subs, order
        ),
        out_shape=(
            jax.ShapeDtypeStruct((shard_rows * subs, width), f32),
            jax.ShapeDtypeStruct((subs, n_rowdev, share_rows, width), f32),
        ),
        in_specs=[vmem, vmem, vmem, pl.BlockSpec(memory_space=pl.ANY)],
        out_specs=(vmem, vmem),
        scratch_shapes=[
            pltpu.VMEM((subs, chips, quarter, width), f32),
            pltpu.VMEM((sibling_count, shard_rows, width), f32),
            pltpu.VMEM((subs, chips - 1, quarter, width), f32),
            pltpu.VMEM((subs, n_rowdev, chips, quarter, width), f32),
            pltpu.VMEM((2, piece, col_rows), f32),
            pltpu.VMEM((sibling_count, own_columns, shard_rows), bf16),
            pltpu.VMEM((sibling_count, own_columns, shard_rows), bf16),
            pltpu.VMEM((subs, n_rowdev, share_rows, width), f32),
            pltpu.VMEM((subs, n_rowdev, share_rows, width), f32),
            pltpu.VMEM((subs, share_rows, width), f32),
            pltpu.VMEM((subs, n_coldev, share_rows, width), f32),
            pltpu.VMEM((subs, share_rows, width), f32),
            *[pltpu.VMEM((col_rows, 2 * n * width), bf16) for n in unit_subs],
            *blocks, *blocks, *blocks,
            dma((units, chips - 1)), dma((units, chips - 1)),
            dma((units, chips)), dma((units, n_coldev)), dma((units,)),
            dma((units, 6)), dma((units, 6)),
            dma((units, chips)), dma((units, chips)),
            dma((2,)),
            dma((units, n_coldev, parts)), dma((units, n_coldev, parts)),
            dma((units, n_coldev, parts)),
            dma((units, n_rowdev)), dma((units, n_rowdev)),
            dma((units, n_coldev)), dma((units, n_coldev)),
            dma((units, n_rowdev)), dma((units, n_rowdev)),
        ],
        compiler_params=pltpu.CompilerParams(
            collective_id=0, has_side_effects=True, vmem_limit_bytes=64_000_000
        ),
        name="gather_product_scatter",
    )(lines, block_sizes.reshape(1, -1), listed, inverse)
    rows = jnp.transpose(out.reshape(shard_rows, 2, sibling_count, width), (0, 2, 1, 3))
    schur = jnp.transpose(schur.reshape(sibling_count, 2, own_columns, width), (0, 2, 1, 3))
    return (
        rows.reshape(shard_rows, sibling_count, own_columns),
        schur.reshape(sibling_count, own_columns, own_columns),
    )


def total_kernel(
    n_rowdev, n_coldev, x_ref, out_ref,
    got, mine, gathered, whole, first_send, first_recv, second_send, second_recv,
    third_send, third_recv,
):
    row = lax.axis_index("row")
    col = lax.axis_index("col")
    barrier = pltpu.get_barrier_semaphore()
    for step in range(1, n_rowdev):
        pl.semaphore_signal(
            barrier, inc=1, device_id=((row + step) % n_rowdev, col), device_id_type=MESH
        )
    for step in range(1, n_coldev):
        pl.semaphore_signal(
            barrier, inc=1, device_id=(row, (col + step) % n_coldev), device_id_type=MESH
        )
    pl.semaphore_wait(barrier, n_rowdev + n_coldev - 2)

    def scatter(step):
        peer = (row + step) % n_rowdev
        return pltpu.make_async_remote_copy(
            src_ref=x_ref.at[peer], dst_ref=got.at[step],
            send_sem=first_send.at[step], recv_sem=first_recv.at[step],
            device_id=(peer, col), device_id_type=MESH,
        )

    def share(step):
        return pltpu.make_async_remote_copy(
            src_ref=mine, dst_ref=gathered.at[step],
            send_sem=second_send.at[step], recv_sem=second_recv.at[step],
            device_id=(row, (col + step) % n_coldev), device_id_type=MESH,
        )

    def spread(step):
        return pltpu.make_async_remote_copy(
            src_ref=whole, dst_ref=out_ref.at[row],
            send_sem=third_send.at[step], recv_sem=third_recv.at[step],
            device_id=((row + step) % n_rowdev, col), device_id_type=MESH,
        )

    for step in range(1, n_rowdev):
        scatter(step).start()
    value = x_ref[row]
    for step in range(1, n_rowdev):
        scatter(step).wait_recv()
        value = value + got[step]
    mine[...] = value
    for step in range(1, n_coldev):
        share(step).start()
    for step in range(1, n_coldev):
        share(step).wait_recv()
    gathered[0] = mine[...]
    value = gathered[col]
    for place in range(1, n_coldev):
        value = value + gathered[(col - place + n_coldev) % n_coldev]
    whole[...] = value
    for step in range(1, n_rowdev):
        spread(step).start()
    out_ref[row] = whole[...]
    for step in range(1, n_rowdev):
        spread(step).wait_recv()
    for step in range(1, n_rowdev):
        scatter(step).wait_send()
        spread(step).wait_send()
    for step in range(1, n_coldev):
        share(step).wait_send()


def total(n_rowdev, n_coldev, value):
    rows, columns = value.shape
    piece = rows // n_rowdev
    vmem = pl.BlockSpec(memory_space=pltpu.VMEM)
    dma = pltpu.SemaphoreType.DMA
    out = pl.pallas_call(
        functools.partial(total_kernel, n_rowdev, n_coldev),
        out_shape=jax.ShapeDtypeStruct((n_rowdev, piece, columns), jnp.float32),
        in_specs=[vmem],
        out_specs=vmem,
        scratch_shapes=[
            pltpu.VMEM((n_rowdev, piece, columns), jnp.float32),
            pltpu.VMEM((piece, columns), jnp.float32),
            pltpu.VMEM((n_coldev, piece, columns), jnp.float32),
            pltpu.VMEM((piece, columns), jnp.float32),
            dma((n_rowdev,)), dma((n_rowdev,)), dma((n_coldev,)), dma((n_coldev,)),
            dma((n_rowdev,)), dma((n_rowdev,)),
        ],
        compiler_params=pltpu.CompilerParams(collective_id=1, has_side_effects=True),
        name="schur_total",
    )(value.reshape(n_rowdev, piece, columns))
    return out.reshape(rows, columns)


def per_device(inverse, factor, diag_inverse, block_sizes, listed):
    n_rowdev = lax.axis_size("row")
    n_coldev = lax.axis_size("col")
    row_place = lax.axis_index("row")
    col_place = lax.axis_index("col")
    shard_rows, sibling_count, width = factor.shape

    chips = n_rowdev // 2
    if n_rowdev == 2 * n_coldev and chips == 4 and shard_rows % (chips * 32) == 0:
        ancestor_rows, terms = planar_product(
            n_rowdev, n_coldev, inverse, factor, block_sizes, listed
        )
        return (ancestor_rows, diag_inverse + terms)
    member = membership(
        (row_place * n_coldev + col_place) * shard_rows, shard_rows, block_sizes, listed
    )
    own = jnp.transpose(factor, (1, 0, 2))
    summed = general_product(n_rowdev, n_coldev, inverse, own * member.T[:, :, None])
    results = [
        -(summed[s] * member[:, s:s + 1])
        for s in range(sibling_count)
    ]
    terms = [
        lax.dot_general(
            own[s], results[s], (((0,), (0,)), ((), ())),
            precision=lax.Precision.HIGHEST, preferred_element_type=jnp.float32,
        )
        for s in range(sibling_count)
    ]
    schur = total(n_rowdev, n_coldev, jnp.concatenate(terms, axis=0))
    schur = schur.reshape(sibling_count, width, width)
    ancestor_rows = jnp.stack(results, axis=1)
    return (ancestor_rows, diag_inverse - schur)


def solution(mesh):
    in_specs = (P("row", "col"), P(("row", "col"), None, None), P(), P(), P())
    out_specs = (P(("row", "col"), None, None), P())
    return jax.shard_map(
        per_device, mesh=mesh, in_specs=in_specs, out_specs=out_specs, check_vma=False
    )
```

```python
import functools
import math

import jax
import jax.numpy as jnp
from jax import lax
from jax.experimental import pallas as pl
from jax.experimental.pallas import tpu as pltpu
from jax.sharding import PartitionSpec as P

MESH = pl.DeviceIdType.MESH


def membership(first_row, row_total, block_sizes, listed):
    count = block_sizes.shape[0]
    until = lax.broadcasted_iota(jnp.int32, (count, count), 1) <= lax.broadcasted_iota(jnp.int32, (count, count), 0)
    block_ends = jnp.sum(jnp.where(until, block_sizes[None, :], 0), axis=1)
    block_starts = block_ends - block_sizes
    positions = first_row + jnp.arange(row_total, dtype=jnp.int32)
    inside = (
        (positions[:, None] >= block_starts[None, :]) & (positions[:, None] < block_ends[None, :])
    ).astype(jnp.float32)
    return jnp.dot(
        inside,
        listed.astype(jnp.float32).T,
        precision=lax.Precision.HIGHEST,
        preferred_element_type=jnp.float32,
    )


def holder(k, n_rowdev, n_coldev):
    ratio = n_rowdev // n_coldev
    part = k // n_coldev
    place = k % n_coldev
    return (place + (part % 2) * (n_coldev - 1 - 2 * place)) * ratio + part


def shard_of(row, n_rowdev, n_coldev):
    ratio = n_rowdev // n_coldev
    part = row % ratio
    place = row // ratio
    return part * n_coldev + place + (part % 2) * (n_coldev - 1 - 2 * place)


def flip(row, bit):
    return row + bit * (1 - 2 * ((row // bit) % 2))


def general_kernel(
    n_rowdev, n_coldev, parts, depth,
    own_ref, inverse_ref, out_ref,
    panel, high, low, tiles, sums, from_below, from_above,
    gather_send, gather_recv, tile_sem, sum_send, below_recv, above_recv,
):
    row = lax.axis_index("row")
    col = lax.axis_index("col")
    sibling_count, shard_rows, width = own_ref.shape
    col_rows = panel.shape[1]
    piece = shard_rows // parts
    bits = [1 << i for i in range(n_rowdev.bit_length() - 1)]

    number = row * n_coldev + col
    target_row = holder(number % n_rowdev, n_rowdev, n_coldev)
    target_col = number // n_rowdev
    source = col * n_rowdev + shard_of(row, n_rowdev, n_coldev)
    source_row = source // n_coldev
    source_col = source % n_coldev
    moving = target_row * n_coldev + target_col != number

    barrier = pltpu.get_barrier_semaphore()

    def greet(to_row, to_col):
        pl.semaphore_signal(barrier, inc=1, device_id=(to_row, to_col), device_id_type=MESH)

    for bit in bits:
        greet(flip(row, bit), col)

    @pl.when(moving)
    def _():
        greet(target_row, target_col)
        greet(source_row, source_col)

    @pl.when(col > 0)
    def _():
        greet(row, col - 1)

    @pl.when(col < n_coldev - 1)
    def _():
        greet(row, col + 1)

    pl.semaphore_wait(
        barrier,
        len(bits)
        + jnp.where(moving, 2, 0)
        + jnp.where(col > 0, 1, 0)
        + jnp.where(col < n_coldev - 1, 1, 0),
    )

    def place(of_row, part):
        start = shard_of(of_row, n_rowdev, n_coldev) * shard_rows + part * piece
        return pl.ds(pl.multiple_of(start, 8), piece)

    def orders(part):
        rest = bits[1:]
        return (rest if part % 2 else rest[::-1]) + bits[:1]

    def move(s, part):
        return pltpu.make_async_remote_copy(
            src_ref=own_ref.at[s, pl.ds(part * piece, piece)],
            dst_ref=panel.at[s, place(target_row, part)],
            send_sem=gather_send.at[s, part, 0],
            recv_sem=gather_recv.at[s, part, 0],
            device_id=(target_row, target_col),
            device_id_type=MESH,
        )

    def keep(s, part):
        return pltpu.make_async_copy(
            own_ref.at[s, pl.ds(part * piece, piece)],
            panel.at[s, place(row, part)],
            gather_recv.at[s, part, 0],
        )

    def exchanges(s, part, stage):
        order = orders(part)
        held = [row]
        for bit in order[:stage - 1]:
            held = held + [flip(r, bit) for r in held]
        partner = flip(row, order[stage - 1])
        copies = []
        for m, slot in enumerate(held):
            entry = (1 << (stage - 1)) + m
            where = panel.at[s, place(slot, part)]
            copies.append(pltpu.make_async_remote_copy(
                src_ref=where,
                dst_ref=where,
                send_sem=gather_send.at[s, part, entry],
                recv_sem=gather_recv.at[s, part, entry],
                device_id=(partner, col),
                device_id_type=MESH,
            ))
        return copies

    def start_stage(s, part, stage):
        if stage == 0:
            @pl.when(moving)
            def _():
                move(s, part).start()

            @pl.when(jnp.logical_not(moving))
            def _():
                keep(s, part).start()
        else:
            for copy in exchanges(s, part, stage):
                copy.start()

    def end_stage(s, part, stage):
        if stage == 0:
            @pl.when(moving)
            def _():
                move(s, part).wait_recv()

            @pl.when(jnp.logical_not(moving))
            def _():
                keep(s, part).wait()
        else:
            for copy in exchanges(s, part, stage):
                copy.wait_recv()

    items = [(s, part) for s in range(sibling_count) for part in range(parts)]
    for s, part in items:
        start_stage(s, part, 0)

    others = (n_coldev - 1) * parts
    total = n_coldev * parts
    swap = col > n_coldev - 1 - col
    near = jnp.where(swap, n_coldev - 1 - col, col)
    lead = n_coldev - 1 - 2 * near
    minor_total = near * parts

    def plan(t):
        inner = t - lead
        paired = jnp.logical_and(inner >= 0, inner < 2 * minor_total)
        minor = jnp.logical_and(paired, inner % 2 == 1)
        major_at = jnp.where(inner < 0, t, jnp.where(paired, lead + inner // 2, t - minor_total))
        index = jnp.where(minor, inner // 2, major_at)
        up = jnp.where(swap, minor, jnp.logical_not(minor))
        block = jnp.where(up, n_coldev - 1 - index // parts, index // parts)
        is_own = t >= others
        block = jnp.where(is_own, col, block)
        part = jnp.where(is_own, t - others, index % parts)
        up = jnp.logical_and(up, jnp.logical_not(is_own))
        down = jnp.logical_and(jnp.logical_not(up), jnp.logical_not(is_own))
        return block, part, up, down, is_own

    def load(s, t):
        block, part, _, _, _ = plan(t % total)
        start = pl.multiple_of(block * shard_rows + part * piece, 8)
        slot = (s * total + t) % 2
        return pltpu.make_async_copy(
            inverse_ref.at[pl.ds(start, piece)], tiles.at[slot], tile_sem.at[slot]
        )

    load(0, 0).start()

    stages = 1 + len(bits)
    for tick in range(parts + stages):
        for part in range(parts):
            stage = tick - part
            if 0 <= stage < stages:
                end_stage(0, part, stage)
                if stage + 1 < stages:
                    start_stage(0, part, stage + 1)

    step = math.gcd(col_rows, 256)

    def split(s):
        @pl.loop(0, col_rows // step)
        def _(i):
            rows = pl.ds(pl.multiple_of(i * step, step), step)
            value = panel[s, rows, :]
            top = value.astype(jnp.bfloat16)
            high[s, rows, :] = top
            low[s, rows, :] = (value - top.astype(jnp.float32)).astype(jnp.bfloat16)

    def pass_up(s, block, part):
        return pltpu.make_async_remote_copy(
            src_ref=sums.at[s, block, part],
            dst_ref=from_below.at[s, block, part],
            send_sem=sum_send.at[s, block, part],
            recv_sem=below_recv.at[s, block, part],
            device_id=(row, col + 1),
            device_id_type=MESH,
        )

    def pass_down(s, block, part):
        return pltpu.make_async_remote_copy(
            src_ref=sums.at[s, block, part],
            dst_ref=from_above.at[s, block, part],
            send_sem=sum_send.at[s, block, part],
            recv_sem=above_recv.at[s, block, part],
            device_id=(row, col - 1),
            device_id_type=MESH,
        )

    hooks = [(stage, part) for stage in range(stages - 1) for part in range(parts)]

    def advance(s, hook):
        stage, part = hook
        end_stage(s, part, stage)
        start_stage(s, part, stage + 1)

    for s in range(sibling_count):
        split(s)
        follows = s + 1 < sibling_count

        @pl.loop(0, total)
        def _(t):
            block, part, up, down, is_own = plan(t)
            slot = (s * total + t) % 2

            @pl.when(t + 1 < (total + 1 if follows else total))
            def _():
                load(s, t + 1).start()

            load(s, t).wait()
            sums[s, block, part] = jnp.zeros((piece, width), jnp.float32)

            @pl.loop(0, col_rows // depth)
            def _(k):
                span = pl.ds(pl.multiple_of(k * depth, depth), depth)
                value = tiles[slot, :, span]
                top = value.astype(jnp.bfloat16)
                rest = (value - top.astype(jnp.float32)).astype(jnp.bfloat16)
                dot = functools.partial(jnp.dot, preferred_element_type=jnp.float32)
                sums[s, block, part] += (
                    dot(top, low[s, span, :])
                    + dot(rest, high[s, span, :])
                    + dot(top, high[s, span, :])
                )

            @pl.when(jnp.logical_and(jnp.logical_not(down), col > 0))
            def _():
                pass_up(s, block, part).wait_recv()
                sums[s, block, part] += from_below[s, block, part]

            @pl.when(jnp.logical_and(jnp.logical_not(up), col < n_coldev - 1))
            def _():
                pass_down(s, block, part).wait_recv()
                sums[s, block, part] += from_above[s, block, part]

            @pl.when(up)
            def _():
                pass_up(s, block, part).start()

            @pl.when(down)
            def _():
                pass_down(s, block, part).start()

            @pl.when(is_own)
            def _():
                out_ref[s, part] = sums[s, block, part]

            if follows:
                for at, hook in enumerate(hooks[:total]):
                    @pl.when(t == at)
                    def _(hook=hook):
                        advance(s + 1, hook)

        if follows:
            for hook in hooks[total:]:
                advance(s + 1, hook)
            for part in range(parts):
                end_stage(s + 1, part, stages - 1)

    for s in range(sibling_count):
        @pl.loop(0, others)
        def _(t):
            block, part, up, down, _ = plan(t)

            @pl.when(up)
            def _():
                pass_up(s, block, part).wait_send()

            @pl.when(down)
            def _():
                pass_down(s, block, part).wait_send()

    for s, part in items:
        @pl.when(moving)
        def _():
            move(s, part).wait_send()

        for stage in range(1, stages):
            for copy in exchanges(s, part, stage):
                copy.wait_send()


def general_product(n_rowdev, n_coldev, inverse, own):
    sibling_count, shard_rows, width = own.shape
    block_total, col_rows = inverse.shape
    parts = 2 if shard_rows % 16 == 0 else 1
    piece = shard_rows // parts
    depth = math.gcd(col_rows, 1280)
    f32 = jnp.float32
    vmem = pl.BlockSpec(memory_space=pltpu.VMEM)
    out = pl.pallas_call(
        functools.partial(general_kernel, n_rowdev, n_coldev, parts, depth),
        out_shape=jax.ShapeDtypeStruct((sibling_count, parts, piece, width), f32),
        in_specs=[vmem, pl.BlockSpec(memory_space=pl.ANY)],
        out_specs=vmem,
        scratch_shapes=[
            pltpu.VMEM((sibling_count, col_rows, width), f32),
            pltpu.VMEM((sibling_count, col_rows, width), jnp.bfloat16),
            pltpu.VMEM((sibling_count, col_rows, width), jnp.bfloat16),
            pltpu.VMEM((2, piece, col_rows), f32),
            pltpu.VMEM((sibling_count, n_coldev, parts, piece, width), f32),
            pltpu.VMEM((sibling_count, n_coldev, parts, piece, width), f32),
            pltpu.VMEM((sibling_count, n_coldev, parts, piece, width), f32),
            pltpu.SemaphoreType.DMA((sibling_count, parts, n_rowdev)),
            pltpu.SemaphoreType.DMA((sibling_count, parts, n_rowdev)),
            pltpu.SemaphoreType.DMA((2,)),
            pltpu.SemaphoreType.DMA((sibling_count, n_coldev, parts)),
            pltpu.SemaphoreType.DMA((sibling_count, n_coldev, parts)),
            pltpu.SemaphoreType.DMA((sibling_count, n_coldev, parts)),
        ],
        compiler_params=pltpu.CompilerParams(
            collective_id=0, has_side_effects=True, vmem_limit_bytes=60_000_000
        ),
        name="gather_product_scatter",
    )(own, inverse)
    return out.reshape(sibling_count, shard_rows, width)


def planar_kernel(
    n_rowdev, n_coldev, parts, sibling_count, unit_subs, order,
    factor_ref, sizes_ref, listed_ref, inverse_ref, out_ref, schur_ref, *scratch,
):
    units = len(unit_subs)
    scratch = list(scratch)

    def take(count):
        taken_refs = scratch[:count]
        del scratch[:count]
        return taken_refs

    own_ref, member_ref, landing, panel, tiles, across_high, across_low = take(7)
    terms, got, mine_sum, gathered, whole = take(5)
    split_refs, sums, from_below, from_above = (take(units) for _ in range(4))
    (
        spread_send, spread_recv, move_send, move_recv, keep_sem, plane_send, plane_recv,
        core_send, core_recv, tile_sem, sum_send, below_recv, above_recv,
        scatter_send, scatter_recv, share_send, share_recv, result_send, result_recv,
    ) = scratch

    row = lax.axis_index("row")
    col = lax.axis_index("col")
    subs, chips, quarter, width = own_ref.shape
    half = quarter // 2
    shard_rows = chips * quarter
    col_rows = n_rowdev * shard_rows
    piece = shard_rows // parts
    per_sibling = subs // sibling_count
    core = row % 2
    chip = row // 2
    near_x, near_y, other_core = flip(row, 2), flip(row, 4), flip(row, 1)
    firsts = [sum(unit_subs[:u]) for u in range(units)]

    def across(d):
        r = row
        for bit in (1, 2):
            if d & bit:
                r = flip(r, 2 * bit)
        return r

    barrier = pltpu.get_barrier_semaphore()
    greeted = [((row + e) % n_rowdev, col) for e in range(1, n_rowdev)]
    greeted += [(row, (col + e) % n_coldev) for e in range(1, n_coldev)]
    for who in greeted:
        pl.semaphore_signal(barrier, inc=1, device_id=who, device_id_type=MESH)

    f32 = jnp.float32
    count = sizes_ref.shape[1]
    down_axis = lax.broadcasted_iota(jnp.int32, (count, count), 0)
    along_axis = lax.broadcasted_iota(jnp.int32, (count, count), 1)
    sizes = sizes_ref[...].astype(f32)
    upright = jnp.sum(jnp.where(down_axis == along_axis, sizes, 0.0), axis=1, keepdims=True)
    ends = jnp.sum(jnp.where(down_axis <= along_axis, upright, 0.0), axis=0, keepdims=True)
    first_row = (row * n_coldev + col) * shard_rows
    positions = (first_row + lax.broadcasted_iota(jnp.int32, (shard_rows, count), 0)).astype(f32)
    inside = jnp.logical_and(positions >= ends - sizes, positions < ends)
    for s in range(sibling_count):
        chosen = jnp.where(inside, listed_ref[s:s + 1, :].astype(f32), 0.0)
        member_ref[s] = jnp.broadcast_to(
            jnp.sum(chosen, axis=1, keepdims=True), (shard_rows, width)
        )

    def lines(sub):
        at = sub % per_sibling * sibling_count + sub // per_sibling
        return pl.ds(at, shard_rows, stride=subs)

    for sub in range(subs):
        masked = factor_ref[lines(sub), :] * member_ref[sub // per_sibling]
        own_ref[sub] = masked.reshape(chips, quarter, width)

    pl.semaphore_wait(barrier, len(greeted))

    def group(u):
        return pl.ds(firsts[u], unit_subs[u])

    def remote(src, dst, send, recv, to_row, to_col):
        return pltpu.make_async_remote_copy(
            src_ref=src, dst_ref=dst, send_sem=send, recv_sem=recv,
            device_id=(to_row, to_col), device_id_type=MESH,
        )

    def spread(u, d):
        to_row = across(d)
        return remote(
            own_ref.at[group(u), to_row // 2], landing.at[group(u), d - 1],
            spread_send.at[u, d - 1], spread_recv.at[u, d - 1], to_row, col,
        )

    def taken(u, d):
        return own_ref.at[group(u), chip] if d == 0 else landing.at[group(u), d - 1]

    def plane_of(d):
        return across(d) // 2

    def move(u, d):
        return remote(
            taken(u, d), panel.at[group(u), core * n_coldev + col, chip],
            move_send.at[u, d], move_recv.at[u, col], row, plane_of(d),
        )

    def arrival(u, source):
        where = panel.at[group(u), core * n_coldev + source, chip]
        return remote(where, where, move_send.at[u, 0], move_recv.at[u, source], row, source)

    def keep(u, d):
        return pltpu.make_async_copy(
            taken(u, d), panel.at[group(u), core * n_coldev + col, chip], keep_sem.at[u]
        )

    def mine(u, of_chip, part):
        shards = pl.ds(core * n_coldev, n_coldev)
        if part is None:
            return panel.at[group(u), shards, of_chip]
        return panel.at[group(u), shards, of_chip, pl.ds(part * half, half)]

    def in_plane(u, at):
        of_chip, part, to_row = (
            (chip, 0, near_x), (chip, 1, near_y), (chip, 1, near_x), (chip, 0, near_y),
            (near_x // 2, 0, near_y), (near_y // 2, 1, near_x),
        )[at]
        where = mine(u, of_chip, part)
        return remote(where, where, plane_send.at[u, at], plane_recv.at[u, at], to_row, col)

    def to_core(u, d):
        where = mine(u, plane_of(d), None)
        return remote(where, where, core_send.at[u, d], core_recv.at[u, d], other_core, col)

    def stage_spread(u):
        for d in range(1, chips):
            spread(u, d).start()

    def stage_move(u):
        for d in range(chips):
            if d:
                spread(u, d).wait_recv()

            @pl.when(plane_of(d) != col)
            def _():
                move(u, d).start()

            @pl.when(plane_of(d) == col)
            def _():
                keep(u, d).start()

    def stage_plane(u):
        keep(u, 0).wait()
        for e in range(1, n_coldev):
            arrival(u, (col + e) % n_coldev).wait_recv()
        for at in range(4):
            in_plane(u, at).start()
        to_core(u, 0).start()

    def stage_pass(u):
        in_plane(u, 0).wait_recv()
        in_plane(u, 4).start()
        in_plane(u, 1).wait_recv()
        in_plane(u, 5).start()

    def stage_core(u):
        in_plane(u, 2).wait_recv()
        to_core(u, 1).start()
        in_plane(u, 3).wait_recv()
        to_core(u, 2).start()

    def stage_last(u):
        in_plane(u, 4).wait_recv()
        in_plane(u, 5).wait_recv()
        to_core(u, 3).start()

    def stage_ready(u):
        for d in range(chips):
            to_core(u, d).wait_recv()

    def peer_of(d):
        r = row
        for at in range(n_rowdev.bit_length() - 1):
            if d >> at & 1:
                r = flip(r, 1 << at)
        return r

    peers = range(n_rowdev - 1, 0, -1)

    def scatter(sub, step):
        peer = peer_of(step)
        return remote(
            terms.at[sub, peer], got.at[sub, step],
            scatter_send.at[sub, step], scatter_recv.at[sub, step], peer, col,
        )

    def share(sub, step):
        return remote(
            mine_sum.at[sub], gathered.at[sub, step],
            share_send.at[sub, step], share_recv.at[sub, step], row, (col + step) % n_coldev,
        )

    def block_of(sub):
        lanes = pl.ds(sub % per_sibling * width, width)
        return schur_ref.at[sub // per_sibling, row, :, lanes]

    def subs_of(u):
        return range(firsts[u], firsts[u] + unit_subs[u])

    def result(sub, d):
        return remote(
            whole.at[sub], block_of(sub),
            result_send.at[sub, d], result_recv.at[sub, d], peer_of(d), col,
        )

    dot = functools.partial(jnp.dot, preferred_element_type=jnp.float32)
    bf16 = jnp.bfloat16

    def halves(value):
        top = value.astype(bf16)
        return top, (value - top.astype(jnp.float32)).astype(bf16)

    def stage_term(u):
        for part in range(parts):
            @pl.when(col > 0)
            def _():
                pass_up(u, col, part).wait_recv()
                sums[u][col, part] += from_below[u][col, part]

            @pl.when(col < n_coldev - 1)
            def _():
                pass_down(u, col, part).wait_recv()
                sums[u][col, part] += from_above[u][col, part]

        def finished(at):
            value = sums[u][col, :, :, pl.ds(at * width, width)]
            return value.reshape(shard_rows, width)

        for at, sub in enumerate(subs_of(u)):
            sibling = sub // per_sibling
            top, rest = halves(finished(at))
            high, low = across_high[sibling], across_low[sibling]
            term = dot(high, rest) + dot(low, top) + dot(high, top)
            terms[sub] = term.reshape(n_rowdev, term.shape[0] // n_rowdev, width)
            for step in peers:
                scatter(sub, step).start()
        for at, sub in enumerate(subs_of(u)):
            out_ref[lines(sub), :] = -(finished(at) * member_ref[sub // per_sibling])

    def stage_share(u):
        for sub in subs_of(u):
            value = terms[sub, row]
            for step in peers[::-1]:
                scatter(sub, step).wait_recv()
                value = value + got[sub, step]
            mine_sum[sub] = value
            for step in range(1, n_coldev):
                share(sub, step).start()

    def stage_result(u):
        for sub in subs_of(u):
            for step in range(1, n_coldev):
                share(sub, step).wait_recv()
            gathered[sub, 0] = mine_sum[sub]
            value = gathered[sub, col]
            for place in range(1, n_coldev):
                value = value + gathered[sub, (col - place + n_coldev) % n_coldev]
            whole[sub] = value
            for d in peers:
                result(sub, d).start()
            block_of(sub)[...] = whole[sub]

    def stage_done(u):
        for sub in subs_of(u):
            for d in peers[::-1]:
                result(sub, d).wait_recv()

    late = ((1, 1, 3), (3, 1, 4), (4, 2, 2), (5, 1, 5), (7, 1, 6), (10, 2, 3), (13, 2, 4), (15, 2, 5), (15, 2, 6), (13, 0, 7), (15, 0, 8), (18, 0, 9), (19, 1, 7), (21, 1, 8), (23, 1, 9), (25, 2, 7), (27, 2, 8), (28, 2, 9), (29, 0, 10), (29, 1, 10), (29, 2, 10))
    stages = (stage_spread, stage_move, stage_plane, stage_pass, stage_core, stage_last, stage_ready)
    ready = len(stages) - 1
    after = (stage_term, stage_share, stage_result, stage_done)

    others = (n_coldev - 1) * parts
    total = n_coldev * parts
    swap = col > n_coldev - 1 - col
    near = jnp.where(swap, n_coldev - 1 - col, col)
    lead = n_coldev - 1 - 2 * near
    minor_total = near * parts

    def plan(t):
        inner = t - lead
        paired = jnp.logical_and(inner >= 0, inner < 2 * minor_total)
        minor = jnp.logical_and(paired, inner % 2 == 1)
        major_at = jnp.where(inner < 0, t, jnp.where(paired, lead + inner // 2, t - minor_total))
        index = jnp.where(minor, inner // 2, major_at)
        up = jnp.where(swap, minor, jnp.logical_not(minor))
        block = jnp.where(up, n_coldev - 1 - index // parts, index // parts)
        is_own = t >= others
        block = jnp.where(is_own, col, block)
        part = jnp.where(is_own, t - others, index % parts)
        up = jnp.logical_and(up, jnp.logical_not(is_own))
        down = jnp.logical_and(jnp.logical_not(up), jnp.logical_not(is_own))
        return block, part, up, down

    def load(u, t):
        block, part, _, _ = plan(t % total)
        start = pl.multiple_of(block * shard_rows + part * piece, 8)
        slot = (u * total + t) % 2
        return pltpu.make_async_copy(
            inverse_ref.at[pl.ds(start, piece)], tiles.at[slot], tile_sem.at[slot]
        )

    def split(u):
        wide = unit_subs[u] * width

        @pl.loop(0, n_rowdev)
        def _(i):
            for at in range(unit_subs[u]):
                for j in range(chips):
                    rows = pl.ds(pl.multiple_of(i * shard_rows + j * quarter, 16), quarter)
                    top, rest = halves(panel[firsts[u] + at, i, j])
                    split_refs[u][rows, pl.ds(at * width, width)] = top
                    split_refs[u][rows, pl.ds(wide + at * width, width)] = rest

    def pass_up(u, block, part):
        return remote(
            sums[u].at[block, part], from_below[u].at[block, part],
            sum_send.at[u, block, part], below_recv.at[u, block, part], row, col + 1,
        )

    def pass_down(u, block, part):
        return remote(
            sums[u].at[block, part], from_above[u].at[block, part],
            sum_send.at[u, block, part], above_recv.at[u, block, part], row, col - 1,
        )

    def multiply(u, slot):
        wide = unit_subs[u] * width
        top, rest = halves(tiles[slot])
        if unit_subs[u] == 1:
            main = dot(top, split_refs[u][...])
            return main[:, wide:] + dot(rest, split_refs[u][:, pl.ds(0, wide)]) + main[:, :wide]
        high = split_refs[u][:, pl.ds(0, wide)]
        return dot(top, split_refs[u][:, pl.ds(wide, wide)]) + dot(rest, high) + dot(top, high)

    def turn_own():
        for sub in range(subs):
            value = own_ref[sub].reshape(shard_rows, width)
            top, rest = halves(value.T)
            rows = pl.ds((sub % per_sibling) * width, width)
            across_high[sub // per_sibling, rows, :] = top
            across_low[sub // per_sibling, rows, :] = rest

    def advance(step):
        u, at = step
        (stages + after)[at](u)

    load(0, 0).start()
    for number, step in enumerate(order):
        advance(step)
        if number == 3:
            turn_own()

    for u in range(units):
        split(u)
        follows = u + 1 < units
        timed = [(at % total, (v, n)) for at, v, n in late if at // total == u]

        @pl.loop(0, total)
        def _(t):
            block, part, up, down = plan(t)
            slot = (u * total + t) % 2

            @pl.when(t + 1 < (total + 1 if follows else total))
            def _():
                load(u, t + 1).start()

            load(u, t).wait()
            sums[u][block, part] = multiply(u, slot)

            @pl.when(jnp.logical_and(up, col > 0))
            def _():
                pass_up(u, block, part).wait_recv()
                sums[u][block, part] += from_below[u][block, part]

            @pl.when(jnp.logical_and(down, col < n_coldev - 1))
            def _():
                pass_down(u, block, part).wait_recv()
                sums[u][block, part] += from_above[u][block, part]

            @pl.when(up)
            def _():
                pass_up(u, block, part).start()

            @pl.when(down)
            def _():
                pass_down(u, block, part).start()

            for when, hook in timed:
                @pl.when(t == when)
                def _(hook=hook):
                    advance(hook)

    for at, v, n in late:
        if at // total == units:
            advance((v, n))

    for u in range(units):
        @pl.loop(0, others)
        def _(t):
            block, part, up, down = plan(t)

            @pl.when(up)
            def _():
                pass_up(u, block, part).wait_send()

            @pl.when(down)
            def _():
                pass_down(u, block, part).wait_send()

    for u in range(units):
        for d in range(1, chips):
            spread(u, d).wait_send()
        for d in range(chips):
            @pl.when(plane_of(d) != col)
            def _():
                move(u, d).wait_send()

            to_core(u, d).wait_send()
        for at in range(6):
            in_plane(u, at).wait_send()
        for sub in subs_of(u):
            for step in peers:
                scatter(sub, step).wait_send()
                result(sub, step).wait_send()
            for step in range(1, n_coldev):
                share(sub, step).wait_send()


def planar_product(n_rowdev, n_coldev, inverse, factor, block_sizes, listed):
    shard_rows, sibling_count, own_columns = factor.shape
    width = own_columns // 2
    subs = 2 * sibling_count
    block_total, col_rows = inverse.shape
    chips = n_rowdev // 2
    quarter = shard_rows // chips
    parts = 2
    piece = shard_rows // parts
    unit_subs = (1, 1, 2)
    units = len(unit_subs)
    order = ((0, 0), (1, 0), (0, 1), (2, 0), (1, 1), (0, 2), (2, 1), (0, 3), (0, 4), (0, 5), (1, 2), (0, 6))
    share_rows = own_columns // n_rowdev
    f32, bf16 = jnp.float32, jnp.bfloat16
    vmem = pl.BlockSpec(memory_space=pltpu.VMEM)
    dma = pltpu.SemaphoreType.DMA
    blocks = [pltpu.VMEM((n_coldev, parts, piece, n * width), f32) for n in unit_subs]
    lines = factor.reshape(shard_rows, sibling_count, 2, width)
    lines = jnp.transpose(lines, (0, 2, 1, 3)).reshape(shard_rows * subs, width)
    out, schur = pl.pallas_call(
        functools.partial(
            planar_kernel, n_rowdev, n_coldev, parts, sibling_count, unit_subs, order
        ),
        out_shape=(
            jax.ShapeDtypeStruct((shard_rows * subs, width), f32),
            jax.ShapeDtypeStruct((sibling_count, n_rowdev, share_rows, own_columns), f32),
        ),
        in_specs=[vmem, vmem, vmem, pl.BlockSpec(memory_space=pl.ANY)],
        out_specs=(vmem, vmem),
        scratch_shapes=[
            pltpu.VMEM((subs, chips, quarter, width), f32),
            pltpu.VMEM((sibling_count, shard_rows, width), f32),
            pltpu.VMEM((subs, chips - 1, quarter, width), f32),
            pltpu.VMEM((subs, n_rowdev, chips, quarter, width), f32),
            pltpu.VMEM((2, piece, col_rows), f32),
            pltpu.VMEM((sibling_count, own_columns, shard_rows), bf16),
            pltpu.VMEM((sibling_count, own_columns, shard_rows), bf16),
            pltpu.VMEM((subs, n_rowdev, share_rows, width), f32),
            pltpu.VMEM((subs, n_rowdev, share_rows, width), f32),
            pltpu.VMEM((subs, share_rows, width), f32),
            pltpu.VMEM((subs, n_coldev, share_rows, width), f32),
            pltpu.VMEM((subs, share_rows, width), f32),
            *[pltpu.VMEM((col_rows, 2 * n * width), bf16) for n in unit_subs],
            *blocks, *blocks, *blocks,
            dma((units, chips - 1)), dma((units, chips - 1)),
            dma((units, chips)), dma((units, n_coldev)), dma((units,)),
            dma((units, 6)), dma((units, 6)),
            dma((units, chips)), dma((units, chips)),
            dma((2,)),
            dma((units, n_coldev, parts)), dma((units, n_coldev, parts)),
            dma((units, n_coldev, parts)),
            dma((subs, n_rowdev)), dma((subs, n_rowdev)),
            dma((subs, n_coldev)), dma((subs, n_coldev)),
            dma((subs, n_rowdev)), dma((subs, n_rowdev)),
        ],
        compiler_params=pltpu.CompilerParams(
            collective_id=0, has_side_effects=True, vmem_limit_bytes=64_000_000
        ),
        name="gather_product_scatter",
    )(lines, block_sizes.reshape(1, -1), listed, inverse)
    rows = jnp.transpose(out.reshape(shard_rows, 2, sibling_count, width), (0, 2, 1, 3))
    return (
        rows.reshape(shard_rows, sibling_count, own_columns),
        schur.reshape(sibling_count, own_columns, own_columns),
    )


def total_kernel(
    n_rowdev, n_coldev, x_ref, out_ref,
    got, mine, gathered, whole, first_send, first_recv, second_send, second_recv,
    third_send, third_recv,
):
    row = lax.axis_index("row")
    col = lax.axis_index("col")
    barrier = pltpu.get_barrier_semaphore()
    for step in range(1, n_rowdev):
        pl.semaphore_signal(
            barrier, inc=1, device_id=((row + step) % n_rowdev, col), device_id_type=MESH
        )
    for step in range(1, n_coldev):
        pl.semaphore_signal(
            barrier, inc=1, device_id=(row, (col + step) % n_coldev), device_id_type=MESH
        )
    pl.semaphore_wait(barrier, n_rowdev + n_coldev - 2)

    def scatter(step):
        peer = (row + step) % n_rowdev
        return pltpu.make_async_remote_copy(
            src_ref=x_ref.at[peer], dst_ref=got.at[step],
            send_sem=first_send.at[step], recv_sem=first_recv.at[step],
            device_id=(peer, col), device_id_type=MESH,
        )

    def share(step):
        return pltpu.make_async_remote_copy(
            src_ref=mine, dst_ref=gathered.at[step],
            send_sem=second_send.at[step], recv_sem=second_recv.at[step],
            device_id=(row, (col + step) % n_coldev), device_id_type=MESH,
        )

    def spread(step):
        return pltpu.make_async_remote_copy(
            src_ref=whole, dst_ref=out_ref.at[row],
            send_sem=third_send.at[step], recv_sem=third_recv.at[step],
            device_id=((row + step) % n_rowdev, col), device_id_type=MESH,
        )

    for step in range(1, n_rowdev):
        scatter(step).start()
    value = x_ref[row]
    for step in range(1, n_rowdev):
        scatter(step).wait_recv()
        value = value + got[step]
    mine[...] = value
    for step in range(1, n_coldev):
        share(step).start()
    for step in range(1, n_coldev):
        share(step).wait_recv()
    gathered[0] = mine[...]
    value = gathered[col]
    for place in range(1, n_coldev):
        value = value + gathered[(col - place + n_coldev) % n_coldev]
    whole[...] = value
    for step in range(1, n_rowdev):
        spread(step).start()
    out_ref[row] = whole[...]
    for step in range(1, n_rowdev):
        spread(step).wait_recv()
    for step in range(1, n_rowdev):
        scatter(step).wait_send()
        spread(step).wait_send()
    for step in range(1, n_coldev):
        share(step).wait_send()


def total(n_rowdev, n_coldev, value):
    rows, columns = value.shape
    piece = rows // n_rowdev
    vmem = pl.BlockSpec(memory_space=pltpu.VMEM)
    dma = pltpu.SemaphoreType.DMA
    out = pl.pallas_call(
        functools.partial(total_kernel, n_rowdev, n_coldev),
        out_shape=jax.ShapeDtypeStruct((n_rowdev, piece, columns), jnp.float32),
        in_specs=[vmem],
        out_specs=vmem,
        scratch_shapes=[
            pltpu.VMEM((n_rowdev, piece, columns), jnp.float32),
            pltpu.VMEM((piece, columns), jnp.float32),
            pltpu.VMEM((n_coldev, piece, columns), jnp.float32),
            pltpu.VMEM((piece, columns), jnp.float32),
            dma((n_rowdev,)), dma((n_rowdev,)), dma((n_coldev,)), dma((n_coldev,)),
            dma((n_rowdev,)), dma((n_rowdev,)),
        ],
        compiler_params=pltpu.CompilerParams(collective_id=1, has_side_effects=True),
        name="schur_total",
    )(value.reshape(n_rowdev, piece, columns))
    return out.reshape(rows, columns)


def per_device(inverse, factor, diag_inverse, block_sizes, listed):
    n_rowdev = lax.axis_size("row")
    n_coldev = lax.axis_size("col")
    row_place = lax.axis_index("row")
    col_place = lax.axis_index("col")
    shard_rows, sibling_count, width = factor.shape

    chips = n_rowdev // 2
    if n_rowdev == 2 * n_coldev and chips == 4 and shard_rows % (chips * 32) == 0:
        ancestor_rows, terms = planar_product(
            n_rowdev, n_coldev, inverse, factor, block_sizes, listed
        )
        return (ancestor_rows, diag_inverse + terms)
    member = membership(
        (row_place * n_coldev + col_place) * shard_rows, shard_rows, block_sizes, listed
    )
    own = jnp.transpose(factor, (1, 0, 2))
    summed = general_product(n_rowdev, n_coldev, inverse, own * member.T[:, :, None])
    results = [
        -(summed[s] * member[:, s:s + 1])
        for s in range(sibling_count)
    ]
    terms = [
        lax.dot_general(
            own[s], results[s], (((0,), (0,)), ((), ())),
            precision=lax.Precision.HIGHEST, preferred_element_type=jnp.float32,
        )
        for s in range(sibling_count)
    ]
    schur = total(n_rowdev, n_coldev, jnp.concatenate(terms, axis=0))
    schur = schur.reshape(sibling_count, width, width)
    ancestor_rows = jnp.stack(results, axis=1)
    return (ancestor_rows, diag_inverse - schur)


def solution(mesh):
    in_specs = (P("row", "col"), P(("row", "col"), None, None), P(), P(), P())
    out_specs = (P(("row", "col"), None, None), P())
    return jax.shard_map(
        per_device, mesh=mesh, in_specs=in_specs, out_specs=out_specs, check_vma=False
    )
```

```python
import functools
import math

import jax
import jax.numpy as jnp
from jax import lax
from jax.experimental import pallas as pl
from jax.experimental.pallas import tpu as pltpu
from jax.sharding import PartitionSpec as P

MESH = pl.DeviceIdType.MESH


def membership(first_row, row_total, block_sizes, listed):
    count = block_sizes.shape[0]
    until = lax.broadcasted_iota(jnp.int32, (count, count), 1) <= lax.broadcasted_iota(jnp.int32, (count, count), 0)
    block_ends = jnp.sum(jnp.where(until, block_sizes[None, :], 0), axis=1)
    block_starts = block_ends - block_sizes
    positions = first_row + jnp.arange(row_total, dtype=jnp.int32)
    inside = (
        (positions[:, None] >= block_starts[None, :]) & (positions[:, None] < block_ends[None, :])
    ).astype(jnp.float32)
    return jnp.dot(
        inside,
        listed.astype(jnp.float32).T,
        precision=lax.Precision.HIGHEST,
        preferred_element_type=jnp.float32,
    )


def holder(k, n_rowdev, n_coldev):
    ratio = n_rowdev // n_coldev
    part = k // n_coldev
    place = k % n_coldev
    return (place + (part % 2) * (n_coldev - 1 - 2 * place)) * ratio + part


def shard_of(row, n_rowdev, n_coldev):
    ratio = n_rowdev // n_coldev
    part = row % ratio
    place = row // ratio
    return part * n_coldev + place + (part % 2) * (n_coldev - 1 - 2 * place)


def flip(row, bit):
    return row + bit * (1 - 2 * ((row // bit) % 2))


def general_kernel(
    n_rowdev, n_coldev, parts, depth,
    own_ref, inverse_ref, out_ref,
    panel, high, low, tiles, sums, from_below, from_above,
    gather_send, gather_recv, tile_sem, sum_send, below_recv, above_recv,
):
    row = lax.axis_index("row")
    col = lax.axis_index("col")
    sibling_count, shard_rows, width = own_ref.shape
    col_rows = panel.shape[1]
    piece = shard_rows // parts
    bits = [1 << i for i in range(n_rowdev.bit_length() - 1)]

    number = row * n_coldev + col
    target_row = holder(number % n_rowdev, n_rowdev, n_coldev)
    target_col = number // n_rowdev
    source = col * n_rowdev + shard_of(row, n_rowdev, n_coldev)
    source_row = source // n_coldev
    source_col = source % n_coldev
    moving = target_row * n_coldev + target_col != number

    barrier = pltpu.get_barrier_semaphore()

    def greet(to_row, to_col):
        pl.semaphore_signal(barrier, inc=1, device_id=(to_row, to_col), device_id_type=MESH)

    for bit in bits:
        greet(flip(row, bit), col)

    @pl.when(moving)
    def _():
        greet(target_row, target_col)
        greet(source_row, source_col)

    @pl.when(col > 0)
    def _():
        greet(row, col - 1)

    @pl.when(col < n_coldev - 1)
    def _():
        greet(row, col + 1)

    pl.semaphore_wait(
        barrier,
        len(bits)
        + jnp.where(moving, 2, 0)
        + jnp.where(col > 0, 1, 0)
        + jnp.where(col < n_coldev - 1, 1, 0),
    )

    def place(of_row, part):
        start = shard_of(of_row, n_rowdev, n_coldev) * shard_rows + part * piece
        return pl.ds(pl.multiple_of(start, 8), piece)

    def orders(part):
        rest = bits[1:]
        return (rest if part % 2 else rest[::-1]) + bits[:1]

    def move(s, part):
        return pltpu.make_async_remote_copy(
            src_ref=own_ref.at[s, pl.ds(part * piece, piece)],
            dst_ref=panel.at[s, place(target_row, part)],
            send_sem=gather_send.at[s, part, 0],
            recv_sem=gather_recv.at[s, part, 0],
            device_id=(target_row, target_col),
            device_id_type=MESH,
        )

    def keep(s, part):
        return pltpu.make_async_copy(
            own_ref.at[s, pl.ds(part * piece, piece)],
            panel.at[s, place(row, part)],
            gather_recv.at[s, part, 0],
        )

    def exchanges(s, part, stage):
        order = orders(part)
        held = [row]
        for bit in order[:stage - 1]:
            held = held + [flip(r, bit) for r in held]
        partner = flip(row, order[stage - 1])
        copies = []
        for m, slot in enumerate(held):
            entry = (1 << (stage - 1)) + m
            where = panel.at[s, place(slot, part)]
            copies.append(pltpu.make_async_remote_copy(
                src_ref=where,
                dst_ref=where,
                send_sem=gather_send.at[s, part, entry],
                recv_sem=gather_recv.at[s, part, entry],
                device_id=(partner, col),
                device_id_type=MESH,
            ))
        return copies

    def start_stage(s, part, stage):
        if stage == 0:
            @pl.when(moving)
            def _():
                move(s, part).start()

            @pl.when(jnp.logical_not(moving))
            def _():
                keep(s, part).start()
        else:
            for copy in exchanges(s, part, stage):
                copy.start()

    def end_stage(s, part, stage):
        if stage == 0:
            @pl.when(moving)
            def _():
                move(s, part).wait_recv()

            @pl.when(jnp.logical_not(moving))
            def _():
                keep(s, part).wait()
        else:
            for copy in exchanges(s, part, stage):
                copy.wait_recv()

    items = [(s, part) for s in range(sibling_count) for part in range(parts)]
    for s, part in items:
        start_stage(s, part, 0)

    others = (n_coldev - 1) * parts
    total = n_coldev * parts
    swap = col > n_coldev - 1 - col
    near = jnp.where(swap, n_coldev - 1 - col, col)
    lead = n_coldev - 1 - 2 * near
    minor_total = near * parts

    def plan(t):
        inner = t - lead
        paired = jnp.logical_and(inner >= 0, inner < 2 * minor_total)
        minor = jnp.logical_and(paired, inner % 2 == 1)
        major_at = jnp.where(inner < 0, t, jnp.where(paired, lead + inner // 2, t - minor_total))
        index = jnp.where(minor, inner // 2, major_at)
        up = jnp.where(swap, minor, jnp.logical_not(minor))
        block = jnp.where(up, n_coldev - 1 - index // parts, index // parts)
        is_own = t >= others
        block = jnp.where(is_own, col, block)
        part = jnp.where(is_own, t - others, index % parts)
        up = jnp.logical_and(up, jnp.logical_not(is_own))
        down = jnp.logical_and(jnp.logical_not(up), jnp.logical_not(is_own))
        return block, part, up, down, is_own

    def load(s, t):
        block, part, _, _, _ = plan(t % total)
        start = pl.multiple_of(block * shard_rows + part * piece, 8)
        slot = (s * total + t) % 2
        return pltpu.make_async_copy(
            inverse_ref.at[pl.ds(start, piece)], tiles.at[slot], tile_sem.at[slot]
        )

    load(0, 0).start()

    stages = 1 + len(bits)
    for tick in range(parts + stages):
        for part in range(parts):
            stage = tick - part
            if 0 <= stage < stages:
                end_stage(0, part, stage)
                if stage + 1 < stages:
                    start_stage(0, part, stage + 1)

    step = math.gcd(col_rows, 256)

    def split(s):
        @pl.loop(0, col_rows // step)
        def _(i):
            rows = pl.ds(pl.multiple_of(i * step, step), step)
            value = panel[s, rows, :]
            top = value.astype(jnp.bfloat16)
            high[s, rows, :] = top
            low[s, rows, :] = (value - top.astype(jnp.float32)).astype(jnp.bfloat16)

    def pass_up(s, block, part):
        return pltpu.make_async_remote_copy(
            src_ref=sums.at[s, block, part],
            dst_ref=from_below.at[s, block, part],
            send_sem=sum_send.at[s, block, part],
            recv_sem=below_recv.at[s, block, part],
            device_id=(row, col + 1),
            device_id_type=MESH,
        )

    def pass_down(s, block, part):
        return pltpu.make_async_remote_copy(
            src_ref=sums.at[s, block, part],
            dst_ref=from_above.at[s, block, part],
            send_sem=sum_send.at[s, block, part],
            recv_sem=above_recv.at[s, block, part],
            device_id=(row, col - 1),
            device_id_type=MESH,
        )

    hooks = [(stage, part) for stage in range(stages - 1) for part in range(parts)]

    def advance(s, hook):
        stage, part = hook
        end_stage(s, part, stage)
        start_stage(s, part, stage + 1)

    for s in range(sibling_count):
        split(s)
        follows = s + 1 < sibling_count

        @pl.loop(0, total)
        def _(t):
            block, part, up, down, is_own = plan(t)
            slot = (s * total + t) % 2

            @pl.when(t + 1 < (total + 1 if follows else total))
            def _():
                load(s, t + 1).start()

            load(s, t).wait()
            sums[s, block, part] = jnp.zeros((piece, width), jnp.float32)

            @pl.loop(0, col_rows // depth)
            def _(k):
                span = pl.ds(pl.multiple_of(k * depth, depth), depth)
                value = tiles[slot, :, span]
                top = value.astype(jnp.bfloat16)
                rest = (value - top.astype(jnp.float32)).astype(jnp.bfloat16)
                dot = functools.partial(jnp.dot, preferred_element_type=jnp.float32)
                sums[s, block, part] += (
                    dot(top, low[s, span, :])
                    + dot(rest, high[s, span, :])
                    + dot(top, high[s, span, :])
                )

            @pl.when(jnp.logical_and(jnp.logical_not(down), col > 0))
            def _():
                pass_up(s, block, part).wait_recv()
                sums[s, block, part] += from_below[s, block, part]

            @pl.when(jnp.logical_and(jnp.logical_not(up), col < n_coldev - 1))
            def _():
                pass_down(s, block, part).wait_recv()
                sums[s, block, part] += from_above[s, block, part]

            @pl.when(up)
            def _():
                pass_up(s, block, part).start()

            @pl.when(down)
            def _():
                pass_down(s, block, part).start()

            @pl.when(is_own)
            def _():
                out_ref[s, part] = sums[s, block, part]

            if follows:
                for at, hook in enumerate(hooks[:total]):
                    @pl.when(t == at)
                    def _(hook=hook):
                        advance(s + 1, hook)

        if follows:
            for hook in hooks[total:]:
                advance(s + 1, hook)
            for part in range(parts):
                end_stage(s + 1, part, stages - 1)

    for s in range(sibling_count):
        @pl.loop(0, others)
        def _(t):
            block, part, up, down, _ = plan(t)

            @pl.when(up)
            def _():
                pass_up(s, block, part).wait_send()

            @pl.when(down)
            def _():
                pass_down(s, block, part).wait_send()

    for s, part in items:
        @pl.when(moving)
        def _():
            move(s, part).wait_send()

        for stage in range(1, stages):
            for copy in exchanges(s, part, stage):
                copy.wait_send()


def general_product(n_rowdev, n_coldev, inverse, own):
    sibling_count, shard_rows, width = own.shape
    block_total, col_rows = inverse.shape
    parts = 2 if shard_rows % 16 == 0 else 1
    piece = shard_rows // parts
    depth = math.gcd(col_rows, 1280)
    f32 = jnp.float32
    vmem = pl.BlockSpec(memory_space=pltpu.VMEM)
    out = pl.pallas_call(
        functools.partial(general_kernel, n_rowdev, n_coldev, parts, depth),
        out_shape=jax.ShapeDtypeStruct((sibling_count, parts, piece, width), f32),
        in_specs=[vmem, pl.BlockSpec(memory_space=pl.ANY)],
        out_specs=vmem,
        scratch_shapes=[
            pltpu.VMEM((sibling_count, col_rows, width), f32),
            pltpu.VMEM((sibling_count, col_rows, width), jnp.bfloat16),
            pltpu.VMEM((sibling_count, col_rows, width), jnp.bfloat16),
            pltpu.VMEM((2, piece, col_rows), f32),
            pltpu.VMEM((sibling_count, n_coldev, parts, piece, width), f32),
            pltpu.VMEM((sibling_count, n_coldev, parts, piece, width), f32),
            pltpu.VMEM((sibling_count, n_coldev, parts, piece, width), f32),
            pltpu.SemaphoreType.DMA((sibling_count, parts, n_rowdev)),
            pltpu.SemaphoreType.DMA((sibling_count, parts, n_rowdev)),
            pltpu.SemaphoreType.DMA((2,)),
            pltpu.SemaphoreType.DMA((sibling_count, n_coldev, parts)),
            pltpu.SemaphoreType.DMA((sibling_count, n_coldev, parts)),
            pltpu.SemaphoreType.DMA((sibling_count, n_coldev, parts)),
        ],
        compiler_params=pltpu.CompilerParams(
            collective_id=0, has_side_effects=True, vmem_limit_bytes=60_000_000
        ),
        name="gather_product_scatter",
    )(own, inverse)
    return out.reshape(sibling_count, shard_rows, width)


def planar_kernel(
    n_rowdev, n_coldev, parts, sibling_count, unit_subs, order,
    factor_ref, sizes_ref, listed_ref, inverse_ref, out_ref, schur_ref, *scratch,
):
    units = len(unit_subs)
    scratch = list(scratch)

    def take(count):
        taken_refs = scratch[:count]
        del scratch[:count]
        return taken_refs

    own_ref, member_ref, landing, panel, tiles, across_high, across_low = take(7)
    terms, got, mine_sum, gathered, whole = take(5)
    split_refs, sums, from_below, from_above = (take(units) for _ in range(4))
    (
        spread_send, spread_recv, move_send, move_recv, keep_sem, plane_send, plane_recv,
        core_send, core_recv, tile_sem, sum_send, below_recv, above_recv,
        scatter_send, scatter_recv, share_send, share_recv, result_send, result_recv,
    ) = scratch

    row = lax.axis_index("row")
    col = lax.axis_index("col")
    subs, chips, quarter, width = own_ref.shape
    half = quarter // 2
    shard_rows = chips * quarter
    col_rows = n_rowdev * shard_rows
    piece = shard_rows // parts
    per_sibling = subs // sibling_count
    core = row % 2
    chip = row // 2
    near_x, near_y, other_core = flip(row, 2), flip(row, 4), flip(row, 1)
    firsts = [sum(unit_subs[:u]) for u in range(units)]

    def across(d):
        r = row
        for bit in (1, 2):
            if d & bit:
                r = flip(r, 2 * bit)
        return r

    barrier = pltpu.get_barrier_semaphore()
    greeted = [((row + e) % n_rowdev, col) for e in range(1, n_rowdev)]
    greeted += [(row, (col + e) % n_coldev) for e in range(1, n_coldev)]
    for who in greeted:
        pl.semaphore_signal(barrier, inc=1, device_id=who, device_id_type=MESH)

    f32 = jnp.float32
    count = sizes_ref.shape[1]
    down_axis = lax.broadcasted_iota(jnp.int32, (count, count), 0)
    along_axis = lax.broadcasted_iota(jnp.int32, (count, count), 1)
    sizes = sizes_ref[...].astype(f32)
    upright = jnp.sum(jnp.where(down_axis == along_axis, sizes, 0.0), axis=1, keepdims=True)
    ends = jnp.sum(jnp.where(down_axis <= along_axis, upright, 0.0), axis=0, keepdims=True)
    first_row = (row * n_coldev + col) * shard_rows
    positions = (first_row + lax.broadcasted_iota(jnp.int32, (shard_rows, count), 0)).astype(f32)
    inside = jnp.logical_and(positions >= ends - sizes, positions < ends)
    for s in range(sibling_count):
        chosen = jnp.where(inside, listed_ref[s:s + 1, :].astype(f32), 0.0)
        member_ref[s] = jnp.broadcast_to(
            jnp.sum(chosen, axis=1, keepdims=True), (shard_rows, width)
        )

    def lines(sub):
        at = sub % per_sibling * sibling_count + sub // per_sibling
        return pl.ds(at, shard_rows, stride=subs)

    def mask(sub):
        masked = factor_ref[lines(sub), :] * member_ref[sub // per_sibling]
        own_ref[sub] = masked.reshape(chips, quarter, width)

    for sub in range(unit_subs[0]):
        mask(sub)
    pl.semaphore_wait(barrier, len(greeted))

    def group(u):
        return pl.ds(firsts[u], unit_subs[u])

    def remote(src, dst, send, recv, to_row, to_col):
        return pltpu.make_async_remote_copy(
            src_ref=src, dst_ref=dst, send_sem=send, recv_sem=recv,
            device_id=(to_row, to_col), device_id_type=MESH,
        )

    def spread(u, d):
        to_row = across(d)
        return remote(
            own_ref.at[group(u), to_row // 2], landing.at[group(u), d - 1],
            spread_send.at[u, d - 1], spread_recv.at[u, d - 1], to_row, col,
        )

    def taken(u, d):
        return own_ref.at[group(u), chip] if d == 0 else landing.at[group(u), d - 1]

    def plane_of(d):
        return across(d) // 2

    def move(u, d):
        return remote(
            taken(u, d), panel.at[group(u), core * n_coldev + col, chip],
            move_send.at[u, d], move_recv.at[u, col], row, plane_of(d),
        )

    def arrival(u, source):
        where = panel.at[group(u), core * n_coldev + source, chip]
        return remote(where, where, move_send.at[u, 0], move_recv.at[u, source], row, source)

    def keep(u, d):
        return pltpu.make_async_copy(
            taken(u, d), panel.at[group(u), core * n_coldev + col, chip], keep_sem.at[u]
        )

    def mine(u, of_chip, part):
        shards = pl.ds(core * n_coldev, n_coldev)
        if part is None:
            return panel.at[group(u), shards, of_chip]
        return panel.at[group(u), shards, of_chip, pl.ds(part * half, half)]

    def in_plane(u, at):
        of_chip, part, to_row = (
            (chip, 0, near_x), (chip, 1, near_y), (chip, 1, near_x), (chip, 0, near_y),
            (near_x // 2, 0, near_y), (near_y // 2, 1, near_x),
        )[at]
        where = mine(u, of_chip, part)
        return remote(where, where, plane_send.at[u, at], plane_recv.at[u, at], to_row, col)

    def to_core(u, d):
        where = mine(u, plane_of(d), None)
        return remote(where, where, core_send.at[u, d], core_recv.at[u, d], other_core, col)

    def stage_spread(u):
        for d in range(1, chips):
            spread(u, d).start()

    def stage_move(u):
        for d in range(chips):
            if d:
                spread(u, d).wait_recv()

            @pl.when(plane_of(d) != col)
            def _():
                move(u, d).start()

            @pl.when(plane_of(d) == col)
            def _():
                keep(u, d).start()

    def stage_plane(u):
        keep(u, 0).wait()
        for e in range(1, n_coldev):
            arrival(u, (col + e) % n_coldev).wait_recv()
        for at in range(4):
            in_plane(u, at).start()
        to_core(u, 0).start()

    def stage_pass(u):
        in_plane(u, 0).wait_recv()
        in_plane(u, 4).start()
        in_plane(u, 1).wait_recv()
        in_plane(u, 5).start()

    def stage_core(u):
        in_plane(u, 2).wait_recv()
        to_core(u, 1).start()
        in_plane(u, 3).wait_recv()
        to_core(u, 2).start()

    def stage_last(u):
        in_plane(u, 4).wait_recv()
        in_plane(u, 5).wait_recv()
        to_core(u, 3).start()

    def stage_ready(u):
        for d in range(chips):
            to_core(u, d).wait_recv()

    def peer_of(d):
        r = row
        for at in range(n_rowdev.bit_length() - 1):
            if d >> at & 1:
                r = flip(r, 1 << at)
        return r

    peers = range(n_rowdev - 1, 0, -1)

    def scatter(sub, step):
        peer = peer_of(step)
        return remote(
            terms.at[sub, peer], got.at[sub, step],
            scatter_send.at[sub, step], scatter_recv.at[sub, step], peer, col,
        )

    def share(sub, step):
        return remote(
            mine_sum.at[sub], gathered.at[sub, step],
            share_send.at[sub, step], share_recv.at[sub, step], row, (col + step) % n_coldev,
        )

    def block_of(sub):
        lanes = pl.ds(sub % per_sibling * width, width)
        return schur_ref.at[sub // per_sibling, row, :, lanes]

    def subs_of(u):
        return range(firsts[u], firsts[u] + unit_subs[u])

    def result(sub, d):
        return remote(
            whole.at[sub], block_of(sub),
            result_send.at[sub, d], result_recv.at[sub, d], peer_of(d), col,
        )

    dot = functools.partial(jnp.dot, preferred_element_type=jnp.float32)
    bf16 = jnp.bfloat16

    def halves(value):
        top = value.astype(bf16)
        return top, (value - top.astype(jnp.float32)).astype(bf16)

    def stage_term(u):
        for part in range(parts):
            @pl.when(col > 0)
            def _():
                pass_up(u, col, part).wait_recv()
                sums[u][col, part] += from_below[u][col, part]

            @pl.when(col < n_coldev - 1)
            def _():
                pass_down(u, col, part).wait_recv()
                sums[u][col, part] += from_above[u][col, part]

        def finished(at):
            value = sums[u][col, :, :, pl.ds(at * width, width)]
            return value.reshape(shard_rows, width)

        for at, sub in enumerate(subs_of(u)):
            sibling = sub // per_sibling
            top, rest = halves(finished(at))
            high, low = across_high[sibling], across_low[sibling]
            term = dot(high, rest) + dot(low, top) + dot(high, top)
            terms[sub] = term.reshape(n_rowdev, term.shape[0] // n_rowdev, width)
            for step in peers:
                scatter(sub, step).start()
        for at, sub in enumerate(subs_of(u)):
            out_ref[lines(sub), :] = -(finished(at) * member_ref[sub // per_sibling])

    def stage_share(u):
        for sub in subs_of(u):
            value = terms[sub, row]
            for step in peers[::-1]:
                scatter(sub, step).wait_recv()
                value = value + got[sub, step]
            mine_sum[sub] = value
            for step in range(1, n_coldev):
                share(sub, step).start()

    def stage_result(u):
        for sub in subs_of(u):
            for step in range(1, n_coldev):
                share(sub, step).wait_recv()
            gathered[sub, 0] = mine_sum[sub]
            value = gathered[sub, col]
            for place in range(1, n_coldev):
                value = value + gathered[sub, (col - place + n_coldev) % n_coldev]
            whole[sub] = value
            for d in peers:
                result(sub, d).start()
            block_of(sub)[...] = whole[sub]

    def stage_done(u):
        for sub in subs_of(u):
            for d in peers[::-1]:
                result(sub, d).wait_recv()

    late = ((1, 1, 3), (3, 1, 4), (4, 2, 2), (5, 1, 5), (7, 1, 6), (10, 2, 3), (13, 2, 4), (15, 2, 5), (15, 2, 6), (13, 0, 7), (15, 0, 8), (18, 0, 9), (19, 1, 7), (21, 1, 8), (23, 1, 9), (25, 2, 7), (27, 2, 8), (28, 2, 9), (29, 0, 10), (29, 1, 10), (29, 2, 10))
    stages = (stage_spread, stage_move, stage_plane, stage_pass, stage_core, stage_last, stage_ready)
    ready = len(stages) - 1
    after = (stage_term, stage_share, stage_result, stage_done)

    others = (n_coldev - 1) * parts
    total = n_coldev * parts
    swap = col > n_coldev - 1 - col
    near = jnp.where(swap, n_coldev - 1 - col, col)
    lead = n_coldev - 1 - 2 * near
    minor_total = near * parts

    def plan(t):
        inner = t - lead
        paired = jnp.logical_and(inner >= 0, inner < 2 * minor_total)
        minor = jnp.logical_and(paired, inner % 2 == 1)
        major_at = jnp.where(inner < 0, t, jnp.where(paired, lead + inner // 2, t - minor_total))
        index = jnp.where(minor, inner // 2, major_at)
        up = jnp.where(swap, minor, jnp.logical_not(minor))
        block = jnp.where(up, n_coldev - 1 - index // parts, index // parts)
        is_own = t >= others
        block = jnp.where(is_own, col, block)
        part = jnp.where(is_own, t - others, index % parts)
        up = jnp.logical_and(up, jnp.logical_not(is_own))
        down = jnp.logical_and(jnp.logical_not(up), jnp.logical_not(is_own))
        return block, part, up, down

    def load(u, t):
        block, part, _, _ = plan(t % total)
        start = pl.multiple_of(block * shard_rows + part * piece, 8)
        slot = (u * total + t) % 2
        return pltpu.make_async_copy(
            inverse_ref.at[pl.ds(start, piece)], tiles.at[slot], tile_sem.at[slot]
        )

    def split(u):
        wide = unit_subs[u] * width

        @pl.loop(0, n_rowdev)
        def _(i):
            for at in range(unit_subs[u]):
                for j in range(chips):
                    rows = pl.ds(pl.multiple_of(i * shard_rows + j * quarter, 16), quarter)
                    top, rest = halves(panel[firsts[u] + at, i, j])
                    split_refs[u][rows, pl.ds(at * width, width)] = top
                    split_refs[u][rows, pl.ds(wide + at * width, width)] = rest

    def pass_up(u, block, part):
        return remote(
            sums[u].at[block, part], from_below[u].at[block, part],
            sum_send.at[u, block, part], below_recv.at[u, block, part], row, col + 1,
        )

    def pass_down(u, block, part):
        return remote(
            sums[u].at[block, part], from_above[u].at[block, part],
            sum_send.at[u, block, part], above_recv.at[u, block, part], row, col - 1,
        )

    def multiply(u, slot):
        wide = unit_subs[u] * width
        top, rest = halves(tiles[slot])
        if unit_subs[u] == 1:
            main = dot(top, split_refs[u][...])
            return main[:, wide:] + dot(rest, split_refs[u][:, pl.ds(0, wide)]) + main[:, :wide]
        high = split_refs[u][:, pl.ds(0, wide)]
        return dot(top, split_refs[u][:, pl.ds(wide, wide)]) + dot(rest, high) + dot(top, high)

    def turn_own():
        for sub in range(subs):
            value = own_ref[sub].reshape(shard_rows, width)
            top, rest = halves(value.T)
            rows = pl.ds((sub % per_sibling) * width, width)
            across_high[sub // per_sibling, rows, :] = top
            across_low[sub // per_sibling, rows, :] = rest

    def advance(step):
        u, at = step
        (stages + after)[at](u)

    load(0, 0).start()
    for number, step in enumerate(order):
        advance(step)
        if number == 0:
            for sub in range(unit_subs[0], subs):
                mask(sub)
        if number == 6:
            turn_own()

    for u in range(units):
        split(u)
        follows = u + 1 < units
        timed = [(at % total, (v, n)) for at, v, n in late if at // total == u]

        @pl.loop(0, total)
        def _(t):
            block, part, up, down = plan(t)
            slot = (u * total + t) % 2

            @pl.when(t + 1 < (total + 1 if follows else total))
            def _():
                load(u, t + 1).start()

            load(u, t).wait()
            sums[u][block, part] = multiply(u, slot)

            @pl.when(jnp.logical_and(up, col > 0))
            def _():
                pass_up(u, block, part).wait_recv()
                sums[u][block, part] += from_below[u][block, part]

            @pl.when(jnp.logical_and(down, col < n_coldev - 1))
            def _():
                pass_down(u, block, part).wait_recv()
                sums[u][block, part] += from_above[u][block, part]

            @pl.when(up)
            def _():
                pass_up(u, block, part).start()

            @pl.when(down)
            def _():
                pass_down(u, block, part).start()

            for when, hook in timed:
                @pl.when(t == when)
                def _(hook=hook):
                    advance(hook)

    def sums_sent(u):
        @pl.loop(0, others)
        def _(t):
            block, part, up, down = plan(t)

            @pl.when(up)
            def _():
                pass_up(u, block, part).wait_send()

            @pl.when(down)
            def _():
                pass_down(u, block, part).wait_send()

    def gather_sent(u):
        for d in range(1, chips):
            spread(u, d).wait_send()
        for d in range(chips):
            @pl.when(plane_of(d) != col)
            def _():
                move(u, d).wait_send()

            to_core(u, d).wait_send()
        for at in range(6):
            in_plane(u, at).wait_send()

    def diagonal_sent(u):
        for sub in subs_of(u):
            for step in peers:
                scatter(sub, step).wait_send()
                result(sub, step).wait_send()
            for step in range(1, n_coldev):
                share(sub, step).wait_send()

    for at, v, n in late:
        if at // total == units:
            advance((v, n))
            if (v, n) == (units - 1, ready + 1):
                for u in range(units):
                    gather_sent(u)
            if (v, n) == (units - 1, ready + 2):
                for u in range(units):
                    sums_sent(u)
            if (v, n) == (units - 1, ready + 3):
                for u in range(units - 1):
                    diagonal_sent(u)
    diagonal_sent(units - 1)


def planar_product(n_rowdev, n_coldev, inverse, factor, block_sizes, listed):
    shard_rows, sibling_count, own_columns = factor.shape
    width = own_columns // 2
    subs = 2 * sibling_count
    block_total, col_rows = inverse.shape
    chips = n_rowdev // 2
    quarter = shard_rows // chips
    parts = 2
    piece = shard_rows // parts
    unit_subs = (1, 1, 2)
    units = len(unit_subs)
    order = ((0, 0), (1, 0), (0, 1), (2, 0), (1, 1), (0, 2), (2, 1), (0, 3), (0, 4), (0, 5), (1, 2), (0, 6))
    share_rows = own_columns // n_rowdev
    f32, bf16 = jnp.float32, jnp.bfloat16
    vmem = pl.BlockSpec(memory_space=pltpu.VMEM)
    dma = pltpu.SemaphoreType.DMA
    blocks = [pltpu.VMEM((n_coldev, parts, piece, n * width), f32) for n in unit_subs]
    lines = factor.reshape(shard_rows, sibling_count, 2, width)
    lines = jnp.transpose(lines, (0, 2, 1, 3)).reshape(shard_rows * subs, width)
    out, schur = pl.pallas_call(
        functools.partial(
            planar_kernel, n_rowdev, n_coldev, parts, sibling_count, unit_subs, order
        ),
        out_shape=(
            jax.ShapeDtypeStruct((shard_rows * subs, width), f32),
            jax.ShapeDtypeStruct((sibling_count, n_rowdev, share_rows, own_columns), f32),
        ),
        in_specs=[vmem, vmem, vmem, pl.BlockSpec(memory_space=pl.ANY)],
        out_specs=(vmem, vmem),
        scratch_shapes=[
            pltpu.VMEM((subs, chips, quarter, width), f32),
            pltpu.VMEM((sibling_count, shard_rows, width), f32),
            pltpu.VMEM((subs, chips - 1, quarter, width), f32),
            pltpu.VMEM((subs, n_rowdev, chips, quarter, width), f32),
            pltpu.VMEM((2, piece, col_rows), f32),
            pltpu.VMEM((sibling_count, own_columns, shard_rows), bf16),
            pltpu.VMEM((sibling_count, own_columns, shard_rows), bf16),
            pltpu.VMEM((subs, n_rowdev, share_rows, width), f32),
            pltpu.VMEM((subs, n_rowdev, share_rows, width), f32),
            pltpu.VMEM((subs, share_rows, width), f32),
            pltpu.VMEM((subs, n_coldev, share_rows, width), f32),
            pltpu.VMEM((subs, share_rows, width), f32),
            *[pltpu.VMEM((col_rows, 2 * n * width), bf16) for n in unit_subs],
            *blocks, *blocks, *blocks,
            dma((units, chips - 1)), dma((units, chips - 1)),
            dma((units, chips)), dma((units, n_coldev)), dma((units,)),
            dma((units, 6)), dma((units, 6)),
            dma((units, chips)), dma((units, chips)),
            dma((2,)),
            dma((units, n_coldev, parts)), dma((units, n_coldev, parts)),
            dma((units, n_coldev, parts)),
            dma((subs, n_rowdev)), dma((subs, n_rowdev)),
            dma((subs, n_coldev)), dma((subs, n_coldev)),
            dma((subs, n_rowdev)), dma((subs, n_rowdev)),
        ],
        compiler_params=pltpu.CompilerParams(
            collective_id=0, has_side_effects=True, vmem_limit_bytes=64_000_000
        ),
        name="gather_product_scatter",
    )(lines, block_sizes.reshape(1, -1), listed, inverse)
    rows = jnp.transpose(out.reshape(shard_rows, 2, sibling_count, width), (0, 2, 1, 3))
    return (
        rows.reshape(shard_rows, sibling_count, own_columns),
        schur.reshape(sibling_count, own_columns, own_columns),
    )


def total_kernel(
    n_rowdev, n_coldev, x_ref, out_ref,
    got, mine, gathered, whole, first_send, first_recv, second_send, second_recv,
    third_send, third_recv,
):
    row = lax.axis_index("row")
    col = lax.axis_index("col")
    barrier = pltpu.get_barrier_semaphore()
    for step in range(1, n_rowdev):
        pl.semaphore_signal(
            barrier, inc=1, device_id=((row + step) % n_rowdev, col), device_id_type=MESH
        )
    for step in range(1, n_coldev):
        pl.semaphore_signal(
            barrier, inc=1, device_id=(row, (col + step) % n_coldev), device_id_type=MESH
        )
    pl.semaphore_wait(barrier, n_rowdev + n_coldev - 2)

    def scatter(step):
        peer = (row + step) % n_rowdev
        return pltpu.make_async_remote_copy(
            src_ref=x_ref.at[peer], dst_ref=got.at[step],
            send_sem=first_send.at[step], recv_sem=first_recv.at[step],
            device_id=(peer, col), device_id_type=MESH,
        )

    def share(step):
        return pltpu.make_async_remote_copy(
            src_ref=mine, dst_ref=gathered.at[step],
            send_sem=second_send.at[step], recv_sem=second_recv.at[step],
            device_id=(row, (col + step) % n_coldev), device_id_type=MESH,
        )

    def spread(step):
        return pltpu.make_async_remote_copy(
            src_ref=whole, dst_ref=out_ref.at[row],
            send_sem=third_send.at[step], recv_sem=third_recv.at[step],
            device_id=((row + step) % n_rowdev, col), device_id_type=MESH,
        )

    for step in range(1, n_rowdev):
        scatter(step).start()
    value = x_ref[row]
    for step in range(1, n_rowdev):
        scatter(step).wait_recv()
        value = value + got[step]
    mine[...] = value
    for step in range(1, n_coldev):
        share(step).start()
    for step in range(1, n_coldev):
        share(step).wait_recv()
    gathered[0] = mine[...]
    value = gathered[col]
    for place in range(1, n_coldev):
        value = value + gathered[(col - place + n_coldev) % n_coldev]
    whole[...] = value
    for step in range(1, n_rowdev):
        spread(step).start()
    out_ref[row] = whole[...]
    for step in range(1, n_rowdev):
        spread(step).wait_recv()
    for step in range(1, n_rowdev):
        scatter(step).wait_send()
        spread(step).wait_send()
    for step in range(1, n_coldev):
        share(step).wait_send()


def total(n_rowdev, n_coldev, value):
    rows, columns = value.shape
    piece = rows // n_rowdev
    vmem = pl.BlockSpec(memory_space=pltpu.VMEM)
    dma = pltpu.SemaphoreType.DMA
    out = pl.pallas_call(
        functools.partial(total_kernel, n_rowdev, n_coldev),
        out_shape=jax.ShapeDtypeStruct((n_rowdev, piece, columns), jnp.float32),
        in_specs=[vmem],
        out_specs=vmem,
        scratch_shapes=[
            pltpu.VMEM((n_rowdev, piece, columns), jnp.float32),
            pltpu.VMEM((piece, columns), jnp.float32),
            pltpu.VMEM((n_coldev, piece, columns), jnp.float32),
            pltpu.VMEM((piece, columns), jnp.float32),
            dma((n_rowdev,)), dma((n_rowdev,)), dma((n_coldev,)), dma((n_coldev,)),
            dma((n_rowdev,)), dma((n_rowdev,)),
        ],
        compiler_params=pltpu.CompilerParams(collective_id=1, has_side_effects=True),
        name="schur_total",
    )(value.reshape(n_rowdev, piece, columns))
    return out.reshape(rows, columns)


def per_device(inverse, factor, diag_inverse, block_sizes, listed):
    n_rowdev = lax.axis_size("row")
    n_coldev = lax.axis_size("col")
    row_place = lax.axis_index("row")
    col_place = lax.axis_index("col")
    shard_rows, sibling_count, width = factor.shape

    chips = n_rowdev // 2
    if n_rowdev == 2 * n_coldev and chips == 4 and shard_rows % (chips * 32) == 0:
        ancestor_rows, terms = planar_product(
            n_rowdev, n_coldev, inverse, factor, block_sizes, listed
        )
        return (ancestor_rows, diag_inverse + terms)
    member = membership(
        (row_place * n_coldev + col_place) * shard_rows, shard_rows, block_sizes, listed
    )
    own = jnp.transpose(factor, (1, 0, 2))
    summed = general_product(n_rowdev, n_coldev, inverse, own * member.T[:, :, None])
    results = [
        -(summed[s] * member[:, s:s + 1])
        for s in range(sibling_count)
    ]
    terms = [
        lax.dot_general(
            own[s], results[s], (((0,), (0,)), ((), ())),
            precision=lax.Precision.HIGHEST, preferred_element_type=jnp.float32,
        )
        for s in range(sibling_count)
    ]
    schur = total(n_rowdev, n_coldev, jnp.concatenate(terms, axis=0))
    schur = schur.reshape(sibling_count, width, width)
    ancestor_rows = jnp.stack(results, axis=1)
    return (ancestor_rows, diag_inverse - schur)


def solution(mesh):
    in_specs = (P("row", "col"), P(("row", "col"), None, None), P(), P(), P())
    out_specs = (P(("row", "col"), None, None), P())
    return jax.shard_map(
        per_device, mesh=mesh, in_specs=in_specs, out_specs=out_specs, check_vma=False
    )
```
